32 devices in a mesh: dp: 2 (over x), seq: 16 (over z, y, core).
Axes of the slice: x: 2, y: 2, z: 4, core: 2. Of those that a mesh axis runs over, the one named last changes fastest.
Arguments:
- frames: bfloat16 [4, 1024, 1024], P('dp', 'seq'), may hold values from -6 to 6
- out_grad: bfloat16 [4, 1024, 1024], P('dp', 'seq'), may hold values from -6 to 6
- order: int32 [4], P('dp'), may hold values from 0 to 3, each once
- lengths: int32 [4], replicated, may hold values from 1 to 1024, 2560 in all
- first_gain: bfloat16 [1024], P(('dp', 'seq')), may hold values from 0.25 to 1.75
- first_shift: bfloat16 [1024], P(('dp', 'seq')), may hold values from -3 to 3
- query_weight: bfloat16 [1024, 1024], P(('dp', 'seq')), may hold values from -0.1875 to 0.1875
- query_bias: bfloat16 [1024], P(('dp', 'seq')), may hold values from -3 to 3
- key_weight: bfloat16 [1024, 1024], P(('dp', 'seq')), may hold values from -0.1875 to 0.1875
- value_weight: bfloat16 [1024, 1024], P(('dp', 'seq')), may hold values from -0.1875 to 0.1875
- value_bias: bfloat16 [1024], P(('dp', 'seq')), may hold values from -3 to 3
- output_weight: bfloat16 [1024, 1024], P(('dp', 'seq')), may hold values from -3 to 3
- output_bias: bfloat16 [1024], P(('dp', 'seq')), may hold values from -3 to 3
- second_gain: bfloat16 [1024], P(('dp', 'seq')), may hold values from 0.25 to 1.75
- second_shift: bfloat16 [1024], P(('dp', 'seq')), may hold values from -3 to 3
- up_weight: bfloat16 [1024, 4096], P(('dp', 'seq')), may hold values from -0.1875 to 0.1875
- up_bias: bfloat16 [4096], P(('dp', 'seq')), may hold values from -3 to 3
- down_weight: bfloat16 [4096, 1024], P(('dp', 'seq')), may hold values from -0.09375 to 0.09375
- down_bias: bfloat16 [1024], P(('dp', 'seq')), may hold values from -3 to 3
Outputs:
- output: bfloat16 [4, 1024, 1024], P('dp', 'seq')
- frames_grad: bfloat16 [4, 1024, 1024], P('dp', 'seq')
- first_gain_grad: float32 [1024], P(('dp', 'seq'))
- first_shift_grad: float32 [1024], P(('dp', 'seq'))
- query_weight_grad: float32 [1024, 1024], P(('dp', 'seq'))
- query_bias_grad: float32 [1024], P(('dp', 'seq'))
- key_weight_grad: float32 [1024, 1024], P(('dp', 'seq'))
- value_weight_grad: float32 [1024, 1024], P(('dp', 'seq'))
- value_bias_grad: float32 [1024], P(('dp', 'seq'))
- output_weight_grad: float32 [1024, 1024], P(('dp', 'seq'))
- output_bias_grad: float32 [1024], P(('dp', 'seq'))
- second_gain_grad: float32 [1024], P(('dp', 'seq'))
- second_shift_grad: float32 [1024], P(('dp', 'seq'))
- up_weight_grad: float32 [1024, 4096], P(('dp', 'seq'))
- up_bias_grad: float32 [4096], P(('dp', 'seq'))
- down_weight_grad: float32 [4096, 1024], P(('dp', 'seq'))
- down_bias_grad: float32 [1024], P(('dp', 'seq'))
The draws below stay inside these ranges and needn't reach their ends.
Inputs may be any that keep to these rules, and one draw needn't show every extreme that they name: order[s] is the utterance held in slot s; each utterance is held by exactly one slot. lengths[u] counts the true frames of utterance u; frames from lengths[u] on are padding and are masked as keys; the longest utterance fills all 1024 frames.
All inputs are finite; a program needn't handle non-finite values.
Results may differ from the reference program's by a relative error of at most 0.012.
Values may be sent and summed in bfloat16 or wider, within the bound.
No kernel may reach another device: no remote copies, remote signals or barrier semaphores. Data moves between devices by JAX's collectives and lax.ppermute only.
A program may use at most 256 MiB of HBM per device.

```python
import math
from functools import partial
import jax
import jax.numpy as jnp
import numpy as np
from jax import lax

D = 1024
HEADS = 16
HEAD = 64
FF = 4096
LEN = 1024
SLOTS = 4


def shard_levels(key, dims, pieces, smallest, top_value):
    level, own = 1.0, jax.random.fold_in(key, 6)
    for position, parts in pieces:
        heights = jnp.exp(jax.random.uniform(jax.random.fold_in(own, position), (parts,), jnp.float32, smallest / len(pieces), top_value / len(pieces)))
        level = level * jnp.repeat(heights, dims[position] // parts).reshape([-1 if axis == position else 1 for axis in range(len(dims))])
    return level


def length_profile(count, total, reach, lean):
    portions = [(1 << 20) // math.isqrt(rank ** lean) + 1 for rank in range(2, count + 1)]
    surplus, counts = total - reach - (count - 1), [1] * (count - 1)
    while surplus > 0:
        candidates = [i for i in range(count - 1) if counts[i] < reach]
        mass, left = sum([portions[i] for i in candidates]), surplus
        for i in candidates:
            more = min(reach - counts[i], max(1, left * portions[i] // mass), surplus)
            counts[i] = counts[i] + more
            surplus = surplus - more
    return np.array([reach] + counts)


def uneven_parts(stream_key, number_of, total, most, skew):
    if number_of == 2:
        one = jax.random.randint(stream_key, (), max(1, total - most), min(most, total - 1) + 1)
        return jnp.stack([one, total - one])
    tallies = jnp.asarray(length_profile(number_of, total, most, skew), jnp.int32)
    pairs = (number_of - 1) // 2
    source_of, receiver = tallies[1:1 + 2 * pairs:2], tallies[2:2 + 2 * pairs:2]
    margin = jnp.minimum(source_of - 1, most - receiver)
    shifted = jax.random.randint(jax.random.fold_in(stream_key, 1), (pairs,), 0, 1 << 20) % (margin + 1)
    tallies = tallies.at[1:1 + 2 * pairs:2].set(source_of - shifted).at[2:2 + 2 * pairs:2].set(receiver + shifted)
    return tallies[jax.random.permutation(jax.random.fold_in(stream_key, 2), number_of)]


def bell_draw(stream_key, dims, deviation, limit, pieces=(), kind=jnp.bfloat16):
    drawn = deviation * jax.random.normal(stream_key, dims, jnp.float32)
    if pieces:
        drawn = drawn * shard_levels(stream_key, dims, pieces, -0.22, 0.18)
    return jnp.clip(drawn, -limit, limit).astype(kind)


def setup_inputs(seed: int = 0) -> dict:
    arg_keys = jax.random.split(jax.random.key(seed), 20)
    return {
        "frames": bell_draw(arg_keys[0], (SLOTS, LEN, D), 1.0, 6.0, ((0, 2), (1, 16))),
        "out_grad": bell_draw(arg_keys[1], (SLOTS, LEN, D), 1.0, 6.0, ((0, 2), (1, 16))),
        "order": jax.random.permutation(arg_keys[2], SLOTS).astype(jnp.int32),
        "lengths": uneven_parts(arg_keys[3], SLOTS, SLOTS * LEN * 5 // 8, LEN, 2).astype(jnp.int32),
        "first_gain": jnp.clip(1.0 + 0.15 * jax.random.normal(arg_keys[4], (D,), jnp.float32), 0.25, 1.75).astype(jnp.bfloat16),
        "first_shift": bell_draw(arg_keys[5], (D,), 0.5, 3.0, ((0, 32),)),
        "query_weight": bell_draw(arg_keys[6], (D, D), D ** -0.5, 0.1875, ((0, 32),)),
        "query_bias": bell_draw(arg_keys[7], (D,), 0.5, 3.0, ((0, 32),)),
        "key_weight": bell_draw(arg_keys[8], (D, D), D ** -0.5, 0.1875, ((0, 32),)),
        "value_weight": bell_draw(arg_keys[9], (D, D), D ** -0.5, 0.1875, ((0, 32),)),
        "value_bias": bell_draw(arg_keys[10], (D,), 0.5, 3.0, ((0, 32),)),
        "output_weight": bell_draw(arg_keys[11], (D, D), 4 ** -0.5, 3.0, ((0, 32),)),
        "output_bias": bell_draw(arg_keys[12], (D,), 0.5, 3.0, ((0, 32),)),
        "second_gain": jnp.clip(1.0 + 0.15 * jax.random.normal(arg_keys[13], (D,), jnp.float32), 0.25, 1.75).astype(jnp.bfloat16),
        "second_shift": bell_draw(arg_keys[14], (D,), 0.5, 3.0, ((0, 32),)),
        "up_weight": bell_draw(arg_keys[15], (D, FF), D ** -0.5, 0.1875, ((0, 32),)),
        "up_bias": bell_draw(arg_keys[16], (FF,), 0.5, 3.0, ((0, 32),)),
        "down_weight": bell_draw(arg_keys[17], (FF, D), FF ** -0.5, 0.09375, ((0, 32),)),
        "down_bias": bell_draw(arg_keys[18], (D,), 0.5, 3.0, ((0, 32),)),
    }


@jax.custom_vjp
def low(v):
    return lax.optimization_barrier(v.astype(jnp.bfloat16)).astype(jnp.float32)

@jax.custom_vjp
def low_back(v):
    return v

def low_keep(v):
    return (low(v), None)

def low_pass(kept, grad):
    return (grad,)

def back_keep(v):
    return (v, None)

def back_low(kept, grad):
    return (low(grad),)
low.defvjp(low_keep, low_pass)
low_back.defvjp(back_keep, back_low)
highest = lax.Precision.HIGHEST
norm_eps = 1e-05

def matmul(left, right):
    return jnp.dot(left, right, precision=highest, preferred_element_type=jnp.float32)

def layer_norm(rows, gain, shift):
    average = lax.optimization_barrier(jnp.mean(rows, axis=-1, keepdims=True))
    centered = rows - average
    scaled = centered * lax.rsqrt(lax.optimization_barrier(jnp.mean(centered * centered, axis=-1, keepdims=True)) + norm_eps)
    return scaled * gain + shift

def attend_block(q_block, k_heads, v_heads, key_valid):
    scores = jnp.einsum('qhe,khe->hqk', q_block, k_heads, precision=highest)
    scores = low_back(scores)
    scores = jnp.where(key_valid[None, None, :], scores, jnp.float32(-1e+30))
    row_max = lax.optimization_barrier(jnp.max(scores, axis=-1, keepdims=True))
    exp_scores = jnp.exp(scores - row_max)
    probs = exp_scores / lax.optimization_barrier(jnp.sum(exp_scores, axis=-1, keepdims=True))
    return jnp.einsum('hqk,khe->qhe', low(probs), v_heads, precision=highest)

def layer(rows, params, key_valid):
    first_gain, first_shift, query_weight, query_bias, key_weight, value_weight, value_bias, output_weight, output_bias, second_gain, second_shift, up_weight, up_bias, down_weight, down_bias = params
    length = rows.shape[0]
    block = min(512, length)
    blocks = length // block
    h_first = low(layer_norm(rows, first_gain, first_shift))
    q_all = low_back(low((matmul(h_first, query_weight) + query_bias) * 0.125))
    k_all = low_back(low(matmul(h_first, key_weight)))
    v_all = low_back(low(matmul(h_first, value_weight) + value_bias))
    q_blocks = q_all.reshape(blocks, block, HEADS, HEAD)
    k_heads = k_all.reshape(length, HEADS, HEAD)
    v_heads = v_all.reshape(length, HEADS, HEAD)
    attended = lax.map(jax.checkpoint(partial(attend_block, k_heads=k_heads, v_heads=v_heads, key_valid=key_valid)), q_blocks)
    mixed = low_back(low(attended.reshape(length, HEADS * HEAD)))
    branch = low_back(matmul(mixed, output_weight) + output_bias)
    middle = rows + branch
    h_second = low(layer_norm(middle, second_gain, second_shift))
    pre_act = low_back(matmul(h_second, up_weight) + up_bias)
    act = low(jax.nn.gelu(pre_act, approximate=False))
    return middle + matmul(act, down_weight) + down_bias

def reference(frames, out_grad, order, lengths, first_gain, first_shift, query_weight, query_bias, key_weight, value_weight, value_bias, output_weight, output_bias, second_gain, second_shift, up_weight, up_bias, down_weight, down_bias):
    params = tuple((p_arr.astype(jnp.float32) for p_arr in (first_gain, first_shift, query_weight, query_bias, key_weight, value_weight, value_bias, output_weight, output_bias, second_gain, second_shift, up_weight, up_bias, down_weight, down_bias)))
    slot_lengths = lengths[order.astype(jnp.int32)]
    valid_all = jnp.arange(LEN, dtype=jnp.int32)[None, :] < slot_lengths[:, None]

    def one_slot(totals, entries):
        slot_rows, slot_grad, slot_valid = entries

        def forward(rows_in, params_in):
            return layer(rows_in, params_in, slot_valid)
        result, pull = jax.vjp(forward, slot_rows.astype(jnp.float32), params)
        rows_grad, params_grad = pull(slot_grad.astype(jnp.float32))
        totals = tuple((acc + new_val for acc, new_val in zip(totals, params_grad)))
        return (totals, (result.astype(jnp.bfloat16), rows_grad.astype(jnp.bfloat16)))
    zeros_init = tuple((jnp.zeros(p_arr.shape, jnp.float32) for p_arr in params))
    totals, (outputs, grads) = lax.scan(one_slot, zeros_init, (frames, out_grad, valid_all))
    return (outputs, grads, totals[0], totals[1], totals[2], totals[3], totals[4], totals[5], totals[6], totals[7], totals[8], totals[9], totals[10], totals[11], totals[12], totals[13], totals[14])
```

```python
import functools

import jax
import jax.numpy as jnp
from jax import lax
from jax.experimental import pallas as pl
from jax.experimental.pallas import tpu as pltpu
from jax.sharding import PartitionSpec as P

HEAD = 64
f32 = jnp.float32
bf16 = jnp.bfloat16
norm_eps = 1e-05
inv_root_two = 0.7071067811865476
inv_root_tau = 0.3989422804014327
NT = (((1,), (1,)), ((), ()))
NN = (((1,), (0,)), ((), ()))
MIB = 1024 * 1024


def dot(a, b, dims=NN):
    return lax.dot_general(a, b, dims, preferred_element_type=f32)


def normalize(rows):
    average = jnp.mean(rows, axis=-1, keepdims=True)
    centered = rows - average
    inv_std = lax.rsqrt(jnp.mean(centered * centered, axis=-1, keepdims=True) + norm_eps)
    return centered * inv_std, inv_std


def norm_back(grad_rows, scaled, inv_std, gain):
    grad_hat = grad_rows * gain
    return inv_std * (
        grad_hat
        - jnp.mean(grad_hat, axis=-1, keepdims=True)
        - scaled * jnp.mean(grad_hat * scaled, axis=-1, keepdims=True)
    )


def vmem_call(kernel, meta, args, outs, name, flops, scratch=(), limit=40):
    spec = pl.BlockSpec(memory_space=pltpu.VMEM)
    nbytes = sum(a.size * a.dtype.itemsize for a in list(args) + list(outs))
    return pl.pallas_call(
        kernel,
        out_shape=tuple(outs),
        in_specs=[pl.BlockSpec(memory_space=pltpu.SMEM)] + [spec] * len(args),
        out_specs=tuple([spec] * len(outs)),
        scratch_shapes=list(scratch),
        compiler_params=pltpu.CompilerParams(vmem_limit_bytes=limit * MIB),
        cost_estimate=pl.CostEstimate(flops=int(flops), bytes_accessed=int(nbytes), transcendentals=0),
        name=name,
    )(meta, *args)


def sds(shape, dtype):
    return jax.ShapeDtypeStruct(shape, dtype)


def qkv_kernel(n, meta, *refs):
    xs = refs[: 2 * n]
    w, vec, bq, bv, x_out, h_out, q_out, k_out, v_out = refs[2 * n :]
    j = meta[0]
    half = xs[0].shape[0]
    hd = bq.shape[1]
    for r in range(n):
        m = j ^ r
        base = pl.multiple_of(m * (2 * half), 2 * half)
        for part in range(2):
            rows = xs[2 * r + part][...]
            at = pl.ds(base + part * half, half)
            x_out[at, :] = rows
            scaled, _ = normalize(rows.astype(f32))
            h_out[at, :] = (scaled * vec[0:1, :] + vec[1:2, :]).astype(bf16)
        at = pl.ds(base, 2 * half)
        qkv = dot(h_out[at, :], w[...])
        q_out[at, :] = ((qkv[:, :hd] + bq[...]) * 0.125).astype(bf16)
        k_out[at, :] = qkv[:, hd : 2 * hd].astype(bf16)
        v_out[at, :] = (qkv[:, 2 * hd :] + bv[...]).astype(bf16)


def key_mask(meta, rows, n, half, width):
    row = lax.broadcasted_iota(jnp.int32, (rows, width), 0)
    member = row // (2 * half)
    inside = row % (2 * half)
    own = (inside < half).astype(jnp.int32)
    h = meta[1]
    block_half = own * h + (1 - own) * (1 - h)
    frame = (block_half * n + member) * half + inside % half
    return frame < meta[2]


def attend_kernel(n, half, qb, meta, q, k, v, o_out, lse_out, bias):
    total = k.shape[0]
    heads = k.shape[1] // HEAD
    bias[...] = jnp.where(key_mask(meta, total, n, half, 128), 0.0, -1.0).astype(f32)
    for head in range(heads):
        cols = slice(head * HEAD, (head + 1) * HEAD)
        kh = k[:, cols]
        vt = v[:, cols].astype(f32).T.astype(bf16)

        def step(i, _, cols=cols, kh=kh, vt=vt, head=head):
            at = pl.ds(pl.multiple_of(i * qb, qb), qb)
            scores = dot(kh, q[at, cols], NT)
            valid = bias[:, 0:1] >= 0.0
            scores = jnp.where(valid, scores, -1e30)
            row_max = jnp.max(scores, axis=0, keepdims=True)
            e = jnp.exp(scores - row_max)
            row_sum = jnp.sum(e, axis=0, keepdims=True)
            ot = dot(vt, e.astype(bf16)) / row_sum
            o_out[at, cols] = ot.T.astype(bf16)
            lse_out[pl.ds(head, 1), at] = row_max + jnp.log(row_sum)
            return 0

        lax.fori_loop(0, total // qb, step, 0)


def mid_kernel(n, meta, o_in, w_out, x_own, x_recv, vec, y_out, h_out, cat):
    hd = o_in.shape[2]
    half = x_own.shape[0]
    for m in range(n):
        cat[:, m * hd : (m + 1) * hd] = o_in[m]
    y = dot(cat[...], w_out[...]) + vec[4:5, :]
    y_out[:half, :] = y[:half] + x_own[...].astype(f32)
    y_out[half:, :] = y[half:] + x_recv[...].astype(f32)
    scaled, _ = normalize(y_out[...])
    h_out[...] = (scaled * vec[5:6, :] + vec[6:7, :]).astype(bf16)


def down_back_kernel(n, meta, *refs):
    dys = refs[:n]
    w_down, dy_out, dg_out = refs[n:]
    j = meta[0]
    rows = dys[0].shape[0]
    for r in range(n):
        at = pl.ds(pl.multiple_of((j ^ r) * rows, rows), rows)
        dy = dys[r][...]
        dy_out[at, :] = dy
        dg_out[at, :] = dot(dy, w_down[...], NT)


def ffn_kernel(n, meta, *refs):
    hs = refs[:n]
    w_up, b_up, dg, h_out, g_out, du_out, keep, send, db_out = refs[n:]
    j = meta[0]
    rows = hs[0].shape[0]
    db_out[...] = jnp.zeros_like(db_out)
    for r in range(n):
        at = pl.ds(pl.multiple_of((j ^ r) * rows, rows), rows)
        h = hs[r][...]
        h_out[at, :] = h
        u = dot(h, w_up[...]) + b_up[...]
        cdf = 0.5 * (1.0 + lax.erf(u * inv_root_two))
        g_out[at, :] = (u * cdf).astype(bf16)
        slope = cdf + u * jnp.exp(-0.5 * u * u) * inv_root_tau
        du = (dg[at, :] * slope).astype(bf16)
        du_out[at, :] = du
        db_out[...] += jnp.sum(du.astype(f32), axis=0, keepdims=True)
        dh = dot(du, w_up[...], NT)
        here = slice((r // 2) * rows, (r // 2 + 1) * rows)
        if r % 2 == 0:
            keep[here, :] = dh
        else:
            send[here, :] = dh.astype(bf16)


def down_kernel(n, meta, g, w_down, keep, send):
    j = meta[0]
    rows = g.shape[0] // n
    for r in range(n):
        at = pl.ds(pl.multiple_of((j ^ r) * rows, rows), rows)
        out = dot(g[at, :], w_down[...])
        here = slice((r // 2) * rows, (r // 2 + 1) * rows)
        if r % 2 == 0:
            keep[here, :] = out
        else:
            send[here, :] = out.astype(bf16)


def pair_kernel(meta, keep, recv, *outs):
    rows = outs[0].shape[0]
    for i, out in enumerate(outs):
        here = slice(i * rows, (i + 1) * rows)
        out[...] = (keep[here, :] + recv[here, :].astype(f32)).astype(out.dtype)


def out_kernel(count, meta, *refs):
    own, y = refs[0], refs[count]
    vec, kept, sent = refs[count + 1 :]
    total = own[...]
    for i in range(1, count):
        total = total + refs[i][...].astype(f32)
    out = (y[...] + total + vec[7:8, :]).astype(bf16)
    half = kept.shape[0]
    kept[...] = out[:half]
    sent[...] = out[half:]


def mid_back_kernel(n, count, meta, *refs):
    own = refs[0]
    y, dy, vec, w_out = refs[count : count + 4]
    dy1_out, da_out, do_out, small = refs[count + 4 :]
    dh = own[...]
    for i in range(1, count):
        dh = dh + refs[i][...].astype(f32)
    scaled, inv_std = normalize(y[...])
    dyf = dy[...].astype(f32)
    dy1 = dyf + norm_back(dh, scaled, inv_std, vec[5:6, :])
    dy1_out[...] = dy1
    da = dy1.astype(bf16)
    da_out[...] = da
    small[0:1, :] = jnp.sum(dh * scaled, axis=0, keepdims=True)
    small[1:2, :] = jnp.sum(dh, axis=0, keepdims=True)
    small[2:3, :] = jnp.sum(da.astype(f32), axis=0, keepdims=True)
    small[3:4, :] = jnp.sum(dyf, axis=0, keepdims=True)
    hd = do_out.shape[2]
    for m in range(n):
        do_out[m] = dot(da, w_out[m * hd : (m + 1) * hd, :], NT).astype(bf16)


def attend_back_kernel(n, half, qb, meta, q, k, v, do, lse, w, dqkv, keep, send, db, bias, acc_k, acc_v):
    total = k.shape[0]
    hd = k.shape[1]
    heads = hd // HEAD
    bias[...] = jnp.where(key_mask(meta, total, n, half, 128), 0.0, -1.0).astype(f32)
    for head in range(heads):
        cols = slice(head * HEAD, (head + 1) * HEAD)
        kh = k[:, cols]
        vh = v[:, cols]
        kt = kh.astype(f32).T.astype(bf16)
        acc_k[...] = jnp.zeros_like(acc_k)
        acc_v[...] = jnp.zeros_like(acc_v)

        def step(i, _, cols=cols, kh=kh, vh=vh, kt=kt, head=head):
            at = pl.ds(pl.multiple_of(i * qb, qb), qb)
            qh = q[at, cols]
            doh = do[at, cols]
            scores = dot(kh, qh, NT)
            valid = bias[:, 0:1] >= 0.0
            probs = jnp.where(valid, jnp.exp(scores - lse[pl.ds(head, 1), at]), 0.0)
            dp = dot(vh, doh, NT)
            centre = jnp.sum(probs * dp, axis=0, keepdims=True)
            ds = (probs * (dp - centre)).astype(bf16)
            acc_v[...] += dot(probs.astype(bf16), doh)
            acc_k[...] += dot(ds, qh)
            dq = dot(kt, ds)
            dqkv[at, cols] = (dq.T.astype(bf16).astype(f32) * 0.125).astype(bf16)
            return 0

        lax.fori_loop(0, total // qb, step, 0)
        dqkv[:, hd + head * HEAD : hd + (head + 1) * HEAD] = acc_k[...].astype(bf16)
        dqkv[:, 2 * hd + head * HEAD : 2 * hd + (head + 1) * HEAD] = acc_v[...].astype(bf16)
    j = meta[0]
    rows = 2 * half
    db[...] = jnp.zeros_like(db)
    for r in range(n):
        at = pl.ds(pl.multiple_of((j ^ r) * rows, rows), rows)
        grads = dqkv[at, :]
        db[...] += jnp.sum(grads.astype(f32), axis=0, keepdims=True)
        dh = dot(grads, w[...], NT)
        here = slice((r // 2) * rows, (r // 2 + 1) * rows)
        if r % 2 == 0:
            keep[here, :] = dh
        else:
            send[here, :] = dh.astype(bf16)


def first_small_kernel(meta, x, dqkv, w, small):
    rows = 128
    small[...] = jnp.zeros_like(small)

    def step(i, _):
        at = pl.ds(pl.multiple_of(i * rows, rows), rows)
        dh = dot(dqkv[at, :], w[...], NT)
        scaled, _ = normalize(x[at, :].astype(f32))
        small[0:1, :] += jnp.sum(dh * scaled, axis=0, keepdims=True)
        small[1:2, :] += jnp.sum(dh, axis=0, keepdims=True)
        return 0

    lax.fori_loop(0, x.shape[0] // rows, step, 0)


def place_kernel(meta, *refs):
    out = refs[-1]
    for r, piece in enumerate(refs[:-1]):
        m = meta[0] ^ r
        for i in range(out.shape[0]):
            out[i, m] = piece[i]


def last_kernel(count, meta, *refs):
    own = refs[0]
    x_own, x_recv, dy1, vec, kept, sent = refs[count:]
    half = kept.shape[0]
    for part, (x, out) in enumerate(((x_own, kept), (x_recv, sent))):
        at = slice(part * half, (part + 1) * half)
        dh = own[at, :]
        for i in range(1, count):
            dh = dh + refs[i][at, :].astype(f32)
        scaled, inv_std = normalize(x[...].astype(f32))
        out[...] = (dy1[at, :] + norm_back(dh, scaled, inv_std, vec[0:1, :])).astype(bf16)


def on_device(
    dp_size,
    seq_size,
    frames,
    out_grad,
    order,
    lengths,
    first_gain,
    first_shift,
    query_weight,
    query_bias,
    key_weight,
    value_weight,
    value_bias,
    output_weight,
    output_bias,
    second_gain,
    second_shift,
    up_weight,
    up_bias,
    down_weight,
    down_bias,
):
    slots, half, width = frames.shape
    n = seq_size // slots
    groups = dp_size * slots
    ndev = dp_size * seq_size
    hd = width // n
    rs = query_weight.shape[0]
    hidden = up_weight.shape[1]
    chunk = hidden // ndev
    mine = hidden // n
    rows = 2 * half
    total = n * rows
    both = ("dp", "seq")

    dp_at = lax.axis_index("dp")
    seq_at = lax.axis_index("seq")
    h = seq_at // n
    j = seq_at % n
    length = lengths[order[h]]
    meta = jnp.stack([j, h, length, dp_at]).astype(jnp.int32)

    def xor(value, bit):
        return lax.ppermute(value, "seq", [(i, i ^ bit) for i in range(seq_size)])

    def xor_dp(value, bit):
        return lax.ppermute(value, "dp", [(i, i ^ bit) for i in range(dp_size)])

    def gather(value):
        got = [value] + [xor(value, r) for r in range(n - 2, 0, -2)]
        even = [got[0]] + got[1:][::-1]
        out = []
        for piece in even:
            out += [piece, xor(piece, 1)]
        return out

    def scatter(keep, send):
        recv = xor(send, 1)
        pieces = vmem_call(
            pair_kernel,
            meta,
            [keep, recv],
            [sds((rows, width), f32)] + [sds((rows, width), bf16)] * (n // 2 - 1),
            "pair",
            keep.size,
        )
        return [pieces[0]] + [xor(pieces[i], 2 * i) for i in range(n // 2 - 1, 0, -1)]

    def take_half(value, bit):
        keep = lax.dynamic_index_in_dim(value, bit, 0, keepdims=False)
        send = lax.dynamic_index_in_dim(value, 1 - bit, 0, keepdims=False)
        return keep, send.astype(bf16)

    bits = []
    step = dp_size // 2
    while step:
        bits.append(step)
        step //= 2

    def gather_groups(value):
        other = xor(value, n)
        value = jnp.where(h == 0, jnp.stack([value, other]), jnp.stack([other, value]))
        for bit in bits[::-1]:
            other = xor_dp(value, bit)
            low = (dp_at & bit) == 0
            value = jnp.where(low, jnp.concatenate([value, other]), jnp.concatenate([other, value]))
        return value

    def reduce_groups(value):
        for bit in bits:
            value = value.reshape((2, value.shape[0] // 2) + value.shape[1:])
            keep, send = take_half(value, (dp_at & bit) // bit)
            value = keep.astype(f32) + xor_dp(send, bit).astype(f32)
        keep, send = take_half(value, h)
        return keep.astype(f32) + xor(send, n).astype(f32)

    def members(value):
        index = [[s * n + i for i in range(n)] for s in range(slots)]
        return lax.all_to_all(value, "seq", 0, 0, tiled=True, axis_index_groups=index)

    x_own = lax.dynamic_index_in_dim(frames, h, 0, keepdims=False)
    x_recv = xor(lax.dynamic_index_in_dim(frames, 1 - h, 0, keepdims=False), n)
    xs = []
    for a, b in zip(gather(x_own), gather(x_recv)):
        xs += [a, b]

    block_rows = -(-(rs + 1) // 8) * 8
    small_in = [first_gain, first_shift, query_bias, value_bias, output_bias, second_gain, second_shift, down_bias]
    tail = jnp.concatenate(small_in + [up_bias])
    tail = jnp.pad(tail, (0, 3 * hd - tail.shape[0]))
    by_head = jnp.concatenate(
        [w.reshape(rs, n, hd).transpose(1, 0, 2) for w in (query_weight, key_weight, value_weight)], axis=2
    )
    by_head = jnp.concatenate(
        [
            by_head,
            jnp.broadcast_to(tail[None, None, :], (n, 1, 3 * hd)),
            jnp.zeros((n, block_rows - rs - 1, 3 * hd), bf16),
        ],
        axis=1,
    )
    everyone = jnp.broadcast_to(by_head[None], (groups,) + by_head.shape).reshape(ndev, block_rows, 3 * hd)
    got = lax.all_to_all(everyone, both, 0, 0, tiled=True)
    w_qkv = got[:, :rs, :].reshape(width, 3 * hd)
    vec = got[:, rs, : 8 * rs].reshape(ndev, 8, rs).transpose(1, 0, 2).reshape(8, width).astype(f32)
    bias_up = got[:, rs, 8 * rs : 8 * rs + chunk].reshape(groups, n, chunk)
    bias_up = lax.dynamic_index_in_dim(bias_up, j, 1, keepdims=False).reshape(1, mine).astype(f32)
    bias_q = lax.dynamic_slice(vec, (2, j * hd), (1, hd))
    bias_v = lax.dynamic_slice(vec, (3, j * hd), (1, hd))

    up_mine = up_weight.reshape(rs, groups, n, chunk).transpose(2, 0, 1, 3).reshape(n, rs, mine)
    up_mine = members(up_mine).reshape(n * rs, mine)
    w_up = gather_groups(up_mine).reshape(width, mine)
    w_down = gather_groups(down_weight).reshape(mine, width)

    out_mine = gather_groups(output_weight)
    out_all = gather(out_mine)
    (w_out,) = vmem_call(place_kernel, meta, out_all, [sds((groups, n, rs, width), bf16)], "place", width * width)
    w_out = w_out.reshape(width, width)

    x_all, h_first, q, k, v = vmem_call(
        functools.partial(qkv_kernel, n),
        meta,
        xs + [w_qkv, vec, bias_q, bias_v],
        [sds((total, width), bf16)] * 2 + [sds((total, hd), bf16)] * 3,
        "qkv",
        2 * total * width * 3 * hd,
    )
    qb = min(256, total)
    o_heads, lse = vmem_call(
        functools.partial(attend_kernel, n, half, qb),
        meta,
        [q, k, v],
        [sds((total, hd), bf16), sds((hd // HEAD, total), f32)],
        "attend",
        8 * total * total * hd,
        scratch=[pltpu.VMEM((total, 128), f32)],
    )
    o_rows = members(o_heads.reshape(n, rows, hd))
    y1, h2 = vmem_call(
        functools.partial(mid_kernel, n),
        meta,
        [o_rows, w_out, x_own, x_recv, vec],
        [sds((rows, width), f32), sds((rows, width), bf16)],
        "mid",
        2 * rows * width * width,
        scratch=[pltpu.VMEM((rows, width), bf16)],
    )

    dy_own = lax.dynamic_index_in_dim(out_grad, h, 0, keepdims=False)
    dy_recv = xor(lax.dynamic_index_in_dim(out_grad, 1 - h, 0, keepdims=False), n)
    dy = jnp.concatenate([dy_own, dy_recv])
    dy_all, dg = vmem_call(
        functools.partial(down_back_kernel, n),
        meta,
        gather(dy) + [w_down],
        [sds((total, width), bf16), sds((total, mine), f32)],
        "down_back",
        2 * total * width * mine,
    )

    part = [sds((total // 2, width), f32), sds((total // 2, width), bf16)]
    h2_all, g, du, keep, send, d_bias_up = vmem_call(
        functools.partial(ffn_kernel, n),
        meta,
        gather(h2) + [w_up, bias_up, dg],
        [sds((total, width), bf16)] + [sds((total, mine), bf16)] * 2 + part + [sds((1, mine), f32)],
        "ffn",
        4 * total * width * mine,
    )
    dh2 = scatter(keep, send)
    dy1, da, do_rows, small_two = vmem_call(
        functools.partial(mid_back_kernel, n, n // 2),
        meta,
        dh2 + [y1, dy, vec, w_out],
        [sds((rows, width), f32), sds((rows, width), bf16), sds((n, rows, hd), bf16), sds((4, width), f32)],
        "mid_back",
        2 * rows * width * width,
    )
    do_heads = members(do_rows).reshape(total, hd)

    keep, send = vmem_call(
        functools.partial(down_kernel, n), meta, [g, w_down], part, "down", 2 * total * width * mine
    )
    kept, sent = vmem_call(
        functools.partial(out_kernel, n // 2),
        meta,
        scatter(keep, send) + [y1, vec],
        [sds((half, width), bf16)] * 2,
        "out",
        rows * width,
    )
    other = xor(sent, n)
    output = jnp.where(h == 0, jnp.stack([kept, other]), jnp.stack([other, kept]))

    d_qkv, keep, send, d_bias_qkv = vmem_call(
        functools.partial(attend_back_kernel, n, half, qb),
        meta,
        [q, k, v, do_heads, lse, w_qkv],
        [sds((total, 3 * hd), bf16)] + part + [sds((1, 3 * hd), f32)],
        "attend_back",
        20 * total * total * hd,
        scratch=[pltpu.VMEM((total, 128), f32), pltpu.VMEM((total, HEAD), f32), pltpu.VMEM((total, HEAD), f32)],
    )
    dh1 = scatter(keep, send)
    (small_one,) = vmem_call(
        first_small_kernel, meta, [x_all, d_qkv, w_qkv], [sds((2, width), f32)], "first_small", 6 * total * width * hd
    )
    kept, sent = vmem_call(
        functools.partial(last_kernel, n // 2),
        meta,
        dh1 + [x_own, x_recv, dy1, vec],
        [sds((half, width), bf16)] * 2,
        "last",
        rows * width,
    )
    other = xor(sent, n)
    frames_grad = jnp.where(h == 0, jnp.stack([kept, other]), jnp.stack([other, kept]))

    d_down = jnp.einsum("rf,rd->fd", g, dy_all, preferred_element_type=f32)
    d_down = reduce_groups(d_down.reshape(groups, chunk, width))
    d_up = jnp.einsum("rd,rf->df", h2_all, du, preferred_element_type=f32)
    d_up = reduce_groups(d_up.reshape(groups, n * rs, mine))
    d_qkv_w = jnp.einsum("rd,rf->df", h_first, d_qkv, preferred_element_type=f32)
    d_qkv_w = reduce_groups(d_qkv_w.reshape(groups, n * rs, 3 * hd))
    da_all = gather(da)
    da_all = [piece[None] for piece in da_all]
    (da_all,) = vmem_call(place_kernel, meta, da_all, [sds((1, n, rows, width), bf16)], "place", width * total)
    da_all = da_all.reshape(total, width)
    d_out = jnp.einsum("rf,rd->fd", o_heads, da_all, preferred_element_type=f32)
    back = jnp.concatenate([d_up.reshape(n, rs, mine), d_qkv_w.reshape(n, rs, 3 * hd)], axis=2).astype(bf16)
    back = members(back).astype(f32)
    up_weight_grad = back[:, :, :mine].reshape(n, rs, groups, chunk).transpose(1, 2, 0, 3).reshape(rs, hidden)
    qkv_grad = back[:, :, mine:].transpose(1, 0, 2).reshape(rs, n, 3, hd)
    query_weight_grad, key_weight_grad, value_weight_grad = (
        qkv_grad[:, :, i, :].reshape(rs, width) for i in range(3)
    )

    group = dp_at * slots + h
    d_out = d_out.reshape(groups, rs, width)
    output_weight_grad = None
    for k_step in range(groups):
        pairs = []
        for d in range(ndev):
            g_of, j_of = (d // seq_size) * slots + (d % seq_size) // n, d % n
            pairs.append((d, j_of * groups + (g_of + k_step) % groups))
        piece = lax.dynamic_index_in_dim(d_out, (group + k_step) % groups, 0, keepdims=False)
        piece = lax.ppermute(piece.astype(bf16), both, pairs).astype(f32)
        output_weight_grad = piece if output_weight_grad is None else output_weight_grad + piece

    vectors = jnp.zeros((2, width), f32)
    vectors = lax.dynamic_update_slice(vectors, d_bias_qkv[:, :hd], (0, j * hd))
    vectors = lax.dynamic_update_slice(vectors, d_bias_qkv[:, 2 * hd :], (1, j * hd))
    vectors = jnp.concatenate([small_one, small_two, vectors])
    vectors = vectors.reshape(8, ndev, rs).transpose(1, 0, 2).reshape(ndev, 8 * rs)
    spread = jnp.zeros((groups, n, chunk), f32)
    spread = lax.dynamic_update_slice(spread, d_bias_up.reshape(groups, 1, chunk), (0, j, 0))
    vectors = jnp.concatenate([vectors, spread.reshape(ndev, chunk)], axis=1)
    vectors = lax.all_to_all(vectors[:, None, :], both, 0, 0, tiled=True)
    vectors = jnp.sum(vectors, axis=(0, 1))
    singles = vectors[: 8 * rs].reshape(8, rs)
    return (
        output,
        frames_grad,
        singles[0],
        singles[1],
        query_weight_grad,
        singles[6],
        key_weight_grad,
        value_weight_grad,
        singles[7],
        output_weight_grad,
        singles[4],
        singles[2],
        singles[3],
        up_weight_grad,
        vectors[8 * rs :],
        d_down,
        singles[5],
    )


def solution(mesh):
    vector = P(("dp", "seq"))
    matrix = P(("dp", "seq"), None)
    rows = P("dp", "seq", None)
    return jax.shard_map(
        functools.partial(on_device, mesh.shape["dp"], mesh.shape["seq"]),
        mesh=mesh,
        in_specs=(
            rows,
            rows,
            P("dp"),
            P(),
            vector,
            vector,
            matrix,
            vector,
            matrix,
            matrix,
            vector,
            matrix,
            vector,
            vector,
            vector,
            matrix,
            vector,
            matrix,
            vector,
        ),
        out_specs=(
            rows,
            rows,
            vector,
            vector,
            matrix,
            vector,
            matrix,
            matrix,
            vector,
            matrix,
            vector,
            vector,
            vector,
            matrix,
            vector,
            matrix,
            vector,
        ),
        check_vma=False,
    )
```

```python
import functools

import jax
import jax.numpy as jnp
from jax import lax
from jax.experimental import pallas as pl
from jax.experimental.pallas import tpu as pltpu
from jax.sharding import PartitionSpec as P

HEAD = 64
f32 = jnp.float32
bf16 = jnp.bfloat16
norm_eps = 1e-05
inv_root_two = 0.7071067811865476
inv_root_tau = 0.3989422804014327
NN = (((1,), (0,)), ((), ()))
NT = (((1,), (1,)), ((), ()))
TN = (((0,), (0,)), ((), ()))
MIB = 1024 * 1024


def dot(a, b, dims=NN):
    return lax.dot_general(a, b, dims, preferred_element_type=f32)


def normalize(rows):
    average = jnp.mean(rows, axis=-1, keepdims=True)
    centered = rows - average
    inv_std = lax.rsqrt(jnp.mean(centered * centered, axis=-1, keepdims=True) + norm_eps)
    return centered * inv_std, inv_std


def norm_back(grad_rows, scaled, inv_std, gain):
    grad_hat = grad_rows * gain
    return inv_std * (
        grad_hat
        - jnp.mean(grad_hat, axis=-1, keepdims=True)
        - scaled * jnp.mean(grad_hat * scaled, axis=-1, keepdims=True)
    )


def sds(shape, dtype):
    return jax.ShapeDtypeStruct(shape, dtype)


def vmem(like):
    return pltpu.VMEM(like.shape, like.dtype)


class Near:
    def __init__(self, array):
        self.array = array
        self.shape, self.dtype = array.shape, array.dtype


def near(arrays):
    return [Near(a) for a in arrays]


class Place:
    def __init__(self, slots, n):
        seq_at = lax.axis_index("seq")
        self.h, self.j = seq_at // n, seq_at % n
        self.group = lax.axis_index("dp") * slots + self.h
        self.length = None


def call(grid, kernel, args, outs, name, flops=0, scratch=(), sems=1, limit=24, lengths=()):
    here = pl.BlockSpec(memory_space=pltpu.HBM)
    anywhere = pl.BlockSpec(memory_space=pl.ANY)
    scalars = pl.BlockSpec(memory_space=pltpu.SMEM)
    nbytes = sum(a.shape[0] * a.shape[1] * a.dtype.itemsize for a in list(args) + list(outs))

    def body(*refs):
        place = Place(*grid)
        if lengths:
            order_ref, lengths_ref = refs[:2]
            place.length = lengths_ref[order_ref[place.h]]
        kernel(place, *refs[len(lengths) :])

    return pl.pallas_call(
        body,
        out_shape=tuple(o.array if isinstance(o, Near) else pltpu.HBM(o.shape, o.dtype) for o in outs),
        in_specs=[scalars] * len(lengths) + [anywhere if isinstance(a, Near) else here for a in args],
        out_specs=tuple(anywhere if isinstance(o, Near) else here for o in outs),
        scratch_shapes=list(scratch) + [pltpu.SemaphoreType.DMA((sems,))],
        compiler_params=pltpu.CompilerParams(vmem_limit_bytes=limit * MIB),
        cost_estimate=pl.CostEstimate(flops=int(flops), bytes_accessed=int(nbytes), transcendentals=0),
        name=name,
    )(
        *lengths,
        *[a.array if isinstance(a, Near) else pltpu.with_memory_space_constraint(a, pltpu.HBM) for a in args],
    )


class Mover:
    def __init__(self, sems):
        self.sems, self.used, self.open = sems, 0, []

    def start(self, source, target):
        copy = pltpu.make_async_copy(source, target, self.sems.at[self.used])
        self.used += 1
        copy.start()
        return copy

    def put(self, source, target):
        self.open.append(self.start(source, target))

    def drain(self):
        for copy in self.open:
            copy.wait()
        self.open = []


def cost(microseconds):
    return microseconds * 1150 * 10**6


def after(value, *others):
    return lax.optimization_barrier((value,) + others)[0]


def rows_at(index, rows):
    return pl.ds(pl.multiple_of(index * rows, rows), rows)


def pack_kernel(n, groups, first_row, place, *refs):
    frames, out_grad, wq, wk, wv, up = refs[:6]
    small = refs[6:15]
    x_own, x_send, dy_own, dy_send, packed, q_s, k_s, v_s, up_s, *rest = refs[15:]
    small_s, packed_s, sems = rest[:9], rest[9], rest[10]
    move = Mover(sems)
    for rows, own, sent in ((frames, x_own, x_send), (out_grad, dy_own, dy_send)):
        move.put(rows.at[1 - place.h], sent)
        move.put(rows.at[place.h], own)
    loads = [move.start(a, b) for a, b in ((wq, q_s), (wk, k_s), (wv, v_s), (up, up_s))]
    loads += [move.start(a, b) for a, b in zip(small, small_s)]
    for copy in loads:
        copy.wait()
    rs = wq.shape[0]
    hd = wq.shape[1] // n
    chunk = small[8].shape[1]
    zeros = jnp.zeros((packed_s.shape[1] - rs, packed_s.shape[2]), bf16)
    for m in range(n):
        cols = slice(m * hd, (m + 1) * hd)
        packed_s[m, rs:, :] = zeros
        packed_s[m, :rs, :hd] = q_s[:, cols]
        packed_s[m, :rs, hd : 2 * hd] = k_s[:, cols]
        packed_s[m, :rs, 2 * hd : 3 * hd] = v_s[:, cols]
        for g in range(groups):
            at = (g * n + m) * chunk
            packed_s[m, :rs, 3 * hd + g * chunk : 3 * hd + (g + 1) * chunk] = up_s[:, at : at + chunk]
        for i in range(8):
            packed_s[m, first_row + i : first_row + i + 1, :rs] = small_s[i][...]
        packed_s[m, first_row : first_row + 1, hd : hd + chunk] = small_s[8][...]
    move.put(packed_s, packed)
    move.drain()


def join_kernel(n, place, got, out_w, down, attn, ffn, got_s, out_s, attn_s, up_s, sems):
    move = Mover(sems)
    load, more = move.start(got, got_s), move.start(out_w, out_s)
    width, mine = down.shape[1], ffn.shape[1]
    chunk = down.shape[0]
    feats = ffn.shape[0] - width // mine * chunk
    for c in range(width // mine):
        move.put(down.at[:, c * mine : (c + 1) * mine], ffn.at[feats + c * chunk : feats + (c + 1) * chunk, :])
    load.wait()
    more.wait()
    hd = width // n
    rs = feats // n
    attn_s[:, :, : 3 * hd] = got_s[:, :, : 3 * hd]
    attn_s[:, :, 3 * hd :] = jnp.zeros((n, attn_s.shape[1], hd), bf16)
    for m in range(n):
        attn_s[m, :rs, 3 * hd :] = out_s[:, m * hd : (m + 1) * hd]
    move.put(attn_s, attn)
    for m in range(n):
        up_s[m * rs : (m + 1) * rs, :] = got_s[m, :rs, 3 * hd :]
    move.put(up_s, ffn.at[:feats, :])
    move.drain()


def key_mask(place, rows, n, half, width):
    row = lax.broadcasted_iota(jnp.int32, (rows, width), 0)
    member = row // (2 * half)
    inside = row % (2 * half)
    own = (inside < half).astype(jnp.int32)
    h = place.h
    block_half = own * h + (1 - own) * (1 - h)
    frame = (block_half * n + member) * half + inside % half
    return frame < place.length


def first_kernel(n, groups, half, qb, first_row, place, *refs):
    xs, gots = refs[:n], refs[n : n + groups]
    outs = refs[n + groups : n + groups + 11]
    hat_out, h_out, qkv_out, o_out, lse_out, w_out, vec_out, bias_up_out, wo_out, keep, send = outs
    x_s, hat_s, h_s, qkv_s, o_s, lse_s, got_s, w_s, vec_s, bias_up_s, wo_s, keep_s, send_s, bias, sems = refs[
        n + groups + 11 :
    ]
    move = Mover(sems)
    j = place.j
    rows = 2 * half
    total = n * rows
    ndev = got_s.shape[0]
    hd = got_s.shape[2] // 4
    rs = x_s.shape[1] // ndev
    chunk = bias_up_s.shape[1] // groups
    load = [move.start(gots[i], got_s.at[pl.ds((place.group ^ i) * n, n)]) for i in range(groups)]
    copies = [move.start(xs[r], x_s.at[rows_at(j ^ r, rows), :]) for r in range(n)]
    bias[...] = jnp.where(key_mask(place, total, n, half, 128), 0.0, -1.0).astype(f32)
    for copy in load:
        copy.wait()
    for d in range(ndev):
        w_s[d * rs : (d + 1) * rs, :] = got_s[d, :rs, : 3 * hd]
        at = slice(d % n * hd, (d % n + 1) * hd)
        wo_s[d // n * rs : (d // n + 1) * rs, at] = got_s[d, :rs, 3 * hd :]
        vec_s[:, d * rs : (d + 1) * rs] = got_s[d, first_row : first_row + 8, :rs].astype(f32)
    bq, bv = [], []
    for t in range(groups):
        bias_up_s[:, t * chunk : (t + 1) * chunk] = got_s[
            t * n + j, first_row : first_row + 1, hd : hd + chunk
        ].astype(f32)
        bq.append(got_s[j * groups + t, first_row + 2 : first_row + 3, :rs].astype(f32))
        bv.append(got_s[j * groups + t, first_row + 3 : first_row + 4, :rs].astype(f32))
    bq = jnp.concatenate(bq, axis=1)
    bv = jnp.concatenate(bv, axis=1)
    move.put(w_s, w_out)
    move.put(vec_s, vec_out)
    move.put(bias_up_s, bias_up_out)
    for r in range(n):
        copies[r].wait()
        base = pl.multiple_of((j ^ r) * rows, rows)
        for part in range(2):
            at = pl.ds(base + part * half, half)
            scaled, _ = normalize(x_s[at, :].astype(f32))
            hat_s[at, :] = scaled.astype(bf16)
            h_s[at, :] = (scaled * vec_s[0:1, :] + vec_s[1:2, :]).astype(bf16)
        at = pl.ds(base, rows)
        qkv = dot(h_s[at, :], w_s[...])
        qkv_s[at, :hd] = ((qkv[:, :hd] + bq) * 0.125).astype(bf16)
        qkv_s[at, hd : 2 * hd] = qkv[:, hd : 2 * hd].astype(bf16)
        qkv_s[at, 2 * hd :] = (qkv[:, 2 * hd :] + bv).astype(bf16)
    move.put(hat_s, hat_out)
    move.put(h_s, h_out)
    move.put(qkv_s, qkv_out)
    heads = hd // HEAD
    for head in range(heads):
        cols = slice(head * HEAD, (head + 1) * HEAD)
        kh = qkv_s[:, hd + head * HEAD : hd + (head + 1) * HEAD]
        vt = qkv_s[:, 2 * hd + head * HEAD : 2 * hd + (head + 1) * HEAD].astype(f32).T.astype(bf16)

        def step(i, _, cols=cols, kh=kh, vt=vt, head=head):
            at = rows_at(i, qb)
            scores = dot(kh, qkv_s[at, cols], NT)
            scores = jnp.where(bias[:, 0:1] >= 0.0, scores, -1e30)
            row_max = jnp.max(scores, axis=0, keepdims=True)
            e = jnp.exp(scores - row_max)
            row_sum = jnp.sum(e, axis=0, keepdims=True)
            ot = dot(vt, e.astype(bf16)) / row_sum
            o_s[at, cols] = ot.T.astype(bf16)
            lse_s[pl.ds(head, 1), at] = row_max + jnp.log(row_sum)
            return 0

        lax.fori_loop(0, total // qb, step, 0)
    move.put(o_s, o_out)
    move.put(lse_s, lse_out)
    move.put(wo_s, wo_out)
    for r in list(range(1, n, 2)) + list(range(0, n, 2)):
        y = dot(o_s[rows_at(j ^ r, rows), :], wo_s[...])
        here = slice((r // 2) * rows, (r // 2 + 1) * rows)
        if r % 2 == 0:
            keep_s[here, :] = y
            move.put(keep_s.at[here, :], keep.at[here, :])
        else:
            send_s[here, :] = y.astype(bf16)
            move.put(send_s.at[here, :], send.at[here, :])
    move.drain()


def mid_kernel(count, place, *refs):
    ins, x, vec = refs[:count], refs[count], refs[count + 1]
    y_out, h_out = refs[count + 2 : count + 4]
    held = refs[count + 4 : 2 * count + 4]
    x_s, vec_s, y_s, h_s, sems = refs[2 * count + 4 :]
    move = Mover(sems)
    loads = [move.start(a, b) for a, b in zip(ins, held)]
    loads += [move.start(x, x_s), move.start(vec, vec_s)]
    for copy in loads:
        copy.wait()
    y = held[0][...]
    for i in range(1, count):
        y = y + held[i][...].astype(f32)
    y = x_s[...].astype(f32) + y + vec_s[4:5, :]
    y_s[...] = y
    scaled, _ = normalize(y)
    h_s[...] = (scaled * vec_s[5:6, :] + vec_s[6:7, :]).astype(bf16)
    move.put(h_s, h_out)
    move.put(y_s, y_out)
    move.drain()


def down_back_kernel(n, groups, place, *refs):
    dys, ws = refs[:n], refs[n : n + groups]
    dy_out, dg_out, w_up_out, w_down_out, dy_s, dg_s, w_up, w_down, sems = refs[n + groups :]
    move = Mover(sems)
    j, g = place.j, place.group
    rows = dys[0].shape[0]
    chunk = w_down.shape[0] // groups
    mine = w_up.shape[1]
    feats = w_up.shape[0] // groups
    first, last = [], []
    for i in range(groups):
        for c in range(w_down.shape[1] // mine):
            source = ws[i].at[feats + c * chunk : feats + (c + 1) * chunk, :]
            first.append(move.start(source, w_down.at[rows_at(g ^ i, chunk), c * mine : (c + 1) * mine]))
    copies = [move.start(dys[r], dy_s.at[rows_at(j ^ r, rows), :]) for r in range(n)]
    for i in range(groups):
        last.append(move.start(ws[i].at[:feats, :], w_up.at[rows_at(g ^ i, feats), :]))
    for copy in first:
        copy.wait()
    move.put(w_down, w_down_out)
    for r in range(n):
        copies[r].wait()
        at = rows_at(j ^ r, rows)
        dg_s[at, :] = dot(dy_s[at, :], w_down[...], NT)
        move.put(dg_s.at[at, :], dg_out.at[at, :])
    for copy in last:
        copy.wait()
    move.put(w_up, w_up_out)
    move.put(dy_s, dy_out)
    move.drain()


def ffn_kernel(n, place, *refs):
    hs = refs[:n]
    w_up_in, b_up_in, dg_in = refs[n : n + 3]
    h_out, g_out, du_out, keep, send, db_out = refs[n + 3 : n + 9]
    w_up, b_up, dg, h_s, g_s, du_s, keep_s, send_s, db, sems = refs[n + 9 :]
    move = Mover(sems)
    j = place.j
    rows = hs[0].shape[0]
    loads = [move.start(w_up_in, w_up), move.start(b_up_in, b_up)]
    copies = []
    for r in range(n):
        at = rows_at(j ^ r, rows)
        copies.append((move.start(hs[r], h_s.at[at, :]), move.start(dg_in.at[at, :], dg.at[at, :])))
    db[...] = jnp.zeros_like(db)
    for copy in loads:
        copy.wait()
    for r in range(n):
        for copy in copies[r]:
            copy.wait()
        at = rows_at(j ^ r, rows)
        u = dot(h_s[at, :], w_up[...]) + b_up[...]
        cdf = 0.5 * (1.0 + lax.erf(u * inv_root_two))
        g_s[at, :] = (u * cdf).astype(bf16)
        slope = cdf + u * jnp.exp(-0.5 * u * u) * inv_root_tau
        du = (dg[at, :] * slope).astype(bf16)
        du_s[at, :] = du
        db[...] += jnp.sum(du.astype(f32), axis=0, keepdims=True)
        dh = dot(du, w_up[...], NT)
        here = slice((r // 2) * rows, (r // 2 + 1) * rows)
        if r % 2 == 0:
            keep_s[here, :] = dh
            move.put(keep_s.at[here, :], keep.at[here, :])
        else:
            send_s[here, :] = dh.astype(bf16)
            move.put(send_s.at[here, :], send.at[here, :])
    move.put(h_s, h_out)
    move.put(g_s, g_out)
    move.put(du_s, du_out)
    move.put(db, db_out)
    move.drain()


def down_kernel(n, place, g_in, w_in, keep, send, g, w, keep_s, send_s, sems):
    move = Mover(sems)
    j = place.j
    rows = g.shape[0] // n
    load = move.start(w_in, w)
    copies = [move.start(g_in.at[rows_at(j ^ r, rows), :], g.at[rows_at(j ^ r, rows), :]) for r in range(n)]
    load.wait()
    for r in range(n):
        copies[r].wait()
        out = dot(g[rows_at(j ^ r, rows), :], w[...])
        here = slice((r // 2) * rows, (r // 2 + 1) * rows)
        if r % 2 == 0:
            keep_s[here, :] = out
            move.put(keep_s.at[here, :], keep.at[here, :])
        else:
            send_s[here, :] = out.astype(bf16)
            move.put(send_s.at[here, :], send.at[here, :])
    move.drain()


def ffn_grads_kernel(groups, place, h_in, du_in, dy_in, g_in, *refs):
    outs = refs[:groups]
    h, du, dy, g, grads, stage, sems = refs[groups:]
    move = Mover(sems)
    loads = [move.start(a, b) for a, b in ((h_in, h), (du_in, du), (dy_in, dy), (g_in, g))]
    feats = h.shape[1] // groups
    mine = du.shape[1]
    chunk = mine // groups
    loads[0].wait()
    loads[1].wait()
    for i in range(groups):
        grads[i, :feats, :] = dot(h[:, i * feats : (i + 1) * feats], du[...], TN)
    loads[2].wait()
    loads[3].wait()
    for c in range(dy.shape[1] // mine):
        part = dot(g[...], dy[:, c * mine : (c + 1) * mine], TN)
        for i in range(groups):
            grads[i, feats + c * chunk : feats + (c + 1) * chunk, :] = part[i * chunk : (i + 1) * chunk, :]
    for i in range(1, groups):
        stage[i - 1] = grads[place.group ^ i].astype(bf16)
        move.put(stage.at[i - 1], outs[i])
    move.put(grads.at[place.group], outs[0])
    move.drain()


def pair_kernel(place, keep, recv, *refs):
    count = (len(refs) - 3) // 2
    outs = refs[:count]
    keep_s, recv_s = refs[count : count + 2]
    stage, sems = refs[count + 2 : 2 * count + 2], refs[2 * count + 2]
    move = Mover(sems)
    rows = outs[0].shape[0]
    order = list(range(1, count)) + [0]
    loads = {}
    for i in order:
        here = slice(i * rows, (i + 1) * rows)
        loads[i] = (
            move.start(keep.at[here, :], keep_s.at[here, :]),
            move.start(recv.at[here, :], recv_s.at[here, :]),
        )
    for i in order:
        here = slice(i * rows, (i + 1) * rows)
        for copy in loads[i]:
            copy.wait()
        stage[i][...] = (keep_s[here, :] + recv_s[here, :].astype(f32)).astype(outs[i].dtype)
        move.put(stage[i], outs[i])
    move.drain()


def fold_kernel(count, place, *refs):
    ins, outs = refs[: 2 * count], refs[2 * count : 3 * count]
    held, stage, sems = refs[3 * count : 5 * count], refs[5 * count : 6 * count], refs[6 * count]
    move = Mover(sems)
    loads = [move.start(a, b) for a, b in zip(ins, held)]
    for i in range(count):
        loads[i].wait()
        loads[count + i].wait()
        stage[i][...] = (held[i][...].astype(f32) + held[count + i][...].astype(f32)).astype(bf16)
        move.put(stage[i], outs[i])
    move.drain()


def out_kernel(count, place, *refs):
    ins = refs[: count + 2]
    kept, sent = refs[count + 2 : count + 4]
    held = refs[count + 4 : 2 * count + 6]
    out_s, sems = refs[2 * count + 6 :]
    move = Mover(sems)
    for copy in [move.start(a, b) for a, b in zip(ins, held)]:
        copy.wait()
    total = held[0][...] + held[count][...]
    for i in range(1, count):
        total = total + held[i][...].astype(f32)
    out_s[...] = (total + held[count + 1][7:8, :]).astype(bf16)
    half = kept.shape[0]
    move.put(out_s.at[half:, :], sent)
    move.put(out_s.at[:half, :], kept)
    move.drain()


def mid_back_kernel(count, place, *refs):
    ins = refs[: count + 3]
    dy1_out, da_out, small_out = refs[count + 3 : count + 6]
    held = refs[count + 6 : 2 * count + 9]
    dy1_s, da_s, small, sems = refs[2 * count + 9 :]
    move = Mover(sems)
    for copy in [move.start(a, b) for a, b in zip(ins, held)]:
        copy.wait()
    dh = held[0][...]
    for i in range(1, count):
        dh = dh + held[i][...].astype(f32)
    y, vec, dy = held[count : count + 3]
    scaled, inv_std = normalize(y[...])
    dyf = dy[...].astype(f32)
    dy1 = dyf + norm_back(dh, scaled, inv_std, vec[5:6, :])
    da = dy1.astype(bf16)
    da_s[...] = da
    move.put(da_s, da_out)
    dy1_s[...] = dy1
    move.put(dy1_s, dy1_out)
    small[0:1, :] = jnp.sum(dh * scaled, axis=0, keepdims=True)
    small[1:2, :] = jnp.sum(dh, axis=0, keepdims=True)
    small[2:3, :] = jnp.sum(da.astype(f32), axis=0, keepdims=True)
    small[3:4, :] = jnp.sum(dyf, axis=0, keepdims=True)
    move.put(small, small_out)
    move.drain()


def attend_back_kernel(n, half, qb, place, *refs):
    das, ins = refs[:n], refs[n : n + 4]
    dqkv_out, keep, send, db_out = refs[n + 4 : n + 8]
    da, qkv, lse, wo, w, dqkv, keep_s, send_s, db, do, bias, acc_k, acc_v, sems = refs[n + 8 :]
    j = place.j
    rows = 2 * half
    move = Mover(sems)
    copies = [move.start(das[r], da.at[rows_at(j ^ r, rows), :]) for r in range(n)]
    loads = [move.start(a, b) for a, b in zip(ins, (wo, qkv, lse, w))]
    total = qkv.shape[0]
    hd = do.shape[1]
    heads = hd // HEAD
    bias[...] = jnp.where(key_mask(place, total, n, half, 128), 0.0, -1.0).astype(f32)
    for copy in loads:
        copy.wait()
    for r in range(n):
        copies[r].wait()
        at = rows_at(j ^ r, rows)
        do[at, :] = dot(da[at, :], wo[...], NT).astype(bf16)
    for head in range(heads):
        cols = slice(head * HEAD, (head + 1) * HEAD)
        kh = qkv[:, hd + head * HEAD : hd + (head + 1) * HEAD]
        vh = qkv[:, 2 * hd + head * HEAD : 2 * hd + (head + 1) * HEAD]
        kt = kh.astype(f32).T.astype(bf16)
        acc_k[...] = jnp.zeros_like(acc_k)
        acc_v[...] = jnp.zeros_like(acc_v)

        def step(i, _, cols=cols, kh=kh, vh=vh, kt=kt, head=head):
            at = rows_at(i, qb)
            qh = qkv[at, cols]
            doh = do[at, cols]
            scores = dot(kh, qh, NT)
            probs = jnp.where(bias[:, 0:1] >= 0.0, jnp.exp(scores - lse[pl.ds(head, 1), at]), 0.0)
            dp = dot(vh, doh, NT)
            centre = jnp.sum(probs * dp, axis=0, keepdims=True)
            ds = (probs * (dp - centre)).astype(bf16)
            acc_v[...] += dot(probs.astype(bf16), doh)
            acc_k[...] += dot(ds, qh)
            dq = dot(kt, ds)
            dqkv[at, cols] = (dq.T.astype(bf16).astype(f32) * 0.125).astype(bf16)
            return 0

        lax.fori_loop(0, total // qb, step, 0)
        dqkv[:, hd + head * HEAD : hd + (head + 1) * HEAD] = acc_k[...].astype(bf16)
        dqkv[:, 2 * hd + head * HEAD : 2 * hd + (head + 1) * HEAD] = acc_v[...].astype(bf16)
    move.put(dqkv, dqkv_out)
    db[...] = jnp.zeros_like(db)
    for r in list(range(1, n, 2)) + list(range(0, n, 2)):
        grads = dqkv[rows_at(j ^ r, rows), :]
        db[...] += jnp.sum(grads.astype(f32), axis=0, keepdims=True)
        dh = dot(grads, w[...], NT)
        here = slice((r // 2) * rows, (r // 2 + 1) * rows)
        if r % 2 == 0:
            keep_s[here, :] = dh
            move.put(keep_s.at[here, :], keep.at[here, :])
        else:
            send_s[here, :] = dh.astype(bf16)
            move.put(send_s.at[here, :], send.at[here, :])
    move.put(db, db_out)
    move.drain()


def attn_grads_kernel(n, groups, first_row, place, *refs):
    das, ins = refs[:n], refs[n : n + 8]
    outs = refs[n + 8 : n + 8 + groups]
    da, hat, h, dqkv, w, o, two, db, up, small, grads, packed_s, sems = refs[n + 8 + groups :]
    move = Mover(sems)
    j = place.j
    loads = [move.start(a, b) for a, b in zip(ins, (dqkv, h, w, hat, o, two, db, up))]
    rows = das[0].shape[0]
    copies = [move.start(das[r], da.at[rows_at(j ^ r, rows), :]) for r in range(n)]
    ndev = packed_s.shape[0]
    hd = dqkv.shape[1] // 3
    rs = h.shape[1] // ndev
    chunk = up.shape[1] // groups
    loads[0].wait()
    loads[1].wait()
    grads[...] = dot(h[...], dqkv[...], TN).astype(bf16)
    for copy in loads[2:]:
        copy.wait()
    small[...] = jnp.zeros_like(small)
    step_rows = 128

    def step(i, _):
        at = rows_at(i, step_rows)
        dh = dot(dqkv[at, :], w[...], NT)
        small[0:1, :] += jnp.sum(dh * hat[at, :].astype(f32), axis=0, keepdims=True)
        small[1:2, :] += jnp.sum(dh, axis=0, keepdims=True)
        return 0

    lax.fori_loop(0, hat.shape[0] // step_rows, step, 0)
    small[4:8, :] = two[...]
    for copy in copies:
        copy.wait()
    out_grad = dot(o[...], da[...], TN).astype(bf16)
    zeros = jnp.zeros((packed_s.shape[1] - rs, packed_s.shape[2]), bf16)
    for d in range(ndev):
        packed_s[d, rs:, :] = zeros
        packed_s[d, :rs, : 3 * hd] = grads[d * rs : (d + 1) * rs, :]
        packed_s[d, :rs, 3 * hd :] = out_grad[d // n * rs : (d // n + 1) * rs, d % n * hd : (d % n + 1) * hd]
        packed_s[d, first_row : first_row + 8, :rs] = small[:, d * rs : (d + 1) * rs].astype(bf16)
    for t in range(groups):
        cols = slice(t * rs, (t + 1) * rs)
        at = j * groups + t
        packed_s[at, first_row + 2 : first_row + 3, :rs] = db[:, :hd][:, cols].astype(bf16)
        packed_s[at, first_row + 3 : first_row + 4, :rs] = db[:, 2 * hd :][:, cols].astype(bf16)
        packed_s[t * n + j, first_row : first_row + 1, hd : hd + chunk] = up[
            :, t * chunk : (t + 1) * chunk
        ].astype(bf16)
    for i in list(range(2, groups)) + [1, 0]:
        move.put(packed_s.at[pl.ds((place.group ^ i) * n, n)], outs[i])
    move.drain()


def last_kernel(count, place, *refs):
    ins = refs[: count + 3]
    kept, sent = refs[count + 3 : count + 5]
    held = refs[count + 5 : 2 * count + 8]
    out_s, sems = refs[2 * count + 8 :]
    move = Mover(sems)
    for copy in [move.start(a, b) for a, b in zip(ins, held)]:
        copy.wait()
    x, dy1, vec = held[count:]
    dh = held[0][...]
    for i in range(1, count):
        dh = dh + held[i][...].astype(f32)
    scaled, inv_std = normalize(x[...].astype(f32))
    out_s[...] = (dy1[...] + norm_back(dh, scaled, inv_std, vec[0:1, :])).astype(bf16)
    half = kept.shape[0]
    move.put(out_s.at[half:, :], sent)
    move.put(out_s.at[:half, :], kept)
    move.drain()


def tail_sum_kernel(n, count, place, *refs):
    attns, ffns = refs[:count], refs[count : 2 * count]
    packed, down_out, out_w = refs[2 * count : 2 * count + 3]
    attn_s, ffn_s = refs[2 * count + 3 : 3 * count + 3], refs[3 * count + 3 : 4 * count + 3]
    packed_s, total, down_s, out_s, sems = refs[4 * count + 3 :]
    move = Mover(sems)
    loads = [move.start(a, b) for a, b in zip(attns + ffns, attn_s + ffn_s)]
    for copy in loads[:count]:
        copy.wait()
    attn = attn_s[0][...].astype(f32)
    for piece in attn_s[1:]:
        attn = attn + piece[...].astype(f32)
    attn = attn.astype(bf16)
    chunk, width = down_s.shape
    hd = width // n
    mine = total.shape[1]
    feats = total.shape[0] - width // mine * chunk
    rs = feats // n
    for m in range(n):
        out_s[:, m * hd : (m + 1) * hd] = attn[m, :rs, 3 * hd :]
    move.put(out_s, out_w)
    packed_s[:, :, : 3 * hd] = attn[:, :, : 3 * hd]
    packed_s[:, :, 3 * hd :] = jnp.zeros((n, packed_s.shape[1], mine), bf16)
    for copy in loads[count:]:
        copy.wait()
    ffn = ffn_s[0][...]
    for piece in ffn_s[1:]:
        ffn = ffn + piece[...].astype(f32)
    total[...] = ffn
    for m in range(n):
        packed_s[m, :rs, 3 * hd :] = total[m * rs : (m + 1) * rs, :].astype(bf16)
    move.put(packed_s, packed)
    for c in range(width // mine):
        down_s[:, c * mine : (c + 1) * mine] = total[feats + c * chunk : feats + (c + 1) * chunk, :]
    move.put(down_s, down_out)
    move.drain()


def unpack_kernel(n, groups, first_row, place, *refs):
    back, out_w = refs[:2]
    halves = refs[2:6]
    output, frames_grad, out_w_grad, up, wq, wk, wv = refs[6:13]
    vectors = refs[13:22]
    back_s, in_s, out_s, up_s, q_s, k_s, v_s = refs[22:29]
    vectors_s, sems = refs[29:38], refs[38]
    move = Mover(sems)
    for i, target in enumerate((output, frames_grad)):
        move.put(halves[2 * i], target.at[place.h])
        move.put(halves[2 * i + 1], target.at[1 - place.h])
    load, more = move.start(back, back_s), move.start(out_w, in_s)
    more.wait()
    out_s[...] = in_s[...].astype(f32)
    move.put(out_s, out_w_grad)
    load.wait()
    rs = wq.shape[0]
    hd = wq.shape[1] // n
    chunk = up.shape[1] // (n * groups)
    sums = jnp.zeros((8, 3 * hd), f32)
    for m in range(n):
        cols = slice(m * hd, (m + 1) * hd)
        for i, target in enumerate((q_s, k_s, v_s)):
            target[:, cols] = back_s[m, :rs, i * hd : (i + 1) * hd].astype(f32)
        for g in range(groups):
            at = (g * n + m) * chunk
            here = 3 * hd + g * chunk
            up_s[:, at : at + chunk] = back_s[m, :rs, here : here + chunk].astype(f32)
        sums = sums + back_s[m, first_row:, : 3 * hd].astype(f32)
    for a, b in ((q_s, wq), (k_s, wk), (v_s, wv), (up_s, up)):
        move.put(a, b)
    for i in range(8):
        vectors_s[i][...] = sums[i : i + 1, :rs]
    vectors_s[8][...] = sums[0:1, hd : hd + chunk]
    for a, b in zip(vectors_s, vectors):
        move.put(a, b)
    move.drain()


def on_device(
    dp_size,
    seq_size,
    frames,
    out_grad,
    order,
    lengths,
    first_gain,
    first_shift,
    query_weight,
    query_bias,
    key_weight,
    value_weight,
    value_bias,
    output_weight,
    output_bias,
    second_gain,
    second_shift,
    up_weight,
    up_bias,
    down_weight,
    down_bias,
):
    slots, half, width = frames.shape
    n = seq_size // slots
    groups = dp_size * slots
    ndev = dp_size * seq_size
    hd = width // n
    heads = hd // HEAD
    rs = query_weight.shape[0]
    hidden = up_weight.shape[1]
    chunk = hidden // ndev
    mine = hidden // n
    parts = width // mine
    feats = n * rs
    rows = 2 * half
    total = n * rows
    qb = min(256, total)
    count = n // 2
    both = ("dp", "seq")
    first_row = -(-rs // 8) * 8
    block_rows = first_row + 8

    grid = (slots, n)

    def xor(value, bit):
        return lax.ppermute(value, "seq", [(i, i ^ bit) for i in range(seq_size)])

    def gather_direct(value):
        got = [xor(value, r) for r in range(n - 2, 0, -2)]
        return [value] + got[::-1]

    def gather_pair(even):
        out = []
        for piece in even:
            out += [piece, xor(piece, 1)]
        return out

    def pair(keep, recv):
        outs = [sds((rows, width), f32)] + [sds((rows, width), bf16)] * (count - 1)
        return call(
        grid,
            pair_kernel,
            [keep, Near(recv)],
            near(outs),
            "pair",
            cost(1),
            scratch=[vmem(keep), vmem(recv)] + [vmem(o) for o in outs],
            sems=3 * count,
        )

    def scatter(pieces):
        return [pieces[0]] + [xor(pieces[i], 2 * i) for i in range(count - 1, 0, -1)][::-1]

    def to_group(value, i):
        pairs = []
        for d in range(ndev):
            dp_of, seq_of = d // seq_size, d % seq_size
            g_of = (dp_of * slots + seq_of // n) ^ i
            pairs.append((d, g_of // slots * seq_size + g_of % slots * n + seq_of % n))
        return lax.ppermute(value, both, pairs)

    def members(value):
        index = [[s * n + i for i in range(n)] for s in range(slots)]
        return lax.all_to_all(value, "seq", 0, 0, tiled=True, axis_index_groups=index)

    def fold(kept, got):
        outs = [sds(a.shape, bf16) for a in kept]
        return call(
            grid,
            functools.partial(fold_kernel, len(kept)),
            near(list(kept) + list(got)),
            near(outs),
            "fold",
            cost(2),
            scratch=[vmem(a) for a in list(kept) + list(got) + outs],
            sems=3 * len(kept),
        )

    def spread(pieces):
        bit = len(pieces)
        while bit < groups:
            pieces = pieces + [to_group(piece, bit) for piece in pieces]
            bit *= 2
        return pieces

    owners = [(d, (d % groups) // slots * seq_size + (d % groups) % slots * n + d // groups) for d in range(ndev)]
    out_w = lax.ppermute(output_weight, both, owners)

    small_in = [first_gain, first_shift, query_bias, value_bias, output_bias, second_gain, second_shift, down_bias]
    small_in = [v.reshape(1, -1) for v in small_in + [up_bias]]
    weights_in = [query_weight, key_weight, value_weight, up_weight]
    half_sds, row_sds = sds((half, width), bf16), sds((rows, width), bf16)
    packed_sds = sds((n, block_rows, 3 * hd + mine), bf16)
    x_own, x_send, dy_own, dy_send, packed = call(
        grid,
        functools.partial(pack_kernel, n, groups, first_row),
        [frames, out_grad] + weights_in + small_in,
        near([half_sds] * 4 + [packed_sds]),
        "pack",
        cost(2),
        scratch=[vmem(w) for w in weights_in] + [vmem(v) for v in small_in] + [vmem(packed_sds)],
        sems=18,
    )
    x_recv = xor(x_send, n)
    got = members(packed)
    x = jnp.concatenate([x_own, after(x_recv, got, out_w)])
    x_even = gather_direct(x)
    attn_sds = sds((n, block_rows, 4 * hd), bf16)
    ffn_sds = sds((feats + parts * chunk, mine), bf16)
    attn_w, ffn_w = call(
        grid,
        functools.partial(join_kernel, n),
        near([got, out_w]) + [down_weight],
        near([attn_sds, ffn_sds]),
        "join",
        cost(2),
        scratch=[vmem(packed_sds), pltpu.VMEM((rs, width), bf16), vmem(attn_sds)]
        + [pltpu.VMEM((feats, mine), bf16)],
        sems=4 + parts,
    )
    attn_ws = spread([attn_w, to_group(attn_w, 1)])
    dy = jnp.concatenate([dy_own, xor(after(dy_send, attn_w), n)])
    xs = gather_pair([x_even[0]] + [after(piece, dy, *attn_ws) for piece in x_even[1:]])

    ffn_w, dy_go, attn_last = lax.optimization_barrier((ffn_w, dy, tuple(attn_ws + xs)))
    ffn_ws = [ffn_w, to_group(ffn_w, 1), to_group(ffn_w, 2)]
    dy_even = gather_direct(dy_go)
    x_sds = sds((total, width), bf16)
    keep_sds, send_sds = sds((total // 2, width), f32), sds((total // 2, width), bf16)
    outs = [
        x_sds,
        x_sds,
        sds((total, 3 * hd), bf16),
        sds((total, hd), bf16),
        sds((heads, total), f32),
        sds((width, 3 * hd), bf16),
        sds((8, width), f32),
        sds((1, mine), f32),
        sds((hd, width), bf16),
        keep_sds,
        send_sds,
    ]
    s_hat, s_h, s_qkv, s_o, s_lse, s_w, s_vec, s_bias, s_wo, s_keep, s_send = [vmem(o) for o in outs]
    s_got = pltpu.VMEM((ndev, block_rows, 4 * hd), bf16)
    hat, h_first, qkv, o_heads, lse, w_qkv, vec, bias_up, wo, keep, send = call(
        grid,
        functools.partial(first_kernel, n, groups, half, qb, first_row),
        near(xs + attn_ws),
        outs[:-1] + near(outs[-1:]),
        "first",
        cost(17),
        scratch=[vmem(x_sds), s_hat, s_h, s_qkv, s_o, s_lse, s_got, s_w, s_vec, s_bias, s_wo, s_keep, s_send]
        + [pltpu.VMEM((total, 128), f32)],
        sems=2 * n + groups + 10,
        limit=32,
        lengths=(order, lengths),
    )
    send = after(send, *ffn_ws[1:], *dy_even[1:])

    y_sds = sds((rows, width), f32)
    y_pieces = pair(keep, xor(send, 1))
    ys = scatter(y_pieces)
    dys = gather_pair([dy_even[0]] + [after(piece, y_pieces[0]) for piece in dy_even[1:]])
    ffn_ws = spread(ffn_ws + [to_group(after(ffn_ws[1], y_pieces[0]), 2)])
    y1, h2 = call(
        grid,
        functools.partial(mid_kernel, count),
        near(ys + [x]) + [vec],
        [y_sds, Near(row_sds)],
        "mid",
        cost(2),
        scratch=[vmem(a) for a in ys + [row_sds, vec, y_sds, row_sds]],
        sems=count + 4,
    )
    h2_even = gather_direct(h2)

    outs = [x_sds, sds((total, mine), f32), sds((width, mine), bf16), sds((mine, width), bf16)]
    dy_all, dg, w_up, w_down = call(
        grid,
        functools.partial(down_back_kernel, n, groups),
        near(dys + ffn_ws),
        outs,
        "down_back",
        cost(5),
        scratch=[vmem(o) for o in outs],
        sems=2 * n + groups * (parts + 1) + 3,
    )
    h2s = gather_pair(h2_even[:1] + [after(piece, dg) for piece in h2_even[1:]])

    act_sds = sds((total, mine), bf16)
    outs = [x_sds, act_sds, act_sds, keep_sds, send_sds, sds((1, mine), f32)]
    h2_all, g, du, keep, send, d_bias_up = call(
        grid,
        functools.partial(ffn_kernel, n),
        near(h2s) + [w_up, bias_up, dg],
        outs[:4] + near(outs[4:5]) + outs[5:],
        "ffn",
        cost(9),
        scratch=[vmem(a) for a in [w_up, bias_up, dg] + outs],
        sems=3 * n + 6,
    )
    dh2 = scatter(pair(keep, xor(send, 1)))

    g_then = after(g, dh2[0])
    out_keep, out_send = call(
        grid,
        functools.partial(down_kernel, n),
        [g_then, w_down],
        [keep_sds, Near(send_sds)],
        "down",
        cost(4),
        scratch=[vmem(a) for a in (g, w_down, keep_sds, send_sds)],
        sems=2 * n + 1,
    )
    ffn_parts = call(
        grid,
        functools.partial(ffn_grads_kernel, groups),
        [h2_all, du, dy_all, g_then],
        [sds(ffn_sds.shape, f32)] + near([ffn_sds] * (groups - 1)),
        "ffn_grads",
        cost(5),
        scratch=[vmem(a) for a in (x_sds, act_sds, x_sds, act_sds)]
        + [pltpu.VMEM((groups,) + ffn_sds.shape, f32), pltpu.VMEM((groups - 1,) + ffn_sds.shape, bf16)],
        sems=4 + groups,
    )

    small_sds = sds((4, width), f32)
    outs = [y_sds, row_sds, small_sds]
    dy1, da, small_two = call(
        grid,
        functools.partial(mid_back_kernel, count),
        near(dh2) + [after(y1, ffn_parts[0], out_keep), vec, Near(dy)],
        outs[:1] + near(outs[1:2]) + outs[2:],
        "mid_back",
        cost(3),
        scratch=[vmem(a) for a in dh2 + [y1, vec, row_sds] + outs],
        sems=count + 6,
    )
    da_even = gather_direct(da)
    ffn_parts = [after(piece, da) for piece in ffn_parts]
    bit = groups // 2
    while bit > 2:
        ffn_parts = fold(ffn_parts[:bit], [to_group(piece, bit) for piece in ffn_parts[bit:]])
        bit //= 2
    ffn_got = [to_group(piece, 2) for piece in ffn_parts[2:4]]
    out_kept = pair(out_keep, xor(after(out_send, da), 1))
    das = gather_pair([da_even[0]] + [after(piece, out_kept[0]) for piece in da_even[1:]])

    out_kept, das = lax.optimization_barrier((tuple(out_kept), tuple(das)))
    out_kept, das = list(out_kept), list(das)
    out_pieces = scatter(out_kept)
    ins = [wo, qkv, lse, w_qkv]
    outs = [sds((total, 3 * hd), bf16), keep_sds, send_sds, sds((1, 3 * hd), f32)]
    d_qkv, keep, send, d_bias_qkv = call(
        grid,
        functools.partial(attend_back_kernel, n, half, qb),
        near(das) + ins,
        outs[:2] + near(outs[2:3]) + outs[3:],
        "attend_back",
        cost(15),
        scratch=[vmem(x_sds)]
        + [vmem(a) for a in (qkv, lse, wo, w_qkv)]
        + [vmem(a) for a in outs]
        + [
            pltpu.VMEM((total, hd), bf16),
            pltpu.VMEM((total, 128), f32),
            pltpu.VMEM((total, HEAD), f32),
            pltpu.VMEM((total, HEAD), f32),
        ],
        sems=2 * n + 6,
        limit=32,
        lengths=(order, lengths),
    )
    recv = xor(after(send, *out_pieces[1:], *ffn_got), 1)

    ins = [d_qkv, h_first, w_qkv, hat, o_heads, small_two, d_bias_qkv, d_bias_up]
    attn_parts = call(
        grid,
        functools.partial(attn_grads_kernel, n, groups, first_row),
        near(das) + ins,
        near([attn_sds] * groups),
        "attn_grads",
        cost(7),
        scratch=[vmem(a) for a in (x_sds, hat, h_first, d_qkv, w_qkv, o_heads, small_two, d_bias_qkv, d_bias_up)]
        + [
            pltpu.VMEM((8, width), f32),
            pltpu.VMEM((width, 3 * hd), bf16),
            pltpu.VMEM((ndev, block_rows, 4 * hd), bf16),
        ],
        sems=n + 8 + groups,
        limit=32,
    )
    dh1_pieces = pair(after(keep, attn_parts[0]), recv)
    dh1 = scatter(dh1_pieces)
    bit = groups // 2
    while bit > 2:
        attn_parts = fold(attn_parts[:bit], [to_group(piece, bit) for piece in attn_parts[bit:]])
        bit //= 2
    attn_got = [to_group(piece, 2) for piece in attn_parts[2:4]]

    (ffn_next,) = fold([after(ffn_parts[1], dh1_pieces[0])], ffn_got[1:])
    ffn_got = [ffn_got[0], to_group(ffn_next, 1)]
    ins = out_pieces + [y1, vec]
    out_own, out_sent = call(
        grid,
        functools.partial(out_kernel, count),
        near([after(ins[0], dh1_pieces[0])] + ins[1:count]) + ins[count:],
        near([half_sds] * 2),
        "out",
        cost(2),
        scratch=[vmem(a) for a in ins + [row_sds]],
        sems=len(ins) + 2,
    )
    out_other = xor(out_sent, n)
    (attn_next,) = fold([after(attn_parts[1], ffn_next, out_own)], attn_got[1:])
    attn_got = [attn_got[0], to_group(attn_next, 1)]

    ins = dh1 + [x, after(dy1, attn_next), vec]
    kept, sent = call(
        grid,
        functools.partial(last_kernel, count),
        near(ins[: count + 1]) + ins[count + 1 :],
        near([half_sds] * 2),
        "last",
        cost(2),
        scratch=[vmem(a) for a in ins + [row_sds]],
        sems=len(ins) + 2,
    )
    other = xor(sent, n)

    down_sds, out_w_sds = sds((chunk, width), f32), sds((rs, width), bf16)
    attn_sums, ffn_sums = [after(attn_parts[0], kept, out_other)] + attn_got, [ffn_parts[0]] + ffn_got
    back, down_weight_grad, out_w = call(
        grid,
        functools.partial(tail_sum_kernel, n, 3),
        near(attn_sums) + ffn_sums[:1] + near(ffn_sums[1:]),
        [Near(packed_sds), down_sds, Near(out_w_sds)],
        "tail_sum",
        cost(2),
        scratch=[vmem(a) for a in attn_sums + ffn_sums]
        + [vmem(packed_sds), pltpu.VMEM(ffn_sds.shape, f32), vmem(down_sds), vmem(out_w_sds)],
        sems=9,
    )
    back = members(back)
    out_w = lax.ppermute(out_w, both, [(b, a) for a, b in owners])
    frames_sds = sds(frames.shape, bf16)
    weight_sds = sds((rs, width), f32)
    outs = [weight_sds, sds((rs, hidden), f32)] + [weight_sds] * 3
    vectors = [sds((1, rs), f32)] * 8 + [sds((1, chunk), f32)]
    output, frames_grad, output_weight_grad, up_weight_grad, d_query, d_key, d_value, *vectors = call(
        grid,
        functools.partial(unpack_kernel, n, groups, first_row),
        near([back, out_w, out_own, out_other, kept, other]),
        [frames_sds] * 2 + outs + vectors,
        "unpack",
        cost(2),
        scratch=[vmem(a) for a in [back, out_w] + outs + vectors],
        sems=20,
    )
    vectors = [v.reshape(-1) for v in vectors]
    return (
        output,
        frames_grad,
        vectors[0],
        vectors[1],
        d_query,
        vectors[2],
        d_key,
        d_value,
        vectors[3],
        output_weight_grad,
        vectors[6],
        vectors[4],
        vectors[5],
        up_weight_grad,
        vectors[8],
        down_weight_grad,
        vectors[7],
    )


def solution(mesh):
    vector = P(("dp", "seq"))
    matrix = P(("dp", "seq"), None)
    rows = P("dp", "seq", None)
    return jax.shard_map(
        functools.partial(on_device, mesh.shape["dp"], mesh.shape["seq"]),
        mesh=mesh,
        in_specs=(
            rows,
            rows,
            P("dp"),
            P(),
            vector,
            vector,
            matrix,
            vector,
            matrix,
            matrix,
            vector,
            matrix,
            vector,
            vector,
            vector,
            matrix,
            vector,
            matrix,
            vector,
        ),
        out_specs=(
            rows,
            rows,
            vector,
            vector,
            matrix,
            vector,
            matrix,
            matrix,
            vector,
            matrix,
            vector,
            vector,
            vector,
            matrix,
            vector,
            matrix,
            vector,
        ),
        check_vma=False,
    )
```

```python
import functools

import jax
import jax.numpy as jnp
from jax import lax
from jax.experimental import pallas as pl
from jax.experimental.pallas import tpu as pltpu
from jax.sharding import PartitionSpec as P

HEAD = 64
f32 = jnp.float32
bf16 = jnp.bfloat16
norm_eps = 1e-05
inv_root_two = 0.7071067811865476
inv_root_tau = 0.3989422804014327
NN = (((1,), (0,)), ((), ()))
NT = (((1,), (1,)), ((), ()))
TN = (((0,), (0,)), ((), ()))
MIB = 1024 * 1024


def dot(a, b, dims=NN):
    return lax.dot_general(a, b, dims, preferred_element_type=f32)


def normalize(rows):
    average = jnp.mean(rows, axis=-1, keepdims=True)
    centered = rows - average
    inv_std = lax.rsqrt(jnp.mean(centered * centered, axis=-1, keepdims=True) + norm_eps)
    return centered * inv_std, inv_std


def norm_back(grad_rows, scaled, inv_std, gain):
    grad_hat = grad_rows * gain
    return inv_std * (
        grad_hat
        - jnp.mean(grad_hat, axis=-1, keepdims=True)
        - scaled * jnp.mean(grad_hat * scaled, axis=-1, keepdims=True)
    )


def sds(shape, dtype):
    return jax.ShapeDtypeStruct(shape, dtype)


def vmem(like):
    return pltpu.VMEM(like.shape, like.dtype)


class Near:
    def __init__(self, array):
        self.array = array
        self.shape, self.dtype = array.shape, array.dtype


def near(arrays):
    return [Near(a) for a in arrays]


class Place:
    def __init__(self, slots, n):
        seq_at = lax.axis_index("seq")
        self.h, self.j = seq_at // n, seq_at % n
        self.dp = lax.axis_index("dp")
        self.group = self.dp * slots + self.h
        self.length = None


def call(grid, kernel, args, outs, name, flops=0, scratch=(), sems=1, limit=None, lengths=()):
    here = pl.BlockSpec(memory_space=pltpu.HBM)
    anywhere = pl.BlockSpec(memory_space=pl.ANY)
    scalars = pl.BlockSpec(memory_space=pltpu.SMEM)
    nbytes = sum(a.shape[0] * a.shape[1] * a.dtype.itemsize for a in list(args) + list(outs))

    def body(*refs):
        place = Place(*grid[:2])
        if lengths:
            order_ref, lengths_ref = refs[:2]
            place.length = lengths_ref[order_ref[place.h]]
        kernel(place, *refs[len(lengths) :])

    return pl.pallas_call(
        body,
        out_shape=tuple(o.array if isinstance(o, Near) else pltpu.HBM(o.shape, o.dtype) for o in outs),
        in_specs=[scalars] * len(lengths) + [anywhere if isinstance(a, Near) else here for a in args],
        out_specs=tuple(anywhere if isinstance(o, Near) else here for o in outs),
        scratch_shapes=list(scratch) + [pltpu.SemaphoreType.DMA((sems,))],
        compiler_params=pltpu.CompilerParams(vmem_limit_bytes=(limit or 8 * grid[2]) * MIB),
        cost_estimate=pl.CostEstimate(flops=int(flops), bytes_accessed=int(nbytes), transcendentals=0),
        name=name,
    )(
        *lengths,
        *[a.array if isinstance(a, Near) else pltpu.with_memory_space_constraint(a, pltpu.HBM) for a in args],
    )


class Mover:
    def __init__(self, sems):
        self.sems, self.used, self.open = sems, 0, []

    def start(self, source, target):
        copy = pltpu.make_async_copy(source, target, self.sems.at[self.used])
        self.used += 1
        copy.start()
        return copy

    def put(self, source, target):
        self.open.append(self.start(source, target))

    def drain(self):
        for copy in self.open:
            copy.wait()
        self.open = []


def cost(microseconds):
    return microseconds * 1150 * 10**6


def after(value, *others):
    return lax.optimization_barrier((value,) + others)[0]


def rows_at(index, rows):
    return pl.ds(pl.multiple_of(index * rows, rows), rows)


def send_rows(move, place, n, rows, source, send_s, keep, send):
    for r in range(1, n, 2):
        here = slice((r // 2) * rows, (r // 2 + 1) * rows)
        send_s[here, :] = source[rows_at(place.j ^ r, rows), :].astype(bf16)
        move.put(send_s.at[here, :], send.at[here, :])
    for r in range(0, n, 2):
        here = slice((r // 2) * rows, (r // 2 + 1) * rows)
        move.put(source.at[rows_at(place.j ^ r, rows), :], keep.at[here, :])


def rows_kernel(place, frames, out_grad, x_own, x_send, dy_own, dy_send, sems):
    move = Mover(sems)
    for rows, own, sent in ((frames, x_own, x_send), (out_grad, dy_own, dy_send)):
        move.put(rows.at[1 - place.h], sent)
        move.put(rows.at[place.h], own)
    move.drain()


def pack_kernel(n, slots, groups, first_row, place, *refs):
    wq, wk, wv = refs[:3]
    small = refs[3:12]
    packed, q_s, k_s, v_s, *rest = refs[12:]
    small_s, (packed_s, sems) = rest[:9], rest[9:]
    move = Mover(sems)
    loads = [move.start(a, b) for a, b in ((wq, q_s), (wk, k_s), (wv, v_s))]
    loads += [move.start(a, b) for a, b in zip(small, small_s)]
    for copy in loads:
        copy.wait()
    rs = wq.shape[0]
    hd = wq.shape[1] // n
    chunk = small[8].shape[1]
    zeros = jnp.zeros((packed_s.shape[1] - rs, packed_s.shape[2]), bf16)
    for m in range(n):
        cols = slice(m * hd, (m + 1) * hd)
        packed_s[m, rs:, :] = zeros
        packed_s[m, :rs, :hd] = q_s[:, cols]
        packed_s[m, :rs, hd : 2 * hd] = k_s[:, cols]
        packed_s[m, :rs, 2 * hd : 3 * hd] = v_s[:, cols]
        for i in range(8):
            packed_s[m, first_row + i : first_row + i + 1, :rs] = small_s[i][...]
        packed_s[m, first_row : first_row + 1, hd : hd + chunk] = small_s[8][...]
    for i in range(slots):
        move.put(packed_s, packed.at[i * n : (i + 1) * n])
    move.drain()


def pack_up_kernel(n, groups, place, up, packed, up_s, packed_s, sems):
    move = Mover(sems)
    move.start(up, up_s).wait()
    chunk = up.shape[1] // (n * groups)
    for m in range(n):
        for g in range(groups):
            at = (g * n + m) * chunk
            packed_s[m, :, g * chunk : (g + 1) * chunk] = up_s[:, at : at + chunk]
    move.put(packed_s, packed)
    move.drain()


def join_kernel(n, place, up, down, ffn, sems):
    move = Mover(sems)
    width, mine = down.shape[1], ffn.shape[1]
    chunk = down.shape[0]
    feats = ffn.shape[0] - width // mine * chunk
    move.put(up, ffn.at[:feats, :])
    for c in range(width // mine):
        move.put(down.at[:, c * mine : (c + 1) * mine], ffn.at[feats + c * chunk : feats + (c + 1) * chunk, :])
    move.drain()


def key_mask(place, rows, n, half, width):
    row = lax.broadcasted_iota(jnp.int32, (rows, width), 0)
    member = row // (2 * half)
    inside = row % (2 * half)
    own = (inside < half).astype(jnp.int32)
    h = place.h
    block_half = own * h + (1 - own) * (1 - h)
    frame = (block_half * n + member) * half + inside % half
    return frame < place.length


def first_kernel(n, dp_size, groups, half, qb, first_row, place, *refs):
    xs, gots, wos = refs[:n], refs[n : n + dp_size], refs[n + dp_size : n + 2 * dp_size]
    at = n + 2 * dp_size
    outs = refs[at : at + 11]
    hat_out, h_out, qkv_out, o_out, lse_out, w_out, vec_out, bias_up_out, wo_out, keep, send = outs
    x_s, hat_s, h_s, qkv_s, o_s, lse_s, got_s, w_s, vec_s, bias_up_s, wo3, wo_s, y_s, send_s, bias, sems = refs[at + 11 :]
    move = Mover(sems)
    j = place.j
    rows = 2 * half
    total = n * rows
    ndev = got_s.shape[0]
    hd = got_s.shape[2] // 3
    seq_size = ndev // dp_size
    rs = x_s.shape[1] // ndev
    chunk = bias_up_s.shape[1] // groups
    load = [move.start(gots[i], got_s.at[pl.ds((place.dp ^ i) * seq_size, seq_size)]) for i in range(dp_size)]
    copies = [move.start(xs[r], x_s.at[rows_at(j ^ r, rows), :]) for r in range(n)]
    slots = groups // dp_size
    outw = [
        move.start(wos[k].at[i], wo3.at[(place.dp ^ k) * slots + (place.h ^ i)])
        for k in range(dp_size)
        for i in range(slots)
    ]
    bias[...] = jnp.where(key_mask(place, total, n, half, 128), 0.0, -1.0).astype(f32)
    for copy in load:
        copy.wait()
    for d in range(ndev):
        w_s[d * rs : (d + 1) * rs, :] = got_s[d, :rs, :]
        vec_s[:, d * rs : (d + 1) * rs] = got_s[d, first_row : first_row + 8, :rs].astype(f32)
    bq, bv = [], []
    for t in range(groups):
        bias_up_s[:, t * chunk : (t + 1) * chunk] = got_s[
            t * n + j, first_row : first_row + 1, hd : hd + chunk
        ].astype(f32)
        bq.append(got_s[j * groups + t, first_row + 2 : first_row + 3, :rs].astype(f32))
        bv.append(got_s[j * groups + t, first_row + 3 : first_row + 4, :rs].astype(f32))
    bq = jnp.concatenate(bq, axis=1)
    bv = jnp.concatenate(bv, axis=1)
    move.put(w_s, w_out)
    move.put(vec_s, vec_out)
    move.put(bias_up_s, bias_up_out)
    for r in range(n):
        copies[r].wait()
        base = pl.multiple_of((j ^ r) * rows, rows)
        for part in range(2):
            at = pl.ds(base + part * half, half)
            scaled, _ = normalize(x_s[at, :].astype(f32))
            hat_s[at, :] = scaled.astype(bf16)
            h_s[at, :] = (scaled * vec_s[0:1, :] + vec_s[1:2, :]).astype(bf16)
    block = min(512, total)
    for i in range(total // block):
        at = slice(i * block, (i + 1) * block)
        qkv = dot(h_s[at, :], w_s[...])
        qkv_s[at, :hd] = ((qkv[:, :hd] + bq) * 0.125).astype(bf16)
        qkv_s[at, hd : 2 * hd] = qkv[:, hd : 2 * hd].astype(bf16)
        qkv_s[at, 2 * hd :] = (qkv[:, 2 * hd :] + bv).astype(bf16)
    move.put(hat_s, hat_out)
    move.put(h_s, h_out)
    move.put(qkv_s, qkv_out)
    heads = hd // HEAD
    for head in range(heads):
        cols = slice(head * HEAD, (head + 1) * HEAD)
        kh = qkv_s[:, hd + head * HEAD : hd + (head + 1) * HEAD]
        vt = qkv_s[:, 2 * hd + head * HEAD : 2 * hd + (head + 1) * HEAD].astype(f32).T.astype(bf16)

        for i in range(total // qb):
            at = slice(i * qb, (i + 1) * qb)
            scores = dot(kh, qkv_s[at, cols], NT)
            scores = jnp.where(bias[:, 0:1] >= 0.0, scores, -1e30)
            row_max = jnp.max(scores, axis=0, keepdims=True)
            e = jnp.exp(scores - row_max)
            row_sum = jnp.sum(e, axis=0, keepdims=True)
            ot = dot(vt, e.astype(bf16)) / row_sum
            o_s[at, cols] = ot.T.astype(bf16)
            lse_s[head : head + 1, at] = row_max + jnp.log(row_sum)
    move.put(o_s, o_out)
    move.put(lse_s, lse_out)
    for copy in outw:
        copy.wait()
    for t in range(groups):
        wo_s[t * rs : (t + 1) * rs, :] = wo3[t]
    move.put(wo_s, wo_out)
    for i in range(total // block):
        at = slice(i * block, (i + 1) * block)
        y_s[at, :] = dot(o_s[at, :], wo_s[...])
    send_rows(move, place, n, rows, y_s, send_s, keep, send)
    move.drain()


def mid_kernel(count, place, *refs):
    ins, x, vec = refs[:count], refs[count], refs[count + 1]
    y_out, h_out = refs[count + 2 : count + 4]
    held = refs[count + 4 : 2 * count + 4]
    x_s, vec_s, y_s, h_s, sems = refs[2 * count + 4 :]
    move = Mover(sems)
    loads = [move.start(a, b) for a, b in zip(ins, held)]
    loads += [move.start(x, x_s), move.start(vec, vec_s)]
    for copy in loads:
        copy.wait()
    y = held[0][...]
    for i in range(1, count):
        y = y + held[i][...].astype(f32)
    y = x_s[...].astype(f32) + y + vec_s[4:5, :]
    y_s[...] = y
    scaled, _ = normalize(y)
    h_s[...] = (scaled * vec_s[5:6, :] + vec_s[6:7, :]).astype(bf16)
    move.put(h_s, h_out)
    move.put(y_s, y_out)
    move.drain()


def down_back_kernel(n, groups, place, *refs):
    dys, ws = refs[:n], refs[n : n + groups]
    dy_out, dg_out, w_up_out, w_down_out, dy_s, dg_s, w_up, w_down, sems = refs[n + groups :]
    move = Mover(sems)
    j, g = place.j, place.group
    rows = dys[0].shape[0]
    chunk = w_down.shape[0] // groups
    mine = w_up.shape[1]
    feats = w_up.shape[0] // groups
    first, last = [], []
    for i in range(groups):
        for c in range(w_down.shape[1] // mine):
            source = ws[i].at[feats + c * chunk : feats + (c + 1) * chunk, :]
            first.append(move.start(source, w_down.at[rows_at(g ^ i, chunk), c * mine : (c + 1) * mine]))
    copies = [move.start(dys[r], dy_s.at[rows_at(j ^ r, rows), :]) for r in range(n)]
    for i in range(groups):
        last.append(move.start(ws[i].at[:feats, :], w_up.at[rows_at(g ^ i, feats), :]))
    for copy in first:
        copy.wait()
    move.put(w_down, w_down_out)
    for copy in copies:
        copy.wait()
    block = min(512, dy_s.shape[0])
    for i in range(dy_s.shape[0] // block):
        at = slice(i * block, (i + 1) * block)
        dg_s[at, :] = dot(dy_s[at, :], w_down[...], NT)
        move.put(dg_s.at[at, :], dg_out.at[at, :])
    for copy in last:
        copy.wait()
    move.put(w_up, w_up_out)
    move.put(dy_s, dy_out)
    move.drain()


def ffn_kernel(n, place, *refs):
    hs = refs[:n]
    w_up_in, b_up_in, dg_in = refs[n : n + 3]
    h_out, g_out, du_out, keep, send, db_out = refs[n + 3 : n + 9]
    w_up, b_up, dg, h_s, g_s, du_s, dh_s, send_s, db, sems = refs[n + 9 :]
    move = Mover(sems)
    rows = hs[0].shape[0]
    total = n * rows
    copies = [move.start(hs[r], h_s.at[rows_at(place.j ^ r, rows), :]) for r in range(n)]
    copies += [move.start(w_up_in, w_up), move.start(b_up_in, b_up)]
    late = move.start(dg_in, dg)
    for copy in copies:
        copy.wait()
    block = min(512, total)
    sums = jnp.zeros(db.shape, f32)
    for i in range(total // block):
        at = slice(i * block, (i + 1) * block)
        u = dot(h_s[at, :], w_up[...]) + b_up[...]
        cdf = 0.5 * (1.0 + lax.erf(u * inv_root_two))
        g_s[at, :] = (u * cdf).astype(bf16)
        slope = cdf + u * jnp.exp(-0.5 * u * u) * inv_root_tau
        if i == 0:
            late.wait()
        du = (dg[at, :] * slope).astype(bf16)
        du_s[at, :] = du
        sums = sums + jnp.sum(du.astype(f32), axis=0, keepdims=True)
        dh_s[at, :] = dot(du, w_up[...], NT)
    db[...] = sums
    send_rows(move, place, n, rows, dh_s, send_s, keep, send)
    move.put(h_s, h_out)
    move.put(g_s, g_out)
    move.put(du_s, du_out)
    move.put(db, db_out)
    move.drain()


def down_kernel(n, place, g_in, w_in, keep, send, g, w, out_s, send_s, sems):
    move = Mover(sems)
    for copy in [move.start(w_in, w), move.start(g_in, g)]:
        copy.wait()
    total = g.shape[0]
    block = min(512, total)
    for i in range(total // block):
        at = slice(i * block, (i + 1) * block)
        out_s[at, :] = dot(g[at, :], w[...])
    send_rows(move, place, n, total // n, out_s, send_s, keep, send)
    move.drain()


def ffn_grads_kernel(groups, place, h_in, du_in, dy_in, g_in, *refs):
    outs = refs[:groups]
    h, du, dy, g, grads, stage, sems = refs[groups:]
    move = Mover(sems)
    loads = [move.start(a, b) for a, b in ((h_in, h), (du_in, du), (dy_in, dy), (g_in, g))]
    feats = h.shape[1] // groups
    mine = du.shape[1]
    chunk = mine // groups
    loads[0].wait()
    loads[1].wait()
    for i in range(groups):
        grads[i, :feats, :] = dot(h[:, i * feats : (i + 1) * feats], du[...], TN)
    loads[2].wait()
    loads[3].wait()
    for c in range(dy.shape[1] // mine):
        part = dot(g[...], dy[:, c * mine : (c + 1) * mine], TN)
        for i in range(groups):
            grads[i, feats + c * chunk : feats + (c + 1) * chunk, :] = part[i * chunk : (i + 1) * chunk, :]
    for i in range(1, groups):
        stage[i - 1] = grads[place.group ^ i].astype(bf16)
        move.put(stage.at[i - 1], outs[i])
    move.put(grads.at[place.group], outs[0])
    move.drain()


def pair_kernel(place, keep, recv, *refs):
    count = (len(refs) - 3) // 2
    outs = refs[:count]
    keep_s, recv_s = refs[count : count + 2]
    stage, sems = refs[count + 2 : 2 * count + 2], refs[2 * count + 2]
    move = Mover(sems)
    rows = outs[0].shape[0]
    order = list(range(1, count)) + [0]
    loads = {}
    for i in order:
        here = slice(i * rows, (i + 1) * rows)
        loads[i] = (
            move.start(keep.at[here, :], keep_s.at[here, :]),
            move.start(recv.at[here, :], recv_s.at[here, :]),
        )
    for i in order:
        here = slice(i * rows, (i + 1) * rows)
        for copy in loads[i]:
            copy.wait()
        stage[i][...] = (keep_s[here, :] + recv_s[here, :].astype(f32)).astype(outs[i].dtype)
        move.put(stage[i], outs[i])
    move.drain()


def fold_kernel(count, place, *refs):
    ins, outs = refs[: 2 * count], refs[2 * count : 3 * count]
    held, stage, sems = refs[3 * count : 5 * count], refs[5 * count : 6 * count], refs[6 * count]
    move = Mover(sems)
    loads = [move.start(a, b) for a, b in zip(ins, held)]
    for i in range(count):
        loads[i].wait()
        loads[count + i].wait()
        stage[i][...] = (held[i][...].astype(f32) + held[count + i][...].astype(f32)).astype(bf16)
        move.put(stage[i], outs[i])
    move.drain()


def out_kernel(count, place, *refs):
    ins = refs[: count + 2]
    kept, sent = refs[count + 2 : count + 4]
    held = refs[count + 4 : 2 * count + 6]
    out_s, sems = refs[2 * count + 6 :]
    move = Mover(sems)
    for copy in [move.start(a, b) for a, b in zip(ins, held)]:
        copy.wait()
    total = held[0][...] + held[count][...]
    for i in range(1, count):
        total = total + held[i][...].astype(f32)
    out_s[...] = (total + held[count + 1][7:8, :]).astype(bf16)
    half = kept.shape[0]
    move.put(out_s.at[half:, :], sent)
    move.put(out_s.at[:half, :], kept)
    move.drain()


def mid_back_kernel(count, place, *refs):
    ins = refs[: count + 3]
    dy1_out, da_out, small_out = refs[count + 3 : count + 6]
    held = refs[count + 6 : 2 * count + 9]
    dy1_s, da_s, small, sems = refs[2 * count + 9 :]
    move = Mover(sems)
    for copy in [move.start(a, b) for a, b in zip(ins, held)]:
        copy.wait()
    dh = held[0][...]
    for i in range(1, count):
        dh = dh + held[i][...].astype(f32)
    y, vec, dy = held[count : count + 3]
    scaled, inv_std = normalize(y[...])
    dyf = dy[...].astype(f32)
    dy1 = dyf + norm_back(dh, scaled, inv_std, vec[5:6, :])
    da = dy1.astype(bf16)
    da_s[...] = da
    move.put(da_s, da_out)
    dy1_s[...] = dy1
    move.put(dy1_s, dy1_out)
    small[0:1, :] = jnp.sum(dh * scaled, axis=0, keepdims=True)
    small[1:2, :] = jnp.sum(dh, axis=0, keepdims=True)
    small[2:3, :] = jnp.sum(da.astype(f32), axis=0, keepdims=True)
    small[3:4, :] = jnp.sum(dyf, axis=0, keepdims=True)
    move.put(small, small_out)
    move.drain()


def attend_back_kernel(n, half, qb, place, *refs):
    das, ins = refs[:n], refs[n : n + 4]
    dqkv_out, keep, send, db_out, da_out = refs[n + 4 : n + 9]
    da, qkv, lse, wo, w, dqkv, dh_s, send_s, db, do, bias, sems = refs[n + 9 :]
    rows = 2 * half
    move = Mover(sems)
    copies = [move.start(das[r], da.at[rows_at(place.j ^ r, rows), :]) for r in range(n)]
    loads = [move.start(a, b) for a, b in zip(ins, (wo, qkv, lse, w))]
    total = qkv.shape[0]
    hd = do.shape[1]
    heads = hd // HEAD
    bias[...] = jnp.where(key_mask(place, total, n, half, 128), 0.0, -1.0).astype(f32)
    loads[0].wait()
    for copy in copies:
        copy.wait()
    move.put(da, da_out)
    block = min(512, total)
    for i in range(total // block):
        at = slice(i * block, (i + 1) * block)
        do[at, :] = dot(da[at, :], wo[...], NT).astype(bf16)
    for copy in loads[1:]:
        copy.wait()
    for head in range(heads):
        cols = slice(head * HEAD, (head + 1) * HEAD)
        kh = qkv[:, hd + head * HEAD : hd + (head + 1) * HEAD]
        vh = qkv[:, 2 * hd + head * HEAD : 2 * hd + (head + 1) * HEAD]
        kt = kh.astype(f32).T.astype(bf16)
        grad_k = grad_v = None
        for i in range(total // qb):
            at = slice(i * qb, (i + 1) * qb)
            qh = qkv[at, cols]
            doh = do[at, cols]
            scores = dot(kh, qh, NT)
            probs = jnp.where(bias[:, 0:1] >= 0.0, jnp.exp(scores - lse[head : head + 1, at]), 0.0)
            dp = dot(vh, doh, NT)
            centre = jnp.sum(probs * dp, axis=0, keepdims=True)
            ds = (probs * (dp - centre)).astype(bf16)
            more_v = dot(probs.astype(bf16), doh)
            more_k = dot(ds, qh)
            grad_v = more_v if grad_v is None else grad_v + more_v
            grad_k = more_k if grad_k is None else grad_k + more_k
            dq = dot(kt, ds)
            dqkv[at, cols] = (dq.T.astype(bf16).astype(f32) * 0.125).astype(bf16)
        dqkv[:, hd + head * HEAD : hd + (head + 1) * HEAD] = grad_k.astype(bf16)
        dqkv[:, 2 * hd + head * HEAD : 2 * hd + (head + 1) * HEAD] = grad_v.astype(bf16)
    move.put(dqkv, dqkv_out)
    sums = jnp.zeros(db.shape, f32)
    for i in range(total // block):
        at = slice(i * block, (i + 1) * block)
        grads = dqkv[at, :]
        sums = sums + jnp.sum(grads.astype(f32), axis=0, keepdims=True)
        dh_s[at, :] = dot(grads, w[...], NT)
    db[...] = sums
    send_rows(move, place, n, rows, dh_s, send_s, keep, send)
    move.put(db, db_out)
    move.drain()


def attn_grads_kernel(n, dp_size, groups, first_row, place, *refs):
    ins, outs = refs[:7], refs[7 : 7 + dp_size]
    dqkv, h, w, hat, two, db, up, small, grads, packed_s, sems = refs[7 + dp_size :]
    move = Mover(sems)
    j = place.j
    loads = [move.start(a, b) for a, b in zip(ins, (dqkv, h, w, hat, two, db, up))]
    ndev = packed_s.shape[0]
    hd = dqkv.shape[1] // 3
    rs = h.shape[1] // ndev
    chunk = up.shape[1] // groups
    loads[0].wait()
    loads[1].wait()
    grads[...] = dot(h[...], dqkv[...], TN).astype(bf16)
    for copy in loads[2:]:
        copy.wait()
    small[...] = jnp.zeros_like(small)
    step_rows = min(512, hat.shape[0])

    def step(i, _):
        at = rows_at(i, step_rows)
        dh = dot(dqkv[at, :], w[...], NT)
        small[0:1, :] += jnp.sum(dh * hat[at, :].astype(f32), axis=0, keepdims=True)
        small[1:2, :] += jnp.sum(dh, axis=0, keepdims=True)
        return 0

    lax.fori_loop(0, hat.shape[0] // step_rows, step, 0)
    small[4:8, :] = two[...]
    zeros = jnp.zeros((packed_s.shape[1] - rs, packed_s.shape[2]), bf16)
    for d in range(ndev):
        packed_s[d, rs:, :] = zeros
        packed_s[d, :rs, :] = grads[d * rs : (d + 1) * rs, :]
        packed_s[d, first_row : first_row + 8, :rs] = small[:, d * rs : (d + 1) * rs].astype(bf16)
    for t in range(groups):
        cols = slice(t * rs, (t + 1) * rs)
        at = j * groups + t
        packed_s[at, first_row + 2 : first_row + 3, :rs] = db[:, :hd][:, cols].astype(bf16)
        packed_s[at, first_row + 3 : first_row + 4, :rs] = db[:, 2 * hd :][:, cols].astype(bf16)
        packed_s[t * n + j, first_row : first_row + 1, hd : hd + chunk] = up[
            :, t * chunk : (t + 1) * chunk
        ].astype(bf16)
    seq_size = ndev // dp_size
    for i in list(range(1, dp_size)) + [0]:
        move.put(packed_s.at[pl.ds((place.dp ^ i) * seq_size, seq_size)], outs[i])
    move.drain()


def out_grads_kernel(dp_size, groups, place, da_in, o_in, *refs):
    outs = refs[:dp_size]
    da, o, grads, stage, sems = refs[dp_size:]
    move = Mover(sems)
    for copy in [move.start(o_in, o), move.start(da_in, da)]:
        copy.wait()
    all_rows = dot(o[...], da[...], TN)
    rs = grads.shape[1]
    for t in range(groups):
        grads[t] = all_rows[t * rs : (t + 1) * rs, :]
    slots = groups // dp_size
    for k in range(dp_size):
        for i in range(slots):
            stage[k, i] = grads[(place.dp ^ k) * slots + (place.h ^ i)].astype(bf16)
        move.put(stage.at[k], outs[k])
    move.drain()


def last_kernel(count, place, *refs):
    ins, rider = refs[: count + 3], refs[count + 3]
    kept, sent = refs[count + 4 : count + 6]
    held = refs[count + 6 : 2 * count + 9]
    out_s, sems = refs[2 * count + 9 :]
    move = Mover(sems)
    half = kept.shape[0]
    move.put(rider.at[1], sent.at[half:, :])
    for copy in [move.start(a, b) for a, b in zip(ins, held)]:
        copy.wait()
    x, dy1, vec = held[count:]
    dh = held[0][...]
    for i in range(1, count):
        dh = dh + held[i][...].astype(f32)
    scaled, inv_std = normalize(x[...].astype(f32))
    out_s[...] = (dy1[...] + norm_back(dh, scaled, inv_std, vec[0:1, :])).astype(bf16)
    move.put(out_s.at[half:, :], sent.at[:half, :])
    move.put(out_s.at[:half, :], kept)
    move.drain()


def ffn_sum_kernel(count, place, *refs):
    ins, (up_out, down_out) = refs[:count], refs[count : count + 2]
    held, (total, up_s, down_s, sems) = refs[count + 2 : 2 * count + 2], refs[2 * count + 2 :]
    move = Mover(sems)
    for copy in [move.start(a, b) for a, b in zip(ins, held)]:
        copy.wait()
    ffn = held[0][...].astype(f32)
    for piece in held[1:]:
        ffn = ffn + piece[...].astype(f32)
    total[...] = ffn
    n, rs, mine = up_s.shape
    chunk, width = down_s.shape
    for m in range(n):
        up_s[m] = total[m * rs : (m + 1) * rs, :].astype(bf16)
    move.put(up_s, up_out)
    feats = n * rs
    for c in range(width // mine):
        down_s[:, c * mine : (c + 1) * mine] = total[feats + c * chunk : feats + (c + 1) * chunk, :]
    move.put(down_s, down_out)
    move.drain()


def unpack_kernel(n, groups, first_row, place, *refs):
    back, up_back, out_w = refs[:3]
    halves = refs[3:7]
    output, frames_grad, out_w_grad, up, wq, wk, wv = refs[7:14]
    vectors = refs[14:23]
    back_s, up_back_s, in_s, out_s, up_s, q_s, k_s, v_s = refs[23:31]
    vectors_s, sems = refs[31:40], refs[40]
    move = Mover(sems)
    load, more, third = move.start(back, back_s), move.start(up_back, up_back_s), move.start(out_w, in_s)
    half = output.shape[1]
    for i, target in enumerate((output, frames_grad)):
        move.put(halves[2 * i], target.at[place.h])
        move.put(halves[2 * i + 1].at[:half, :], target.at[1 - place.h])
    third.wait()
    out_s[...] = in_s[...].astype(f32)
    move.put(out_s, out_w_grad)
    rs = wq.shape[0]
    hd = wq.shape[1] // n
    chunk = up.shape[1] // (n * groups)
    more.wait()
    for m in range(n):
        for g in range(groups):
            at = (g * n + m) * chunk
            up_s[:, at : at + chunk] = up_back_s[m, :, g * chunk : (g + 1) * chunk].astype(f32)
    move.put(up_s, up)
    load.wait()
    sums = jnp.zeros((8, 3 * hd), f32)
    for m in range(n):
        cols = slice(m * hd, (m + 1) * hd)
        total = back_s[m].astype(f32)
        for i in range(m + n, back_s.shape[0], n):
            total = total + back_s[i].astype(f32)
        for i, target in enumerate((q_s, k_s, v_s)):
            target[:, cols] = total[:rs, i * hd : (i + 1) * hd]
        sums = sums + total[first_row:, :]
    for a, b in ((q_s, wq), (k_s, wk), (v_s, wv)):
        move.put(a, b)
    for i in range(8):
        vectors_s[i][...] = sums[i : i + 1, :rs]
    vectors_s[8][...] = sums[0:1, hd : hd + chunk]
    for a, b in zip(vectors_s, vectors):
        move.put(a, b)
    move.drain()


def on_device(
    dp_size,
    seq_size,
    frames,
    out_grad,
    order,
    lengths,
    first_gain,
    first_shift,
    query_weight,
    query_bias,
    key_weight,
    value_weight,
    value_bias,
    output_weight,
    output_bias,
    second_gain,
    second_shift,
    up_weight,
    up_bias,
    down_weight,
    down_bias,
):
    slots, half, width = frames.shape
    n = seq_size // slots
    groups = dp_size * slots
    ndev = dp_size * seq_size
    hd = width // n
    heads = hd // HEAD
    rs = query_weight.shape[0]
    hidden = up_weight.shape[1]
    chunk = hidden // ndev
    mine = hidden // n
    parts = width // mine
    feats = n * rs
    rows = 2 * half
    total = n * rows
    qb = max(128, min(total, (1 << 20) // total))
    count = n // 2
    both = ("dp", "seq")
    first_row = -(-rs // 8) * 8
    block_rows = first_row + 8

    scale = -(-total // 1024)
    grid = (slots, n, scale)

    def xor(value, bit):
        return lax.ppermute(value, "seq", [(i, i ^ bit) for i in range(seq_size)])

    def gather_direct(value):
        got = [xor(value, r) for r in range(n - 2, 0, -2)]
        return [value] + got[::-1]

    def gather_pair(even):
        out = []
        for piece in even:
            out += [piece, xor(piece, 1)]
        return out

    def pair(keep, recv):
        outs = [sds((rows, width), f32)] + [sds((rows, width), bf16)] * (count - 1)
        return call(
        grid,
            pair_kernel,
            [keep, Near(recv)],
            near(outs),
            "pair",
            cost(1),
            scratch=[vmem(keep), vmem(recv)] + [vmem(o) for o in outs],
            sems=3 * count,
        )

    def scatter(pieces):
        return [pieces[0]] + [xor(pieces[i], 2 * i) for i in range(count - 1, 0, -1)][::-1]

    def to_group(value, i):
        pairs = []
        for d in range(ndev):
            dp_of, seq_of = d // seq_size, d % seq_size
            g_of = (dp_of * slots + seq_of // n) ^ i
            pairs.append((d, g_of // slots * seq_size + g_of % slots * n + seq_of % n))
        return lax.ppermute(value, both, pairs)

    def members(value):
        index = [[s * n + i for i in range(n)] for s in range(slots)]
        return lax.all_to_all(value, "seq", 0, 0, tiled=True, axis_index_groups=index)

    def fold(kept, got):
        outs = [sds(a.shape, bf16) for a in kept]
        return call(
            grid,
            functools.partial(fold_kernel, len(kept)),
            near(list(kept) + list(got)),
            near(outs),
            "fold",
            cost(2),
            scratch=[vmem(a) for a in list(kept) + list(got) + outs],
            sems=3 * len(kept),
        )

    def spread(pieces):
        bit = len(pieces)
        while bit < groups:
            pieces = pieces + [to_group(piece, bit) for piece in pieces]
            bit *= 2
        return pieces

    def to_dp(value, i):
        return lax.ppermute(value, "dp", [(d, d ^ i) for d in range(dp_size)])

    owners = [(d, (d % groups) // slots * seq_size + (d % groups) % slots * n + d // groups) for d in range(ndev)]
    out_w = lax.ppermute(output_weight, both, owners)

    small_in = [first_gain, first_shift, query_bias, value_bias, output_bias, second_gain, second_shift, down_bias]
    small_in = [v.reshape(1, -1) for v in small_in + [up_bias]]
    weights_in = [query_weight, key_weight, value_weight]
    half_sds, row_sds = sds((half, width), bf16), sds((rows, width), bf16)
    packed_sds, up_sds = sds((seq_size, block_rows, 3 * hd), bf16), sds((n, rs, mine), bf16)
    x_own, x_send, dy_own, dy_send = call(
        grid, rows_kernel, [frames, out_grad], near([half_sds] * 4), "rows", cost(1), sems=4
    )
    x_recv = xor(x_send, n)
    (packed,) = call(
        grid,
        functools.partial(pack_kernel, n, slots, groups, first_row),
        [after(weights_in[0], x_send)] + weights_in[1:] + small_in,
        near([packed_sds]),
        "pack",
        cost(2),
        scratch=[vmem(w) for w in weights_in] + [vmem(v) for v in small_in] + [pltpu.VMEM((n, block_rows, 3 * hd), bf16)],
        sems=12 + slots,
    )
    (up_packed,) = call(
        grid,
        functools.partial(pack_up_kernel, n, groups),
        [up_weight],
        near([up_sds]),
        "pack_up",
        cost(1),
        scratch=[vmem(up_weight), vmem(up_sds)],
        sems=2,
    )
    up_mine = members(up_packed)
    attn_w = lax.all_to_all(after(packed, up_mine), "seq", 0, 0, tiled=True)
    x = jnp.concatenate([x_own, x_recv])
    x_even = gather_direct(x)
    wos = [jnp.stack([out_w, xor(out_w, n)])]
    dy_recv = xor(after(dy_send, attn_w), n)
    attn_ws = [attn_w]
    while len(attn_ws) < dp_size:
        wos += [to_dp(piece, len(wos)) for piece in wos]
        attn_ws += [to_dp(piece, len(attn_ws)) for piece in attn_ws]
    ffn_sds = sds((feats + parts * chunk, mine), bf16)
    (ffn_w,) = call(
        grid,
        functools.partial(join_kernel, n),
        near([up_mine.reshape(feats, mine), down_weight]),
        near([ffn_sds]),
        "join",
        cost(1),
        sems=1 + parts,
    )
    ffn_half = to_group(after(ffn_w, attn_w), 1)
    xs = gather_pair([after(piece, attn_ws[-1], wos[-1]) for piece in x_even])
    dy = jnp.concatenate([dy_own, dy_recv])

    ffn_go, dy_go, xs, attn_ws, wos = lax.optimization_barrier((ffn_w, dy, tuple(xs), tuple(attn_ws), tuple(wos)))
    xs, attn_ws, wos = list(xs), list(attn_ws), list(wos)
    ffn_ws = [ffn_w, ffn_half, to_group(ffn_go, 2)]
    dy_even = gather_direct(dy_go)
    x_sds = sds((total, width), bf16)
    keep_sds, send_sds = sds((total // 2, width), f32), sds((total // 2, width), bf16)
    outs = [
        x_sds,
        x_sds,
        sds((total, 3 * hd), bf16),
        sds((total, hd), bf16),
        sds((heads, total), f32),
        sds((width, 3 * hd), bf16),
        sds((8, width), f32),
        sds((1, mine), f32),
        sds((hd, width), bf16),
        keep_sds,
        send_sds,
    ]
    s_hat, s_h, s_qkv, s_o, s_lse, s_w, s_vec, s_bias, s_wo, _, s_send = [vmem(o) for o in outs]
    s_rows = pltpu.VMEM((total, width), f32)
    s_got = pltpu.VMEM((ndev, block_rows, 3 * hd), bf16)
    s_wo3 = pltpu.VMEM((groups, rs, width), bf16)
    hat, h_first, qkv, o_heads, lse, w_qkv, vec, bias_up, wo, keep, send = call(
        grid,
        functools.partial(first_kernel, n, dp_size, groups, half, qb, first_row),
        near(xs + attn_ws + wos),
        outs[:-1] + near(outs[-1:]),
        "first",
        cost(17),
        scratch=[vmem(x_sds), s_hat, s_h, s_qkv, s_o, s_lse, s_got, s_w, s_vec, s_bias, s_wo3, s_wo, s_rows, s_send]
        + [pltpu.VMEM((total, 128), f32)],
        sems=3 * n + groups + dp_size + 10,
        lengths=(order, lengths),
        limit=48,
    )
    send = after(send, *ffn_ws[1:], *dy_even[1:])

    y_sds = sds((rows, width), f32)
    y_pieces = pair(keep, xor(send, 1))
    ys = scatter(y_pieces)
    dys = gather_pair([dy_even[0]] + [after(piece, y_pieces[0]) for piece in dy_even[1:]])
    ffn_ws = spread(ffn_ws + [to_group(after(ffn_ws[1], y_pieces[0]), 2)])
    y1, h2 = call(
        grid,
        functools.partial(mid_kernel, count),
        near(ys + [x]) + [vec],
        [y_sds, Near(row_sds)],
        "mid",
        cost(2),
        scratch=[vmem(a) for a in ys + [row_sds, vec, y_sds, row_sds]],
        sems=count + 4,
    )
    h2_even = gather_direct(h2)

    outs = [x_sds, sds((total, mine), f32), sds((width, mine), bf16), sds((mine, width), bf16)]
    dy_all, dg, w_up, w_down = call(
        grid,
        functools.partial(down_back_kernel, n, groups),
        near(dys + ffn_ws),
        outs,
        "down_back",
        cost(5),
        scratch=[vmem(o) for o in outs],
        sems=2 * n + groups * (parts + 1) + 3,
        limit=14 * scale,
    )
    h2s = gather_pair(h2_even[:1] + [after(piece, dg) for piece in h2_even[1:]])

    act_sds = sds((total, mine), bf16)
    outs = [x_sds, act_sds, act_sds, keep_sds, send_sds, sds((1, mine), f32)]
    h2_all, g, du, keep, send, d_bias_up = call(
        grid,
        functools.partial(ffn_kernel, n),
        near(h2s) + [w_up, bias_up, dg],
        outs[:4] + near(outs[4:5]) + outs[5:],
        "ffn",
        cost(9),
        scratch=[vmem(a) for a in [w_up, bias_up, dg] + outs[:3]] + [s_rows, vmem(outs[4]), vmem(outs[5])],
        sems=3 * n + 7,
        limit=28 * scale,
    )
    dh2 = scatter(pair(keep, xor(send, 1)))

    g_then = after(g, dh2[0])
    out_keep, out_send = call(
        grid,
        functools.partial(down_kernel, n),
        [g_then, w_down],
        [keep_sds, Near(send_sds)],
        "down",
        cost(4),
        scratch=[vmem(g), vmem(w_down), s_rows, vmem(send_sds)],
        sems=n + 2,
        limit=16 * scale,
    )
    ffn_parts = call(
        grid,
        functools.partial(ffn_grads_kernel, groups),
        [h2_all, du, dy_all, g_then],
        [sds(ffn_sds.shape, f32)] + near([ffn_sds] * (groups - 1)),
        "ffn_grads",
        cost(5),
        scratch=[vmem(a) for a in (x_sds, act_sds, x_sds, act_sds)]
        + [pltpu.VMEM((groups,) + ffn_sds.shape, f32), pltpu.VMEM((groups - 1,) + ffn_sds.shape, bf16)],
        sems=4 + groups,
        limit=20 * scale,
    )

    small_sds = sds((4, width), f32)
    outs = [y_sds, row_sds, small_sds]
    dy1, da, small_two = call(
        grid,
        functools.partial(mid_back_kernel, count),
        near(dh2) + [after(y1, ffn_parts[0], out_keep), vec, Near(dy)],
        outs[:1] + near(outs[1:2]) + outs[2:],
        "mid_back",
        cost(3),
        scratch=[vmem(a) for a in dh2 + [y1, vec, row_sds] + outs],
        sems=count + 6,
    )
    da_even = gather_direct(da)
    bit = groups // 2
    while bit > 2:
        ffn_parts = fold(ffn_parts[:bit], [to_group(piece, bit) for piece in ffn_parts[bit:]])
        bit //= 2
    ffn_got = [to_group(piece, 2) for piece in ffn_parts[2:4]]
    out_kept = pair(out_keep, xor(after(out_send, da), 1))
    (ffn_next,) = fold([after(ffn_parts[1], out_kept[0])], ffn_got[1:])
    das = gather_pair([da_even[0]] + [after(piece, ffn_next) for piece in da_even[1:]])

    out_kept, das, ffn_next = lax.optimization_barrier((tuple(out_kept), tuple(das), ffn_next))
    out_kept, das = list(out_kept), list(das)
    ffn_got = [ffn_got[0], to_group(ffn_next, 1)]
    out_pieces = scatter(out_kept)
    ins = [wo, qkv, lse, w_qkv]
    outs = [sds((total, 3 * hd), bf16), keep_sds, send_sds, sds((1, 3 * hd), f32), x_sds]
    d_qkv, keep, send, d_bias_qkv, da_all = call(
        grid,
        functools.partial(attend_back_kernel, n, half, qb),
        near(das) + ins,
        outs[:2] + near(outs[2:3]) + outs[3:],
        "attend_back",
        cost(15),
        scratch=[vmem(x_sds)]
        + [vmem(a) for a in (qkv, lse, wo, w_qkv, outs[0])]
        + [s_rows, vmem(outs[2]), vmem(outs[3]), pltpu.VMEM((total, hd), bf16), pltpu.VMEM((total, 128), f32)],
        sems=2 * n + 9,
        lengths=(order, lengths),
        limit=48,
    )
    recv = xor(after(send, *out_pieces[1:], *ffn_got), 1)

    ins = [d_qkv, h_first, w_qkv, hat, small_two, d_bias_qkv, d_bias_up]
    attn_parts = call(
        grid,
        functools.partial(attn_grads_kernel, n, dp_size, groups, first_row),
        ins,
        near([packed_sds] * dp_size),
        "attn_grads",
        cost(6),
        scratch=[vmem(a) for a in ins]
        + [
            pltpu.VMEM((8, width), f32),
            pltpu.VMEM((width, 3 * hd), bf16),
            pltpu.VMEM((ndev, block_rows, 3 * hd), bf16),
        ],
        sems=7 + dp_size,
        limit=20 * scale,
    )
    dh1_pieces = pair(after(keep, attn_parts[0]), recv)
    dh1 = scatter(dh1_pieces)
    bit = dp_size // 2
    while bit > 1:
        attn_parts = fold(attn_parts[:bit], [to_dp(piece, bit) for piece in attn_parts[bit:]])
        bit //= 2
    attn_got = to_dp(attn_parts[1], 1)

    ffn_sums = [after(ffn_parts[0], dh1_pieces[0])] + ffn_got
    down_sds = sds((chunk, width), f32)
    up_back, down_weight_grad = call(
        grid,
        functools.partial(ffn_sum_kernel, 3),
        ffn_sums[:1] + near(ffn_sums[1:]),
        [Near(up_sds), down_sds],
        "ffn_sum",
        cost(2),
        scratch=[vmem(a) for a in ffn_sums] + [pltpu.VMEM(ffn_sds.shape, f32), vmem(up_sds), vmem(down_sds)],
        sems=5,
    )
    up_back = members(up_back)
    out_parts = call(
        grid,
        functools.partial(out_grads_kernel, dp_size, groups),
        [da_all, after(o_heads, dh1_pieces[0])],
        near([sds((slots, rs, width), bf16)] * dp_size),
        "out_grads",
        cost(2),
        scratch=[
            vmem(x_sds),
            vmem(o_heads),
            pltpu.VMEM((groups, rs, width), f32),
            pltpu.VMEM((dp_size, slots, rs, width), bf16),
        ],
        sems=2 + dp_size,
        limit=10 * scale,
    )
    bit = dp_size // 2
    while bit > 1:
        out_parts = fold(out_parts[:bit], [to_dp(piece, bit) for piece in out_parts[bit:]])
        bit //= 2

    (attn_sum,) = fold([after(attn_parts[0], up_back)], [attn_got])
    back = lax.all_to_all(attn_sum, "seq", 0, 0, tiled=True)
    (out_w_sum,) = fold([after(out_parts[0], attn_sum)], [to_dp(out_parts[1], 1)])

    ins = out_pieces + [y1, vec]
    out_own, out_sent = call(
        grid,
        functools.partial(out_kernel, count),
        near([after(ins[0], attn_sum)] + ins[1:count]) + ins[count:],
        near([half_sds] * 2),
        "out",
        cost(2),
        scratch=[vmem(a) for a in ins + [row_sds]],
        sems=len(ins) + 2,
    )
    out_other = xor(out_sent, n)

    ins = dh1 + [x, after(dy1, attn_sum), vec]
    kept, sent = call(
        grid,
        functools.partial(last_kernel, count),
        near(ins[: count + 1]) + ins[count + 1 :] + near([out_w_sum]),
        near([half_sds, sds((half + rs, width), bf16)]),
        "last",
        cost(2),
        scratch=[vmem(a) for a in ins + [row_sds]],
        sems=len(ins) + 3,
    )
    other = xor(sent, n)
    out_w = (out_w_sum[0].astype(f32) + other[half:].astype(f32)).astype(bf16)
    out_w = lax.ppermute(out_w, both, [(b, a) for a, b in owners])
    frames_sds = sds(frames.shape, bf16)
    weight_sds = sds((rs, width), f32)
    outs = [weight_sds, sds((rs, hidden), f32)] + [weight_sds] * 3
    vectors = [sds((1, rs), f32)] * 8 + [sds((1, chunk), f32)]
    output, frames_grad, output_weight_grad, up_weight_grad, d_query, d_key, d_value, *vectors = call(
        grid,
        functools.partial(unpack_kernel, n, groups, first_row),
        near([back, up_back, out_w, out_own, out_other, kept, other]),
        [frames_sds] * 2 + outs + vectors,
        "unpack",
        cost(2),
        scratch=[vmem(a) for a in [back, up_back, out_w] + outs + vectors],
        sems=24,
    )
    vectors = [v.reshape(-1) for v in vectors]
    return (
        output,
        frames_grad,
        vectors[0],
        vectors[1],
        d_query,
        vectors[2],
        d_key,
        d_value,
        vectors[3],
        output_weight_grad,
        vectors[6],
        vectors[4],
        vectors[5],
        up_weight_grad,
        vectors[8],
        down_weight_grad,
        vectors[7],
    )


def solution(mesh):
    vector = P(("dp", "seq"))
    matrix = P(("dp", "seq"), None)
    rows = P("dp", "seq", None)
    return jax.shard_map(
        functools.partial(on_device, mesh.shape["dp"], mesh.shape["seq"]),
        mesh=mesh,
        in_specs=(
            rows,
            rows,
            P("dp"),
            P(),
            vector,
            vector,
            matrix,
            vector,
            matrix,
            matrix,
            vector,
            matrix,
            vector,
            vector,
            vector,
            matrix,
            vector,
            matrix,
            vector,
        ),
        out_specs=(
            rows,
            rows,
            vector,
            vector,
            matrix,
            vector,
            matrix,
            matrix,
            vector,
            matrix,
            vector,
            vector,
            vector,
            matrix,
            vector,
            matrix,
            vector,
        ),
        check_vma=False,
    )
```

```python
import functools

import jax
import jax.numpy as jnp
from jax import lax
from jax.experimental import pallas as pl
from jax.experimental.pallas import tpu as pltpu
from jax.sharding import PartitionSpec as P

HEAD = 64
f32 = jnp.float32
bf16 = jnp.bfloat16
norm_eps = 1e-05
inv_root_two = 0.7071067811865476
inv_root_tau = 0.3989422804014327
NN = (((1,), (0,)), ((), ()))
NT = (((1,), (1,)), ((), ()))
TN = (((0,), (0,)), ((), ()))
MIB = 1024 * 1024


def dot(a, b, dims=NN):
    return lax.dot_general(a, b, dims, preferred_element_type=f32)


def normalize(rows):
    average = jnp.mean(rows, axis=-1, keepdims=True)
    centered = rows - average
    inv_std = lax.rsqrt(jnp.mean(centered * centered, axis=-1, keepdims=True) + norm_eps)
    return centered * inv_std, inv_std


def norm_back(grad_rows, scaled, inv_std, gain):
    grad_hat = grad_rows * gain
    return inv_std * (
        grad_hat
        - jnp.mean(grad_hat, axis=-1, keepdims=True)
        - scaled * jnp.mean(grad_hat * scaled, axis=-1, keepdims=True)
    )


def sds(shape, dtype):
    return jax.ShapeDtypeStruct(shape, dtype)


def vmem(like):
    return pltpu.VMEM(like.shape, like.dtype)


class Near:
    def __init__(self, array):
        self.array = array
        self.shape, self.dtype = array.shape, array.dtype


def near(arrays):
    return [Near(a) for a in arrays]


class Place:
    def __init__(self, slots, n):
        seq_at = lax.axis_index("seq")
        self.h, self.j = seq_at // n, seq_at % n
        self.dp = lax.axis_index("dp")
        self.group = self.dp * slots + self.h
        self.length = None


def call(grid, kernel, args, outs, name, flops=0, scratch=(), sems=1, limit=None, lengths=()):
    here = pl.BlockSpec(memory_space=pltpu.HBM)
    anywhere = pl.BlockSpec(memory_space=pl.ANY)
    scalars = pl.BlockSpec(memory_space=pltpu.SMEM)
    nbytes = sum(a.shape[0] * a.shape[1] * a.dtype.itemsize for a in list(args) + list(outs))

    def body(*refs):
        place = Place(*grid[:2])
        if lengths:
            order_ref, lengths_ref = refs[:2]
            place.length = lengths_ref[order_ref[place.h]]
        kernel(place, *refs[len(lengths) :])

    return pl.pallas_call(
        body,
        out_shape=tuple(o.array if isinstance(o, Near) else pltpu.HBM(o.shape, o.dtype) for o in outs),
        in_specs=[scalars] * len(lengths) + [anywhere if isinstance(a, Near) else here for a in args],
        out_specs=tuple(anywhere if isinstance(o, Near) else here for o in outs),
        scratch_shapes=list(scratch) + [pltpu.SemaphoreType.DMA((sems,))],
        compiler_params=pltpu.CompilerParams(vmem_limit_bytes=(limit or 8 * grid[2]) * MIB),
        cost_estimate=pl.CostEstimate(flops=int(flops), bytes_accessed=int(nbytes), transcendentals=0),
        name=name,
    )(
        *lengths,
        *[a.array if isinstance(a, Near) else pltpu.with_memory_space_constraint(a, pltpu.HBM) for a in args],
    )


class Mover:
    def __init__(self, sems):
        self.sems, self.used, self.open = sems, 0, []

    def start(self, source, target):
        copy = pltpu.make_async_copy(source, target, self.sems.at[self.used])
        self.used += 1
        copy.start()
        return copy

    def put(self, source, target):
        self.open.append(self.start(source, target))

    def drain(self):
        for copy in self.open:
            copy.wait()
        self.open = []


def cost(microseconds):
    return microseconds * 1150 * 10**6


def after(value, *others):
    return lax.optimization_barrier((value,) + others)[0]


def rows_at(index, rows):
    return pl.ds(pl.multiple_of(index * rows, rows), rows)


def send_rows(move, place, n, rows, source, send_s, keep, send):
    for r in range(1, n, 2):
        here = slice((r // 2) * rows, (r // 2 + 1) * rows)
        send_s[here, :] = source[rows_at(place.j ^ r, rows), :].astype(bf16)
        move.put(send_s.at[here, :], send.at[here, :])
    for r in range(0, n, 2):
        here = slice((r // 2) * rows, (r // 2 + 1) * rows)
        move.put(source.at[rows_at(place.j ^ r, rows), :], keep.at[here, :])


def rows_kernel(place, frames, out_grad, x_own, x_send, dy_own, dy_send, sems):
    move = Mover(sems)
    for rows, own, sent in ((frames, x_own, x_send), (out_grad, dy_own, dy_send)):
        move.put(rows.at[1 - place.h], sent)
        move.put(rows.at[place.h], own)
    move.drain()


def pack_kernel(n, slots, groups, first_row, place, *refs):
    wq, wk, wv = refs[:3]
    small = refs[3:12]
    packed, q_s, k_s, v_s, *rest = refs[12:]
    small_s, (packed_s, sems) = rest[:9], rest[9:]
    move = Mover(sems)
    loads = [move.start(a, b) for a, b in ((wq, q_s), (wk, k_s), (wv, v_s))]
    loads += [move.start(a, b) for a, b in zip(small, small_s)]
    for copy in loads:
        copy.wait()
    rs = wq.shape[0]
    hd = wq.shape[1] // n
    chunk = small[8].shape[1]
    zeros = jnp.zeros((packed_s.shape[1] - rs, packed_s.shape[2]), bf16)
    for m in range(n):
        cols = slice(m * hd, (m + 1) * hd)
        packed_s[m, rs:, :] = zeros
        packed_s[m, :rs, :hd] = q_s[:, cols]
        packed_s[m, :rs, hd : 2 * hd] = k_s[:, cols]
        packed_s[m, :rs, 2 * hd : 3 * hd] = v_s[:, cols]
        for i in range(8):
            packed_s[m, first_row + i : first_row + i + 1, :rs] = small_s[i][...]
        packed_s[m, first_row : first_row + 1, hd : hd + chunk] = small_s[8][...]
    for i in range(slots):
        move.put(packed_s, packed.at[i * n : (i + 1) * n])
    move.drain()


def pack_up_kernel(n, groups, place, up, packed, up_s, packed_s, sems):
    move = Mover(sems)
    move.start(up, up_s).wait()
    chunk = up.shape[1] // (n * groups)
    for m in range(n):
        for g in range(groups):
            at = (g * n + m) * chunk
            packed_s[m, :, g * chunk : (g + 1) * chunk] = up_s[:, at : at + chunk]
    move.put(packed_s, packed)
    move.drain()


def join_kernel(n, place, up, down, ffn, sems):
    move = Mover(sems)
    width, mine = down.shape[1], ffn.shape[1]
    chunk = down.shape[0]
    feats = ffn.shape[0] - width // mine * chunk
    move.put(up, ffn.at[:feats, :])
    for c in range(width // mine):
        move.put(down.at[:, c * mine : (c + 1) * mine], ffn.at[feats + c * chunk : feats + (c + 1) * chunk, :])
    move.drain()


def key_mask(place, rows, n, half, width):
    row = lax.broadcasted_iota(jnp.int32, (rows, width), 0)
    member = row // (2 * half)
    inside = row % (2 * half)
    own = (inside < half).astype(jnp.int32)
    h = place.h
    block_half = own * h + (1 - own) * (1 - h)
    frame = (block_half * n + member) * half + inside % half
    return frame < place.length


def first_kernel(n, dp_size, groups, half, qb, first_row, place, *refs):
    xs, gots, wos = refs[:n], refs[n : n + dp_size], refs[n + dp_size : n + dp_size + groups // dp_size]
    at = n + dp_size + groups // dp_size
    outs = refs[at : at + 11]
    hat_out, h_out, qkv_out, o_out, lse_out, w_out, vec_out, bias_up_out, wo_out, keep, send = outs
    x_s, hat_s, h_s, qkv_s, o_s, lse_s, got_s, w_s, vec_s, bias_up_s, wo3, wo_s, y_s, send_s, bias, sems = refs[at + 11 :]
    move = Mover(sems)
    j = place.j
    rows = 2 * half
    total = n * rows
    ndev = got_s.shape[0]
    hd = got_s.shape[2] // 3
    seq_size = ndev // dp_size
    rs = x_s.shape[1] // ndev
    chunk = bias_up_s.shape[1] // groups
    load = [move.start(gots[i], got_s.at[pl.ds((place.dp ^ i) * seq_size, seq_size)]) for i in range(dp_size)]
    copies = [move.start(xs[r], x_s.at[rows_at(j ^ r, rows), :]) for r in range(n)]
    slots = groups // dp_size
    outw = [
        move.start(wos[i].at[k], wo3.at[(place.dp ^ k) * slots + (place.h ^ i)])
        for k in range(dp_size)
        for i in range(slots)
    ]
    bias[...] = jnp.where(key_mask(place, total, n, half, 128), 0.0, -1.0).astype(f32)
    for copy in load:
        copy.wait()
    for d in range(ndev):
        w_s[d * rs : (d + 1) * rs, :] = got_s[d, :rs, :]
        vec_s[:, d * rs : (d + 1) * rs] = got_s[d, first_row : first_row + 8, :rs].astype(f32)
    bq, bv = [], []
    for t in range(groups):
        bias_up_s[:, t * chunk : (t + 1) * chunk] = got_s[
            t * n + j, first_row : first_row + 1, hd : hd + chunk
        ].astype(f32)
        bq.append(got_s[j * groups + t, first_row + 2 : first_row + 3, :rs].astype(f32))
        bv.append(got_s[j * groups + t, first_row + 3 : first_row + 4, :rs].astype(f32))
    bq = jnp.concatenate(bq, axis=1)
    bv = jnp.concatenate(bv, axis=1)
    move.put(w_s, w_out)
    move.put(vec_s, vec_out)
    move.put(bias_up_s, bias_up_out)
    for r in range(n):
        copies[r].wait()
        base = pl.multiple_of((j ^ r) * rows, rows)
        for part in range(2):
            at = pl.ds(base + part * half, half)
            scaled, _ = normalize(x_s[at, :].astype(f32))
            hat_s[at, :] = scaled.astype(bf16)
            h_s[at, :] = (scaled * vec_s[0:1, :] + vec_s[1:2, :]).astype(bf16)
    block = min(512, total)
    for i in range(total // block):
        at = slice(i * block, (i + 1) * block)
        qkv = dot(h_s[at, :], w_s[...])
        qkv_s[at, :hd] = ((qkv[:, :hd] + bq) * 0.125).astype(bf16)
        qkv_s[at, hd : 2 * hd] = qkv[:, hd : 2 * hd].astype(bf16)
        qkv_s[at, 2 * hd :] = (qkv[:, 2 * hd :] + bv).astype(bf16)
    move.put(hat_s, hat_out)
    move.put(h_s, h_out)
    move.put(qkv_s, qkv_out)
    heads = hd // HEAD
    for head in range(heads):
        cols = slice(head * HEAD, (head + 1) * HEAD)
        kh = qkv_s[:, hd + head * HEAD : hd + (head + 1) * HEAD]
        vt = qkv_s[:, 2 * hd + head * HEAD : 2 * hd + (head + 1) * HEAD].astype(f32).T.astype(bf16)

        def step(i, _, cols=cols, kh=kh, vt=vt, head=head):
            at = rows_at(i, qb)
            scores = dot(kh, qkv_s[at, cols], NT)
            scores = jnp.where(bias[:, 0:1] >= 0.0, scores, -1e30)
            row_max = jnp.max(scores, axis=0, keepdims=True)
            e = jnp.exp(scores - row_max)
            row_sum = jnp.sum(e, axis=0, keepdims=True)
            ot = dot(vt, e.astype(bf16)) / row_sum
            o_s[at, cols] = ot.T.astype(bf16)
            lse_s[head : head + 1, at] = row_max + jnp.log(row_sum)
            return 0

        lax.fori_loop(0, total // qb, step, 0)
    move.put(o_s, o_out)
    move.put(lse_s, lse_out)
    for copy in outw:
        copy.wait()
    for t in range(groups):
        wo_s[t * rs : (t + 1) * rs, :] = wo3[t]
    move.put(wo_s, wo_out)
    for i in range(total // block):
        at = slice(i * block, (i + 1) * block)
        y_s[at, :] = dot(o_s[at, :], wo_s[...])
    send_rows(move, place, n, rows, y_s, send_s, keep, send)
    move.drain()


def mid_kernel(count, place, *refs):
    ins, x, vec = refs[:count], refs[count], refs[count + 1]
    y_out, h_out = refs[count + 2 : count + 4]
    held = refs[count + 4 : 2 * count + 4]
    x_s, vec_s, y_s, h_s, sems = refs[2 * count + 4 :]
    move = Mover(sems)
    loads = [move.start(a, b) for a, b in zip(ins, held)]
    loads += [move.start(x, x_s), move.start(vec, vec_s)]
    for copy in loads:
        copy.wait()
    y = held[0][...]
    for i in range(1, count):
        y = y + held[i][...].astype(f32)
    y = x_s[...].astype(f32) + y + vec_s[4:5, :]
    y_s[...] = y
    scaled, _ = normalize(y)
    h_s[...] = (scaled * vec_s[5:6, :] + vec_s[6:7, :]).astype(bf16)
    move.put(h_s, h_out)
    move.put(y_s, y_out)
    move.drain()


def down_back_kernel(n, groups, place, *refs):
    dys, ws = refs[:n], refs[n : n + groups]
    dy_out, dg_out, w_up_out, w_down_out, dy_s, dg_s, w_up, w_down, sems = refs[n + groups :]
    move = Mover(sems)
    j, g = place.j, place.group
    rows = dys[0].shape[0]
    chunk = w_down.shape[0] // groups
    mine = w_up.shape[1]
    feats = w_up.shape[0] // groups
    first, last = [], []
    for i in range(groups):
        for c in range(w_down.shape[1] // mine):
            source = ws[i].at[feats + c * chunk : feats + (c + 1) * chunk, :]
            first.append(move.start(source, w_down.at[rows_at(g ^ i, chunk), c * mine : (c + 1) * mine]))
    copies = [move.start(dys[r], dy_s.at[rows_at(j ^ r, rows), :]) for r in range(n)]
    for i in range(groups):
        last.append(move.start(ws[i].at[:feats, :], w_up.at[rows_at(g ^ i, feats), :]))
    for copy in first:
        copy.wait()
    move.put(w_down, w_down_out)
    for copy in copies:
        copy.wait()
    block = min(512, dy_s.shape[0])
    for i in range(dy_s.shape[0] // block):
        at = slice(i * block, (i + 1) * block)
        dg_s[at, :] = dot(dy_s[at, :], w_down[...], NT)
        move.put(dg_s.at[at, :], dg_out.at[at, :])
    for copy in last:
        copy.wait()
    move.put(w_up, w_up_out)
    move.put(dy_s, dy_out)
    move.drain()


def ffn_kernel(n, place, *refs):
    hs = refs[:n]
    w_up_in, b_up_in, dg_in = refs[n : n + 3]
    h_out, g_out, du_out, keep, send, db_out = refs[n + 3 : n + 9]
    w_up, b_up, dg, h_s, g_s, du_s, dh_s, send_s, db, sems = refs[n + 9 :]
    move = Mover(sems)
    rows = hs[0].shape[0]
    total = n * rows
    copies = [move.start(hs[r], h_s.at[rows_at(place.j ^ r, rows), :]) for r in range(n)]
    copies += [move.start(w_up_in, w_up), move.start(b_up_in, b_up)]
    late = move.start(dg_in, dg)
    for copy in copies:
        copy.wait()
    block = min(512, total)
    sums = jnp.zeros(db.shape, f32)
    for i in range(total // block):
        at = slice(i * block, (i + 1) * block)
        u = dot(h_s[at, :], w_up[...]) + b_up[...]
        cdf = 0.5 * (1.0 + lax.erf(u * inv_root_two))
        g_s[at, :] = (u * cdf).astype(bf16)
        slope = cdf + u * jnp.exp(-0.5 * u * u) * inv_root_tau
        if i == 0:
            late.wait()
        du = (dg[at, :] * slope).astype(bf16)
        du_s[at, :] = du
        sums = sums + jnp.sum(du.astype(f32), axis=0, keepdims=True)
        dh_s[at, :] = dot(du, w_up[...], NT)
    db[...] = sums
    send_rows(move, place, n, rows, dh_s, send_s, keep, send)
    move.put(h_s, h_out)
    move.put(g_s, g_out)
    move.put(du_s, du_out)
    move.put(db, db_out)
    move.drain()


def down_kernel(n, place, g_in, w_in, keep, send, g, w, out_s, send_s, sems):
    move = Mover(sems)
    for copy in [move.start(w_in, w), move.start(g_in, g)]:
        copy.wait()
    total = g.shape[0]
    block = min(512, total)
    for i in range(total // block):
        at = slice(i * block, (i + 1) * block)
        out_s[at, :] = dot(g[at, :], w[...])
    send_rows(move, place, n, total // n, out_s, send_s, keep, send)
    move.drain()


def ffn_grads_kernel(groups, place, h_in, du_in, dy_in, g_in, *refs):
    outs = refs[:groups]
    h, du, dy, g, grads, stage, sems = refs[groups:]
    move = Mover(sems)
    loads = [move.start(a, b) for a, b in ((h_in, h), (du_in, du), (dy_in, dy), (g_in, g))]
    feats = h.shape[1] // groups
    mine = du.shape[1]
    chunk = mine // groups
    loads[0].wait()
    loads[1].wait()
    for i in range(groups):
        grads[i, :feats, :] = dot(h[:, i * feats : (i + 1) * feats], du[...], TN)
    loads[2].wait()
    loads[3].wait()
    for c in range(dy.shape[1] // mine):
        part = dot(g[...], dy[:, c * mine : (c + 1) * mine], TN)
        for i in range(groups):
            grads[i, feats + c * chunk : feats + (c + 1) * chunk, :] = part[i * chunk : (i + 1) * chunk, :]
    for i in range(1, groups):
        stage[i - 1] = grads[place.group ^ i].astype(bf16)
        move.put(stage.at[i - 1], outs[i])
    move.put(grads.at[place.group], outs[0])
    move.drain()


def pair_kernel(place, keep, recv, *refs):
    count = (len(refs) - 3) // 2
    outs = refs[:count]
    keep_s, recv_s = refs[count : count + 2]
    stage, sems = refs[count + 2 : 2 * count + 2], refs[2 * count + 2]
    move = Mover(sems)
    rows = outs[0].shape[0]
    order = list(range(1, count)) + [0]
    loads = {}
    for i in order:
        here = slice(i * rows, (i + 1) * rows)
        loads[i] = (
            move.start(keep.at[here, :], keep_s.at[here, :]),
            move.start(recv.at[here, :], recv_s.at[here, :]),
        )
    for i in order:
        here = slice(i * rows, (i + 1) * rows)
        for copy in loads[i]:
            copy.wait()
        stage[i][...] = (keep_s[here, :] + recv_s[here, :].astype(f32)).astype(outs[i].dtype)
        move.put(stage[i], outs[i])
    move.drain()


def fold_kernel(count, place, *refs):
    ins, outs = refs[: 2 * count], refs[2 * count : 3 * count]
    held, stage, sems = refs[3 * count : 5 * count], refs[5 * count : 6 * count], refs[6 * count]
    move = Mover(sems)
    loads = [move.start(a, b) for a, b in zip(ins, held)]
    for i in range(count):
        loads[i].wait()
        loads[count + i].wait()
        stage[i][...] = (held[i][...].astype(f32) + held[count + i][...].astype(f32)).astype(bf16)
        move.put(stage[i], outs[i])
    move.drain()


def out_kernel(count, place, *refs):
    ins = refs[: count + 2]
    kept, sent = refs[count + 2 : count + 4]
    held = refs[count + 4 : 2 * count + 6]
    out_s, sems = refs[2 * count + 6 :]
    move = Mover(sems)
    for copy in [move.start(a, b) for a, b in zip(ins, held)]:
        copy.wait()
    total = held[0][...] + held[count][...]
    for i in range(1, count):
        total = total + held[i][...].astype(f32)
    out_s[...] = (total + held[count + 1][7:8, :]).astype(bf16)
    half = kept.shape[0]
    move.put(out_s.at[half:, :], sent)
    move.put(out_s.at[:half, :], kept)
    move.drain()


def mid_back_kernel(count, place, *refs):
    ins = refs[: count + 3]
    dy1_out, da_out, small_out = refs[count + 3 : count + 6]
    held = refs[count + 6 : 2 * count + 9]
    dy1_s, da_s, small, sems = refs[2 * count + 9 :]
    move = Mover(sems)
    for copy in [move.start(a, b) for a, b in zip(ins, held)]:
        copy.wait()
    dh = held[0][...]
    for i in range(1, count):
        dh = dh + held[i][...].astype(f32)
    y, vec, dy = held[count : count + 3]
    scaled, inv_std = normalize(y[...])
    dyf = dy[...].astype(f32)
    dy1 = dyf + norm_back(dh, scaled, inv_std, vec[5:6, :])
    da = dy1.astype(bf16)
    da_s[...] = da
    move.put(da_s, da_out)
    dy1_s[...] = dy1
    move.put(dy1_s, dy1_out)
    small[0:1, :] = jnp.sum(dh * scaled, axis=0, keepdims=True)
    small[1:2, :] = jnp.sum(dh, axis=0, keepdims=True)
    small[2:3, :] = jnp.sum(da.astype(f32), axis=0, keepdims=True)
    small[3:4, :] = jnp.sum(dyf, axis=0, keepdims=True)
    move.put(small, small_out)
    move.drain()


def attend_back_kernel(n, half, qb, place, *refs):
    das, ins = refs[:n], refs[n : n + 4]
    dqkv_out, keep, send, db_out, da_out = refs[n + 4 : n + 9]
    da, qkv, lse, wo, w, dqkv, dh_s, send_s, db, do, bias, acc_k, acc_v, sems = refs[n + 9 :]
    rows = 2 * half
    move = Mover(sems)
    copies = [move.start(das[r], da.at[rows_at(place.j ^ r, rows), :]) for r in range(n)]
    loads = [move.start(a, b) for a, b in zip(ins, (wo, qkv, lse, w))]
    total = qkv.shape[0]
    hd = do.shape[1]
    heads = hd // HEAD
    bias[...] = jnp.where(key_mask(place, total, n, half, 128), 0.0, -1.0).astype(f32)
    loads[0].wait()
    for copy in copies:
        copy.wait()
    move.put(da, da_out)
    block = min(512, total)
    for i in range(total // block):
        at = slice(i * block, (i + 1) * block)
        do[at, :] = dot(da[at, :], wo[...], NT).astype(bf16)
    for copy in loads[1:]:
        copy.wait()
    for head in range(heads):
        cols = slice(head * HEAD, (head + 1) * HEAD)
        kh = qkv[:, hd + head * HEAD : hd + (head + 1) * HEAD]
        vh = qkv[:, 2 * hd + head * HEAD : 2 * hd + (head + 1) * HEAD]
        kt = kh.astype(f32).T.astype(bf16)
        acc_k[...] = jnp.zeros_like(acc_k)
        acc_v[...] = jnp.zeros_like(acc_v)

        def step(i, _, cols=cols, kh=kh, vh=vh, kt=kt, head=head):
            at = rows_at(i, qb)
            qh = qkv[at, cols]
            doh = do[at, cols]
            scores = dot(kh, qh, NT)
            probs = jnp.where(bias[:, 0:1] >= 0.0, jnp.exp(scores - lse[head : head + 1, at]), 0.0)
            dp = dot(vh, doh, NT)
            centre = jnp.sum(probs * dp, axis=0, keepdims=True)
            ds = (probs * (dp - centre)).astype(bf16)
            acc_v[...] += dot(probs.astype(bf16), doh)
            acc_k[...] += dot(ds, qh)
            dq = dot(kt, ds)
            dqkv[at, cols] = (dq.T.astype(bf16).astype(f32) * 0.125).astype(bf16)
            return 0

        lax.fori_loop(0, total // qb, step, 0)
        dqkv[:, hd + head * HEAD : hd + (head + 1) * HEAD] = acc_k[...].astype(bf16)
        dqkv[:, 2 * hd + head * HEAD : 2 * hd + (head + 1) * HEAD] = acc_v[...].astype(bf16)
    move.put(dqkv, dqkv_out)
    sums = jnp.zeros(db.shape, f32)
    for i in range(total // block):
        at = slice(i * block, (i + 1) * block)
        grads = dqkv[at, :]
        sums = sums + jnp.sum(grads.astype(f32), axis=0, keepdims=True)
        dh_s[at, :] = dot(grads, w[...], NT)
    db[...] = sums
    send_rows(move, place, n, rows, dh_s, send_s, keep, send)
    move.put(db, db_out)
    move.drain()


def attn_grads_kernel(n, dp_size, groups, first_row, place, *refs):
    ins, outs = refs[:7], refs[7 : 7 + dp_size]
    dqkv, h, w, hat, two, db, up, small, grads, packed_s, sems = refs[7 + dp_size :]
    move = Mover(sems)
    j = place.j
    loads = [move.start(a, b) for a, b in zip(ins, (dqkv, h, w, hat, two, db, up))]
    ndev = packed_s.shape[0]
    hd = dqkv.shape[1] // 3
    rs = h.shape[1] // ndev
    chunk = up.shape[1] // groups
    loads[0].wait()
    loads[1].wait()
    grads[...] = dot(h[...], dqkv[...], TN).astype(bf16)
    for copy in loads[2:]:
        copy.wait()
    small[...] = jnp.zeros_like(small)
    step_rows = min(512, hat.shape[0])

    def step(i, _):
        at = rows_at(i, step_rows)
        dh = dot(dqkv[at, :], w[...], NT)
        small[0:1, :] += jnp.sum(dh * hat[at, :].astype(f32), axis=0, keepdims=True)
        small[1:2, :] += jnp.sum(dh, axis=0, keepdims=True)
        return 0

    lax.fori_loop(0, hat.shape[0] // step_rows, step, 0)
    small[4:8, :] = two[...]
    zeros = jnp.zeros((packed_s.shape[1] - rs, packed_s.shape[2]), bf16)
    for d in range(ndev):
        packed_s[d, rs:, :] = zeros
        packed_s[d, :rs, :] = grads[d * rs : (d + 1) * rs, :]
        packed_s[d, first_row : first_row + 8, :rs] = small[:, d * rs : (d + 1) * rs].astype(bf16)
    for t in range(groups):
        cols = slice(t * rs, (t + 1) * rs)
        at = j * groups + t
        packed_s[at, first_row + 2 : first_row + 3, :rs] = db[:, :hd][:, cols].astype(bf16)
        packed_s[at, first_row + 3 : first_row + 4, :rs] = db[:, 2 * hd :][:, cols].astype(bf16)
        packed_s[t * n + j, first_row : first_row + 1, hd : hd + chunk] = up[
            :, t * chunk : (t + 1) * chunk
        ].astype(bf16)
    seq_size = ndev // dp_size
    for i in list(range(1, dp_size)) + [0]:
        move.put(packed_s.at[pl.ds((place.dp ^ i) * seq_size, seq_size)], outs[i])
    move.drain()


def out_grads_kernel(dp_size, groups, place, da_in, o_in, *refs):
    outs = refs[:dp_size]
    da, o, grads, stage, sems = refs[dp_size:]
    move = Mover(sems)
    for copy in [move.start(o_in, o), move.start(da_in, da)]:
        copy.wait()
    all_rows = dot(o[...], da[...], TN)
    rs = grads.shape[1]
    for t in range(groups):
        grads[t] = all_rows[t * rs : (t + 1) * rs, :]
    slots = groups // dp_size
    for k in range(dp_size):
        for i in range(slots):
            stage[k, i] = grads[(place.dp ^ k) * slots + (place.h ^ i)].astype(bf16)
        move.put(stage.at[k], outs[k])
    move.drain()


def last_kernel(count, place, *refs):
    ins, rider = refs[: count + 3], refs[count + 3]
    kept, sent = refs[count + 4 : count + 6]
    held = refs[count + 6 : 2 * count + 9]
    out_s, sems = refs[2 * count + 9 :]
    move = Mover(sems)
    half = kept.shape[0]
    move.put(rider.at[1], sent.at[half:, :])
    for copy in [move.start(a, b) for a, b in zip(ins, held)]:
        copy.wait()
    x, dy1, vec = held[count:]
    dh = held[0][...]
    for i in range(1, count):
        dh = dh + held[i][...].astype(f32)
    scaled, inv_std = normalize(x[...].astype(f32))
    out_s[...] = (dy1[...] + norm_back(dh, scaled, inv_std, vec[0:1, :])).astype(bf16)
    move.put(out_s.at[half:, :], sent.at[:half, :])
    move.put(out_s.at[:half, :], kept)
    move.drain()


def ffn_sum_kernel(count, place, *refs):
    ins, (up_out, down_out) = refs[:count], refs[count : count + 2]
    held, (total, up_s, down_s, sems) = refs[count + 2 : 2 * count + 2], refs[2 * count + 2 :]
    move = Mover(sems)
    for copy in [move.start(a, b) for a, b in zip(ins, held)]:
        copy.wait()
    ffn = held[0][...].astype(f32)
    for piece in held[1:]:
        ffn = ffn + piece[...].astype(f32)
    total[...] = ffn
    n, rs, mine = up_s.shape
    chunk, width = down_s.shape
    for m in range(n):
        up_s[m] = total[m * rs : (m + 1) * rs, :].astype(bf16)
    move.put(up_s, up_out)
    feats = n * rs
    for c in range(width // mine):
        down_s[:, c * mine : (c + 1) * mine] = total[feats + c * chunk : feats + (c + 1) * chunk, :]
    move.put(down_s, down_out)
    move.drain()


def unpack_kernel(n, groups, first_row, place, *refs):
    back, up_back, out_w = refs[:3]
    halves = refs[3:7]
    output, frames_grad, out_w_grad, up, wq, wk, wv = refs[7:14]
    vectors = refs[14:23]
    back_s, up_back_s, in_s, out_s, up_s, q_s, k_s, v_s = refs[23:31]
    vectors_s, sems = refs[31:40], refs[40]
    move = Mover(sems)
    load, more, third = move.start(back, back_s), move.start(up_back, up_back_s), move.start(out_w, in_s)
    half = output.shape[1]
    for i, target in enumerate((output, frames_grad)):
        move.put(halves[2 * i], target.at[place.h])
        move.put(halves[2 * i + 1].at[:half, :], target.at[1 - place.h])
    third.wait()
    out_s[...] = in_s[...].astype(f32)
    move.put(out_s, out_w_grad)
    rs = wq.shape[0]
    hd = wq.shape[1] // n
    chunk = up.shape[1] // (n * groups)
    more.wait()
    for m in range(n):
        for g in range(groups):
            at = (g * n + m) * chunk
            up_s[:, at : at + chunk] = up_back_s[m, :, g * chunk : (g + 1) * chunk].astype(f32)
    move.put(up_s, up)
    load.wait()
    sums = jnp.zeros((8, 3 * hd), f32)
    for m in range(n):
        cols = slice(m * hd, (m + 1) * hd)
        total = back_s[m].astype(f32)
        for i in range(m + n, back_s.shape[0], n):
            total = total + back_s[i].astype(f32)
        for i, target in enumerate((q_s, k_s, v_s)):
            target[:, cols] = total[:rs, i * hd : (i + 1) * hd]
        sums = sums + total[first_row:, :]
    for a, b in ((q_s, wq), (k_s, wk), (v_s, wv)):
        move.put(a, b)
    for i in range(8):
        vectors_s[i][...] = sums[i : i + 1, :rs]
    vectors_s[8][...] = sums[0:1, hd : hd + chunk]
    for a, b in zip(vectors_s, vectors):
        move.put(a, b)
    move.drain()


def on_device(
    dp_size,
    seq_size,
    frames,
    out_grad,
    order,
    lengths,
    first_gain,
    first_shift,
    query_weight,
    query_bias,
    key_weight,
    value_weight,
    value_bias,
    output_weight,
    output_bias,
    second_gain,
    second_shift,
    up_weight,
    up_bias,
    down_weight,
    down_bias,
):
    slots, half, width = frames.shape
    n = seq_size // slots
    groups = dp_size * slots
    ndev = dp_size * seq_size
    hd = width // n
    heads = hd // HEAD
    rs = query_weight.shape[0]
    hidden = up_weight.shape[1]
    chunk = hidden // ndev
    mine = hidden // n
    parts = width // mine
    feats = n * rs
    rows = 2 * half
    total = n * rows
    qb = 512
    count = n // 2
    both = ("dp", "seq")
    first_row = -(-rs // 8) * 8
    block_rows = first_row + 8

    scale = -(-total // 1024)
    grid = (slots, n, scale)

    def xor(value, bit):
        return lax.ppermute(value, "seq", [(i, i ^ bit) for i in range(seq_size)])

    def gather_direct(value):
        got = [xor(value, r) for r in range(n - 2, 0, -2)]
        return [value] + got[::-1]

    def gather_pair(even):
        out = []
        for piece in even:
            out += [piece, xor(piece, 1)]
        return out

    def pair(keep, recv):
        outs = [sds((rows, width), f32)] + [sds((rows, width), bf16)] * (count - 1)
        return call(
        grid,
            pair_kernel,
            [keep, Near(recv)],
            near(outs),
            "pair",
            cost(1),
            scratch=[vmem(keep), vmem(recv)] + [vmem(o) for o in outs],
            sems=3 * count,
        )

    def scatter(pieces):
        return [pieces[0]] + [xor(pieces[i], 2 * i) for i in range(count - 1, 0, -1)][::-1]

    def to_group(value, i):
        pairs = []
        for d in range(ndev):
            dp_of, seq_of = d // seq_size, d % seq_size
            g_of = (dp_of * slots + seq_of // n) ^ i
            pairs.append((d, g_of // slots * seq_size + g_of % slots * n + seq_of % n))
        return lax.ppermute(value, both, pairs)

    def members(value):
        index = [[s * n + i for i in range(n)] for s in range(slots)]
        return lax.all_to_all(value, "seq", 0, 0, tiled=True, axis_index_groups=index)

    def fold(kept, got):
        outs = [sds(a.shape, bf16) for a in kept]
        return call(
            grid,
            functools.partial(fold_kernel, len(kept)),
            near(list(kept) + list(got)),
            near(outs),
            "fold",
            cost(2),
            scratch=[vmem(a) for a in list(kept) + list(got) + outs],
            sems=3 * len(kept),
        )

    def spread(pieces):
        bit = len(pieces)
        while bit < groups:
            pieces = pieces + [to_group(piece, bit) for piece in pieces]
            bit *= 2
        return pieces

    def to_dp(value, i):
        return lax.ppermute(value, "dp", [(d, d ^ i) for d in range(dp_size)])

    def owner_pairs(k):
        pairs = []
        for d in range(ndev):
            g_of = (d % groups) ^ (k * slots)
            pairs.append((d, g_of // slots * seq_size + g_of % slots * n + d // groups))
        return pairs

    owners = owner_pairs(0)
    out_w = jnp.stack([lax.ppermute(output_weight, both, owner_pairs(k)) for k in range(dp_size)])

    small_in = [first_gain, first_shift, query_bias, value_bias, output_bias, second_gain, second_shift, down_bias]
    small_in = [v.reshape(1, -1) for v in small_in + [up_bias]]
    weights_in = [query_weight, key_weight, value_weight]
    half_sds, row_sds = sds((half, width), bf16), sds((rows, width), bf16)
    packed_sds, up_sds = sds((seq_size, block_rows, 3 * hd), bf16), sds((n, rs, mine), bf16)
    x_own, x_send, dy_own, dy_send = call(
        grid, rows_kernel, [frames, out_grad], near([half_sds] * 4), "rows", cost(1), sems=4
    )
    x_recv = xor(x_send, n)
    (packed,) = call(
        grid,
        functools.partial(pack_kernel, n, slots, groups, first_row),
        [after(weights_in[0], x_send)] + weights_in[1:] + small_in,
        near([packed_sds]),
        "pack",
        cost(2),
        scratch=[vmem(w) for w in weights_in] + [vmem(v) for v in small_in] + [pltpu.VMEM((n, block_rows, 3 * hd), bf16)],
        sems=12 + slots,
    )
    (up_packed,) = call(
        grid,
        functools.partial(pack_up_kernel, n, groups),
        [up_weight],
        near([up_sds]),
        "pack_up",
        cost(1),
        scratch=[vmem(up_weight), vmem(up_sds)],
        sems=2,
    )
    attn_w = lax.all_to_all(packed, "seq", 0, 0, tiled=True)
    up_mine = members(after(up_packed, attn_w))
    x = jnp.concatenate([x_own, x_recv])
    x_even = gather_direct(x)
    wos = [out_w, xor(out_w, n)]
    dy_recv = xor(after(dy_send, attn_w), n)
    attn_ws = [attn_w]
    while len(attn_ws) < dp_size:
        attn_ws += [to_dp(piece, len(attn_ws)) for piece in attn_ws]
    ffn_sds = sds((feats + parts * chunk, mine), bf16)
    (ffn_w,) = call(
        grid,
        functools.partial(join_kernel, n),
        near([up_mine.reshape(feats, mine), down_weight]),
        near([ffn_sds]),
        "join",
        cost(1),
        sems=1 + parts,
    )
    ffn_half = to_group(after(ffn_w, attn_w), 1)
    xs = gather_pair([after(piece, attn_ws[-1], wos[-1]) for piece in x_even])
    dy = jnp.concatenate([dy_own, dy_recv])

    ffn_go, dy_go, xs, attn_ws, wos = lax.optimization_barrier((ffn_w, dy, tuple(xs), tuple(attn_ws), tuple(wos)))
    xs, attn_ws, wos = list(xs), list(attn_ws), list(wos)
    ffn_ws = [ffn_w, ffn_half, to_group(ffn_go, 2)]
    dy_even = gather_direct(dy_go)
    x_sds = sds((total, width), bf16)
    keep_sds, send_sds = sds((total // 2, width), f32), sds((total // 2, width), bf16)
    outs = [
        x_sds,
        x_sds,
        sds((total, 3 * hd), bf16),
        sds((total, hd), bf16),
        sds((heads, total), f32),
        sds((width, 3 * hd), bf16),
        sds((8, width), f32),
        sds((1, mine), f32),
        sds((hd, width), bf16),
        keep_sds,
        send_sds,
    ]
    s_hat, s_h, s_qkv, s_o, s_lse, s_w, s_vec, s_bias, s_wo, _, s_send = [vmem(o) for o in outs]
    s_rows = pltpu.VMEM((total, width), f32)
    s_got = pltpu.VMEM((ndev, block_rows, 3 * hd), bf16)
    s_wo3 = pltpu.VMEM((groups, rs, width), bf16)
    hat, h_first, qkv, o_heads, lse, w_qkv, vec, bias_up, wo, keep, send = call(
        grid,
        functools.partial(first_kernel, n, dp_size, groups, half, qb, first_row),
        near(xs + attn_ws + wos),
        outs[:-1] + near(outs[-1:]),
        "first",
        cost(17),
        scratch=[vmem(x_sds), s_hat, s_h, s_qkv, s_o, s_lse, s_got, s_w, s_vec, s_bias, s_wo3, s_wo, s_rows, s_send]
        + [pltpu.VMEM((total, 128), f32)],
        sems=3 * n + groups + dp_size + 10,
        lengths=(order, lengths),
        limit=48,
    )
    send = after(send, *ffn_ws[1:], *dy_even[1:])

    y_sds = sds((rows, width), f32)
    y_pieces = pair(keep, xor(send, 1))
    ys = scatter(y_pieces)
    dys = gather_pair([dy_even[0]] + [after(piece, y_pieces[0]) for piece in dy_even[1:]])
    ffn_ws = spread(ffn_ws + [to_group(after(ffn_ws[1], y_pieces[0]), 2)])
    y1, h2 = call(
        grid,
        functools.partial(mid_kernel, count),
        near(ys + [x]) + [vec],
        [y_sds, Near(row_sds)],
        "mid",
        cost(2),
        scratch=[vmem(a) for a in ys + [row_sds, vec, y_sds, row_sds]],
        sems=count + 4,
    )
    h2_even = gather_direct(h2)

    outs = [x_sds, sds((total, mine), f32), sds((width, mine), bf16), sds((mine, width), bf16)]
    dy_all, dg, w_up, w_down = call(
        grid,
        functools.partial(down_back_kernel, n, groups),
        near(dys + ffn_ws),
        outs,
        "down_back",
        cost(5),
        scratch=[vmem(o) for o in outs],
        sems=2 * n + groups * (parts + 1) + 3,
        limit=14 * scale,
    )
    h2s = gather_pair(h2_even[:1] + [after(piece, dg) for piece in h2_even[1:]])

    act_sds = sds((total, mine), bf16)
    outs = [x_sds, act_sds, act_sds, keep_sds, send_sds, sds((1, mine), f32)]
    h2_all, g, du, keep, send, d_bias_up = call(
        grid,
        functools.partial(ffn_kernel, n),
        near(h2s) + [w_up, bias_up, dg],
        outs[:4] + near(outs[4:5]) + outs[5:],
        "ffn",
        cost(9),
        scratch=[vmem(a) for a in [w_up, bias_up, dg] + outs[:3]] + [s_rows, vmem(outs[4]), vmem(outs[5])],
        sems=3 * n + 7,
        limit=28 * scale,
    )
    dh2 = scatter(pair(keep, xor(send, 1)))

    g_then = after(g, dh2[0])
    out_keep, out_send = call(
        grid,
        functools.partial(down_kernel, n),
        [g_then, w_down],
        [keep_sds, Near(send_sds)],
        "down",
        cost(4),
        scratch=[vmem(g), vmem(w_down), s_rows, vmem(send_sds)],
        sems=n + 2,
        limit=16 * scale,
    )
    ffn_parts = call(
        grid,
        functools.partial(ffn_grads_kernel, groups),
        [h2_all, du, dy_all, g_then],
        [sds(ffn_sds.shape, f32)] + near([ffn_sds] * (groups - 1)),
        "ffn_grads",
        cost(5),
        scratch=[vmem(a) for a in (x_sds, act_sds, x_sds, act_sds)]
        + [pltpu.VMEM((groups,) + ffn_sds.shape, f32), pltpu.VMEM((groups - 1,) + ffn_sds.shape, bf16)],
        sems=4 + groups,
        limit=20 * scale,
    )

    small_sds = sds((4, width), f32)
    outs = [y_sds, row_sds, small_sds]
    dy1, da, small_two = call(
        grid,
        functools.partial(mid_back_kernel, count),
        near(dh2) + [after(y1, ffn_parts[0], out_keep), vec, Near(dy)],
        outs[:1] + near(outs[1:2]) + outs[2:],
        "mid_back",
        cost(3),
        scratch=[vmem(a) for a in dh2 + [y1, vec, row_sds] + outs],
        sems=count + 6,
    )
    da_even = gather_direct(da)
    bit = groups // 2
    while bit > 2:
        ffn_parts = fold(ffn_parts[:bit], [to_group(piece, bit) for piece in ffn_parts[bit:]])
        bit //= 2
    ffn_got = [to_group(piece, 2) for piece in ffn_parts[2:4]]
    out_kept = pair(out_keep, xor(after(out_send, da), 1))
    (ffn_next,) = fold([after(ffn_parts[1], out_kept[0])], ffn_got[1:])
    das = gather_pair([da_even[0]] + [after(piece, ffn_next) for piece in da_even[1:]])

    out_kept, das, ffn_next = lax.optimization_barrier((tuple(out_kept), tuple(das), ffn_next))
    out_kept, das = list(out_kept), list(das)
    ffn_got = [ffn_got[0], to_group(ffn_next, 1)]
    out_pieces = scatter(out_kept)
    ins = [wo, qkv, lse, w_qkv]
    outs = [sds((total, 3 * hd), bf16), keep_sds, send_sds, sds((1, 3 * hd), f32), x_sds]
    d_qkv, keep, send, d_bias_qkv, da_all = call(
        grid,
        functools.partial(attend_back_kernel, n, half, qb),
        near(das) + ins,
        outs[:2] + near(outs[2:3]) + outs[3:],
        "attend_back",
        cost(15),
        scratch=[vmem(x_sds)]
        + [vmem(a) for a in (qkv, lse, wo, w_qkv, outs[0])]
        + [s_rows, vmem(outs[2]), vmem(outs[3]), pltpu.VMEM((total, hd), bf16), pltpu.VMEM((total, 128), f32)]
        + [pltpu.VMEM((total, HEAD), f32)] * 2,
        sems=2 * n + 9,
        lengths=(order, lengths),
        limit=48,
    )
    recv = xor(after(send, *out_pieces[1:], *ffn_got), 1)

    ins = [d_qkv, h_first, w_qkv, hat, small_two, d_bias_qkv, d_bias_up]
    attn_parts = call(
        grid,
        functools.partial(attn_grads_kernel, n, dp_size, groups, first_row),
        ins,
        near([packed_sds] * dp_size),
        "attn_grads",
        cost(6),
        scratch=[vmem(a) for a in ins]
        + [
            pltpu.VMEM((8, width), f32),
            pltpu.VMEM((width, 3 * hd), bf16),
            pltpu.VMEM((ndev, block_rows, 3 * hd), bf16),
        ],
        sems=7 + dp_size,
        limit=20 * scale,
    )
    dh1_pieces = pair(after(keep, attn_parts[0]), recv)
    dh1 = scatter(dh1_pieces)
    bit = dp_size // 2
    while bit > 1:
        attn_parts = fold(attn_parts[:bit], [to_dp(piece, bit) for piece in attn_parts[bit:]])
        bit //= 2
    attn_got = to_dp(attn_parts[1], 1)

    ffn_sums = [after(ffn_parts[0], dh1_pieces[0])] + ffn_got
    down_sds = sds((chunk, width), f32)
    up_back, down_weight_grad = call(
        grid,
        functools.partial(ffn_sum_kernel, 3),
        ffn_sums[:1] + near(ffn_sums[1:]),
        [Near(up_sds), down_sds],
        "ffn_sum",
        cost(2),
        scratch=[vmem(a) for a in ffn_sums] + [pltpu.VMEM(ffn_sds.shape, f32), vmem(up_sds), vmem(down_sds)],
        sems=5,
    )
    up_back = members(up_back)
    out_parts = call(
        grid,
        functools.partial(out_grads_kernel, dp_size, groups),
        [da_all, after(o_heads, dh1_pieces[0])],
        near([sds((slots, rs, width), bf16)] * dp_size),
        "out_grads",
        cost(2),
        scratch=[
            vmem(x_sds),
            vmem(o_heads),
            pltpu.VMEM((groups, rs, width), f32),
            pltpu.VMEM((dp_size, slots, rs, width), bf16),
        ],
        sems=2 + dp_size,
        limit=10 * scale,
    )
    bit = dp_size // 2
    while bit > 1:
        out_parts = fold(out_parts[:bit], [to_dp(piece, bit) for piece in out_parts[bit:]])
        bit //= 2

    (attn_sum,) = fold([after(attn_parts[0], up_back)], [attn_got])
    back = lax.all_to_all(attn_sum, "seq", 0, 0, tiled=True)
    (out_w_sum,) = fold([after(out_parts[0], attn_sum)], [to_dp(out_parts[1], 1)])

    ins = out_pieces + [y1, vec]
    out_own, out_sent = call(
        grid,
        functools.partial(out_kernel, count),
        near([after(ins[0], attn_sum)] + ins[1:count]) + ins[count:],
        near([half_sds] * 2),
        "out",
        cost(2),
        scratch=[vmem(a) for a in ins + [row_sds]],
        sems=len(ins) + 2,
    )
    out_other = xor(out_sent, n)

    ins = dh1 + [x, after(dy1, attn_sum), vec]
    kept, sent = call(
        grid,
        functools.partial(last_kernel, count),
        near(ins[: count + 1]) + ins[count + 1 :] + near([out_w_sum]),
        near([half_sds, sds((half + rs, width), bf16)]),
        "last",
        cost(2),
        scratch=[vmem(a) for a in ins + [row_sds]],
        sems=len(ins) + 3,
    )
    other = xor(sent, n)
    out_w = (out_w_sum[0].astype(f32) + other[half:].astype(f32)).astype(bf16)
    out_w = lax.ppermute(out_w, both, [(b, a) for a, b in owners])
    frames_sds = sds(frames.shape, bf16)
    weight_sds = sds((rs, width), f32)
    outs = [weight_sds, sds((rs, hidden), f32)] + [weight_sds] * 3
    vectors = [sds((1, rs), f32)] * 8 + [sds((1, chunk), f32)]
    output, frames_grad, output_weight_grad, up_weight_grad, d_query, d_key, d_value, *vectors = call(
        grid,
        functools.partial(unpack_kernel, n, groups, first_row),
        near([back, up_back, out_w, out_own, out_other, kept, other]),
        [frames_sds] * 2 + outs + vectors,
        "unpack",
        cost(2),
        scratch=[vmem(a) for a in [back, up_back, out_w] + outs + vectors],
        sems=24,
    )
    vectors = [v.reshape(-1) for v in vectors]
    return (
        output,
        frames_grad,
        vectors[0],
        vectors[1],
        d_query,
        vectors[2],
        d_key,
        d_value,
        vectors[3],
        output_weight_grad,
        vectors[6],
        vectors[4],
        vectors[5],
        up_weight_grad,
        vectors[8],
        down_weight_grad,
        vectors[7],
    )


def solution(mesh):
    vector = P(("dp", "seq"))
    matrix = P(("dp", "seq"), None)
    rows = P("dp", "seq", None)
    return jax.shard_map(
        functools.partial(on_device, mesh.shape["dp"], mesh.shape["seq"]),
        mesh=mesh,
        in_specs=(
            rows,
            rows,
            P("dp"),
            P(),
            vector,
            vector,
            matrix,
            vector,
            matrix,
            matrix,
            vector,
            matrix,
            vector,
            vector,
            vector,
            matrix,
            vector,
            matrix,
            vector,
        ),
        out_specs=(
            rows,
            rows,
            vector,
            vector,
            matrix,
            vector,
            matrix,
            matrix,
            vector,
            matrix,
            vector,
            vector,
            vector,
            matrix,
            vector,
            matrix,
            vector,
        ),
        check_vma=False,
    )
```

```python
import functools

import jax
import jax.numpy as jnp
from jax import lax
from jax.experimental import pallas as pl
from jax.experimental.pallas import tpu as pltpu
from jax.sharding import PartitionSpec as P

HEAD = 64
f32 = jnp.float32
bf16 = jnp.bfloat16
norm_eps = 1e-05
inv_root_two = 0.7071067811865476
inv_root_tau = 0.3989422804014327
NN = (((1,), (0,)), ((), ()))
NT = (((1,), (1,)), ((), ()))
TN = (((0,), (0,)), ((), ()))
MIB = 1024 * 1024


def dot(a, b, dims=NN):
    return lax.dot_general(a, b, dims, preferred_element_type=f32)


def normalize(rows):
    average = jnp.mean(rows, axis=-1, keepdims=True)
    centered = rows - average
    inv_std = lax.rsqrt(jnp.mean(centered * centered, axis=-1, keepdims=True) + norm_eps)
    return centered * inv_std, inv_std


def norm_back(grad_rows, scaled, inv_std, gain):
    grad_hat = grad_rows * gain
    return inv_std * (
        grad_hat
        - jnp.mean(grad_hat, axis=-1, keepdims=True)
        - scaled * jnp.mean(grad_hat * scaled, axis=-1, keepdims=True)
    )


def sds(shape, dtype):
    return jax.ShapeDtypeStruct(shape, dtype)


def vmem(like):
    return pltpu.VMEM(like.shape, like.dtype)


class Near:
    def __init__(self, array):
        self.array = array
        self.shape, self.dtype = array.shape, array.dtype


def near(arrays):
    return [Near(a) for a in arrays]


class Place:
    def __init__(self, slots, n):
        seq_at = lax.axis_index("seq")
        self.h, self.j = seq_at // n, seq_at % n
        self.dp = lax.axis_index("dp")
        self.group = self.dp * slots + self.h
        self.length = None


def call(grid, kernel, args, outs, name, flops=0, scratch=(), sems=1, limit=None, lengths=()):
    here = pl.BlockSpec(memory_space=pltpu.HBM)
    anywhere = pl.BlockSpec(memory_space=pl.ANY)
    scalars = pl.BlockSpec(memory_space=pltpu.SMEM)
    nbytes = sum(a.shape[0] * a.shape[1] * a.dtype.itemsize for a in list(args) + list(outs))

    def body(*refs):
        place = Place(*grid[:2])
        if lengths:
            order_ref, lengths_ref = refs[:2]
            place.length = lengths_ref[order_ref[place.h]]
        kernel(place, *refs[len(lengths) :])

    return pl.pallas_call(
        body,
        out_shape=tuple(o.array if isinstance(o, Near) else pltpu.HBM(o.shape, o.dtype) for o in outs),
        in_specs=[scalars] * len(lengths) + [anywhere if isinstance(a, Near) else here for a in args],
        out_specs=tuple(anywhere if isinstance(o, Near) else here for o in outs),
        scratch_shapes=list(scratch) + [pltpu.SemaphoreType.DMA((sems,))],
        compiler_params=pltpu.CompilerParams(vmem_limit_bytes=(limit or 8 * grid[2]) * MIB),
        cost_estimate=pl.CostEstimate(flops=int(flops), bytes_accessed=int(nbytes), transcendentals=0),
        name=name,
    )(
        *lengths,
        *[a.array if isinstance(a, Near) else pltpu.with_memory_space_constraint(a, pltpu.HBM) for a in args],
    )


class Mover:
    def __init__(self, sems):
        self.sems, self.used, self.open = sems, 0, []

    def start(self, source, target):
        copy = pltpu.make_async_copy(source, target, self.sems.at[self.used])
        self.used += 1
        copy.start()
        return copy

    def put(self, source, target):
        self.open.append(self.start(source, target))

    def drain(self):
        for copy in self.open:
            copy.wait()
        self.open = []


def cost(microseconds):
    return microseconds * 1150 * 10**6


def after(value, *others):
    return lax.optimization_barrier((value,) + others)[0]


def rows_at(index, rows):
    return pl.ds(pl.multiple_of(index * rows, rows), rows)


def send_rows(move, place, n, rows, source, stage, keep, send):
    for r in list(range(1, n, 2)) + list(range(0, n, 2)):
        here = slice((r // 2) * rows, (r // 2 + 1) * rows)
        stage[r % 2, here, :] = source[rows_at(place.j ^ r, rows), :].astype(bf16)
        move.put(stage.at[r % 2, here, :], (send if r % 2 else keep).at[here, :])


def rows_kernel(place, frames, out_grad, x_own, x_send, dy_own, dy_send, sems):
    move = Mover(sems)
    for rows, own, sent in ((frames, x_own, x_send), (out_grad, dy_own, dy_send)):
        move.put(rows.at[1 - place.h], sent)
        move.put(rows.at[place.h], own)
    move.drain()


def pack_kernel(n, slots, groups, first_row, place, *refs):
    wq, wk, wv = refs[:3]
    small = refs[3:12]
    packed, q_s, k_s, v_s, *rest = refs[12:]
    small_s, (packed_s, sems) = rest[:9], rest[9:]
    move = Mover(sems)
    loads = [move.start(a, b) for a, b in ((wq, q_s), (wk, k_s), (wv, v_s))]
    loads += [move.start(a, b) for a, b in zip(small, small_s)]
    for copy in loads:
        copy.wait()
    rs = wq.shape[0]
    hd = wq.shape[1] // n
    chunk = small[8].shape[1]
    zeros = jnp.zeros((packed_s.shape[1] - rs, packed_s.shape[2]), bf16)
    for m in range(n):
        cols = slice(m * hd, (m + 1) * hd)
        packed_s[m, rs:, :] = zeros
        packed_s[m, :rs, :hd] = q_s[:, cols]
        packed_s[m, :rs, hd : 2 * hd] = k_s[:, cols]
        packed_s[m, :rs, 2 * hd : 3 * hd] = v_s[:, cols]
        for i in range(8):
            packed_s[m, first_row + i : first_row + i + 1, :rs] = small_s[i][...]
        packed_s[m, first_row : first_row + 1, hd : hd + chunk] = small_s[8][...]
    for i in range(slots):
        move.put(packed_s, packed.at[i * n : (i + 1) * n])
    move.drain()


def pack_up_kernel(n, groups, place, up, packed, up_s, packed_s, sems):
    move = Mover(sems)
    move.start(up, up_s).wait()
    chunk = up.shape[1] // (n * groups)
    for m in range(n):
        for g in range(groups):
            at = (g * n + m) * chunk
            packed_s[m, :, g * chunk : (g + 1) * chunk] = up_s[:, at : at + chunk]
    move.put(packed_s, packed)
    move.drain()


def join_kernel(n, place, up, down, ffn, sems):
    move = Mover(sems)
    width, mine = down.shape[1], ffn.shape[1]
    chunk = down.shape[0]
    feats = ffn.shape[0] - width // mine * chunk
    move.put(up, ffn.at[:feats, :])
    for c in range(width // mine):
        move.put(down.at[:, c * mine : (c + 1) * mine], ffn.at[feats + c * chunk : feats + (c + 1) * chunk, :])
    move.drain()


def key_mask(place, rows, n, half, width):
    row = lax.broadcasted_iota(jnp.int32, (rows, width), 0)
    member = row // (2 * half)
    inside = row % (2 * half)
    own = (inside < half).astype(jnp.int32)
    h = place.h
    block_half = own * h + (1 - own) * (1 - h)
    frame = (block_half * n + member) * half + inside % half
    return frame < place.length


def first_kernel(n, dp_size, groups, half, qb, first_row, place, *refs):
    xs, gots, wos = refs[:n], refs[n : n + dp_size], refs[n + dp_size : n + dp_size + groups // dp_size]
    at = n + dp_size + groups // dp_size
    outs = refs[at : at + 11]
    hat_out, h_out, qkv_out, o_out, lse_out, w_out, vec_out, bias_up_out, wo_out, keep, send = outs
    x_s, hat_s, h_s, qkv_s, o_s, lse_s, got_s, w_s, vec_s, bias_up_s, wo3, wo_s, y_s, send_s, bias, sems = refs[at + 11 :]
    move = Mover(sems)
    j = place.j
    rows = 2 * half
    total = n * rows
    ndev = got_s.shape[0]
    hd = got_s.shape[2] // 3
    seq_size = ndev // dp_size
    rs = x_s.shape[1] // ndev
    chunk = bias_up_s.shape[1] // groups
    load = [move.start(gots[i], got_s.at[pl.ds((place.dp ^ i) * seq_size, seq_size)]) for i in range(dp_size)]
    copies = [move.start(xs[r], x_s.at[rows_at(j ^ r, rows), :]) for r in range(n)]
    slots = groups // dp_size
    outw = [
        move.start(wos[i].at[k], wo3.at[(place.dp ^ k) * slots + (place.h ^ i)])
        for k in range(dp_size)
        for i in range(slots)
    ]
    bias[...] = jnp.where(key_mask(place, total, n, half, 128), 0.0, -1.0).astype(f32)
    for copy in load:
        copy.wait()
    for d in range(ndev):
        w_s[d * rs : (d + 1) * rs, :] = got_s[d, :rs, :]
        vec_s[:, d * rs : (d + 1) * rs] = got_s[d, first_row : first_row + 8, :rs].astype(f32)
    bq, bv = [], []
    for t in range(groups):
        bias_up_s[:, t * chunk : (t + 1) * chunk] = got_s[
            t * n + j, first_row : first_row + 1, hd : hd + chunk
        ].astype(f32)
        bq.append(got_s[j * groups + t, first_row + 2 : first_row + 3, :rs].astype(f32))
        bv.append(got_s[j * groups + t, first_row + 3 : first_row + 4, :rs].astype(f32))
    bq = jnp.concatenate(bq, axis=1)
    bv = jnp.concatenate(bv, axis=1)
    move.put(w_s, w_out)
    move.put(vec_s, vec_out)
    move.put(bias_up_s, bias_up_out)
    for r in range(n):
        copies[r].wait()
        base = pl.multiple_of((j ^ r) * rows, rows)
        for part in range(2):
            at = pl.ds(base + part * half, half)
            scaled, _ = normalize(x_s[at, :].astype(f32))
            hat_s[at, :] = scaled.astype(bf16)
            h_s[at, :] = (scaled * vec_s[0:1, :] + vec_s[1:2, :]).astype(bf16)
    block = min(512, total)
    for i in range(total // block):
        at = slice(i * block, (i + 1) * block)
        qkv = dot(h_s[at, :], w_s[...])
        qkv_s[at, :hd] = ((qkv[:, :hd] + bq) * 0.125).astype(bf16)
        qkv_s[at, hd : 2 * hd] = qkv[:, hd : 2 * hd].astype(bf16)
        qkv_s[at, 2 * hd :] = (qkv[:, 2 * hd :] + bv).astype(bf16)
    move.put(hat_s, hat_out)
    move.put(h_s, h_out)
    move.put(qkv_s, qkv_out)
    heads = hd // HEAD
    for head in range(heads):
        cols = slice(head * HEAD, (head + 1) * HEAD)
        kh = qkv_s[:, hd + head * HEAD : hd + (head + 1) * HEAD]
        vt = qkv_s[:, 2 * hd + head * HEAD : 2 * hd + (head + 1) * HEAD].astype(f32).T.astype(bf16)

        def step(i, _, cols=cols, kh=kh, vt=vt, head=head):
            at = rows_at(i, qb)
            scores = dot(kh, qkv_s[at, cols], NT)
            scores = jnp.where(bias[:, 0:1] >= 0.0, scores, -1e30)
            row_max = jnp.max(scores, axis=0, keepdims=True)
            e = jnp.exp(scores - row_max)
            row_sum = jnp.sum(e, axis=0, keepdims=True)
            ot = dot(vt, e.astype(bf16)) / row_sum
            o_s[at, cols] = ot.T.astype(bf16)
            lse_s[head : head + 1, at] = row_max + jnp.log(row_sum)
            return 0

        lax.fori_loop(0, total // qb, step, 0)
    move.put(o_s, o_out)
    move.put(lse_s, lse_out)
    for copy in outw:
        copy.wait()
    for t in range(groups):
        wo_s[t * rs : (t + 1) * rs, :] = wo3[t]
    move.put(wo_s, wo_out)
    for i in range(total // block):
        at = slice(i * block, (i + 1) * block)
        y_s[at, :] = dot(o_s[at, :], wo_s[...])
    send_rows(move, place, n, rows, y_s, send_s, keep, send)
    move.drain()


def mid_kernel(count, place, *refs):
    ins, x, vec = refs[:count], refs[count], refs[count + 1]
    y_out, h_out = refs[count + 2 : count + 4]
    held = refs[count + 4 : 2 * count + 4]
    x_s, vec_s, y_s, h_s, sems = refs[2 * count + 4 :]
    move = Mover(sems)
    loads = [move.start(a, b) for a, b in zip(ins, held)]
    loads += [move.start(x, x_s), move.start(vec, vec_s)]
    for copy in loads:
        copy.wait()
    y = held[0][...]
    for i in range(1, count):
        y = y + held[i][...].astype(f32)
    y = x_s[...].astype(f32) + y + vec_s[4:5, :]
    y_s[...] = y
    scaled, _ = normalize(y)
    h_s[...] = (scaled * vec_s[5:6, :] + vec_s[6:7, :]).astype(bf16)
    move.put(h_s, h_out)
    move.put(y_s, y_out)
    move.drain()


def down_back_kernel(n, groups, place, *refs):
    dys, ws = refs[:n], refs[n : n + groups]
    dy_out, dg_out, w_up_out, w_down_out, dy_s, dg_s, w_up, w_down, sems = refs[n + groups :]
    move = Mover(sems)
    j, g = place.j, place.group
    rows = dys[0].shape[0]
    chunk = w_down.shape[0] // groups
    mine = w_up.shape[1]
    feats = w_up.shape[0] // groups
    first, last = [], []
    for i in range(groups):
        for c in range(w_down.shape[1] // mine):
            source = ws[i].at[feats + c * chunk : feats + (c + 1) * chunk, :]
            first.append(move.start(source, w_down.at[rows_at(g ^ i, chunk), c * mine : (c + 1) * mine]))
    copies = [move.start(dys[r], dy_s.at[rows_at(j ^ r, rows), :]) for r in range(n)]
    for i in range(groups):
        last.append(move.start(ws[i].at[:feats, :], w_up.at[rows_at(g ^ i, feats), :]))
    for copy in first:
        copy.wait()
    move.put(w_down, w_down_out)
    for copy in copies:
        copy.wait()
    block = min(512, dy_s.shape[0])
    for i in range(dy_s.shape[0] // block):
        at = slice(i * block, (i + 1) * block)
        dg_s[at, :] = dot(dy_s[at, :], w_down[...], NT)
        move.put(dg_s.at[at, :], dg_out.at[at, :])
    for copy in last:
        copy.wait()
    move.put(w_up, w_up_out)
    move.put(dy_s, dy_out)
    move.drain()


def ffn_kernel(n, place, *refs):
    hs = refs[:n]
    w_up_in, b_up_in, dg_in = refs[n : n + 3]
    h_out, g_out, du_out, keep, send, db_out = refs[n + 3 : n + 9]
    w_up, b_up, dg, h_s, g_s, du_s, dh_s, send_s, db, sems = refs[n + 9 :]
    move = Mover(sems)
    rows = hs[0].shape[0]
    total = n * rows
    copies = [move.start(hs[r], h_s.at[rows_at(place.j ^ r, rows), :]) for r in range(n)]
    copies += [move.start(w_up_in, w_up), move.start(b_up_in, b_up)]
    late = move.start(dg_in, dg)
    for copy in copies:
        copy.wait()
    block = min(512, total)
    sums = jnp.zeros(db.shape, f32)
    for i in range(total // block):
        at = slice(i * block, (i + 1) * block)
        u = dot(h_s[at, :], w_up[...]) + b_up[...]
        cdf = 0.5 * (1.0 + lax.erf(u * inv_root_two))
        g_s[at, :] = (u * cdf).astype(bf16)
        slope = cdf + u * jnp.exp(-0.5 * u * u) * inv_root_tau
        if i == 0:
            late.wait()
        du = (dg[at, :] * slope).astype(bf16)
        du_s[at, :] = du
        sums = sums + jnp.sum(du.astype(f32), axis=0, keepdims=True)
        dh_s[at, :] = dot(du, w_up[...], NT)
    db[...] = sums
    send_rows(move, place, n, rows, dh_s, send_s, keep, send)
    move.put(h_s, h_out)
    move.put(g_s, g_out)
    move.put(du_s, du_out)
    move.put(db, db_out)
    move.drain()


def down_kernel(n, place, g_in, w_in, keep, send, g, w, out_s, send_s, sems):
    move = Mover(sems)
    for copy in [move.start(w_in, w), move.start(g_in, g)]:
        copy.wait()
    total = g.shape[0]
    block = min(512, total)
    for i in range(total // block):
        at = slice(i * block, (i + 1) * block)
        out_s[at, :] = dot(g[at, :], w[...])
    send_rows(move, place, n, total // n, out_s, send_s, keep, send)
    move.drain()


def ffn_grads_kernel(groups, place, h_in, du_in, dy_in, g_in, *refs):
    outs = refs[:groups]
    h, du, dy, g, grads, stage, sems = refs[groups:]
    move = Mover(sems)
    loads = [move.start(a, b) for a, b in ((h_in, h), (du_in, du), (dy_in, dy), (g_in, g))]
    feats = h.shape[1] // groups
    mine = du.shape[1]
    chunk = mine // groups
    loads[0].wait()
    loads[1].wait()
    for i in range(groups):
        grads[i, :feats, :] = dot(h[:, i * feats : (i + 1) * feats], du[...], TN)
    loads[2].wait()
    loads[3].wait()
    for c in range(dy.shape[1] // mine):
        part = dot(g[...], dy[:, c * mine : (c + 1) * mine], TN)
        for i in range(groups):
            grads[i, feats + c * chunk : feats + (c + 1) * chunk, :] = part[i * chunk : (i + 1) * chunk, :]
    for i in range(1, groups):
        stage[i - 1] = grads[place.group ^ i].astype(bf16)
        move.put(stage.at[i - 1], outs[i])
    move.put(grads.at[place.group], outs[0])
    move.drain()


def pair_kernel(place, keep, recv, *refs):
    count = (len(refs) - 3) // 2
    outs = refs[:count]
    keep_s, recv_s = refs[count : count + 2]
    stage, sems = refs[count + 2 : 2 * count + 2], refs[2 * count + 2]
    move = Mover(sems)
    rows = outs[0].shape[0]
    order = list(range(1, count)) + [0]
    loads = {}
    for i in order:
        here = slice(i * rows, (i + 1) * rows)
        loads[i] = (
            move.start(keep.at[here, :], keep_s.at[here, :]),
            move.start(recv.at[here, :], recv_s.at[here, :]),
        )
    for i in order:
        here = slice(i * rows, (i + 1) * rows)
        for copy in loads[i]:
            copy.wait()
        stage[i][...] = (keep_s[here, :].astype(f32) + recv_s[here, :].astype(f32)).astype(outs[i].dtype)
        move.put(stage[i], outs[i])
    move.drain()


def fold_kernel(count, place, *refs):
    ins, outs = refs[: 2 * count], refs[2 * count : 3 * count]
    held, stage, sems = refs[3 * count : 5 * count], refs[5 * count : 6 * count], refs[6 * count]
    move = Mover(sems)
    loads = [move.start(a, b) for a, b in zip(ins, held)]
    for i in range(count):
        loads[i].wait()
        loads[count + i].wait()
        stage[i][...] = (held[i][...].astype(f32) + held[count + i][...].astype(f32)).astype(bf16)
        move.put(stage[i], outs[i])
    move.drain()


def out_kernel(count, place, *refs):
    ins = refs[: count + 2]
    kept, sent = refs[count + 2 : count + 4]
    held = refs[count + 4 : 2 * count + 6]
    out_s, sems = refs[2 * count + 6 :]
    move = Mover(sems)
    for copy in [move.start(a, b) for a, b in zip(ins, held)]:
        copy.wait()
    total = held[0][...] + held[count][...]
    for i in range(1, count):
        total = total + held[i][...].astype(f32)
    out_s[...] = (total + held[count + 1][7:8, :]).astype(bf16)
    half = kept.shape[0]
    move.put(out_s.at[half:, :], sent)
    move.put(out_s.at[:half, :], kept)
    move.drain()


def mid_back_kernel(count, place, *refs):
    ins = refs[: count + 3]
    dy1_out, da_out, small_out = refs[count + 3 : count + 6]
    held = refs[count + 6 : 2 * count + 9]
    dy1_s, da_s, small, sems = refs[2 * count + 9 :]
    move = Mover(sems)
    for copy in [move.start(a, b) for a, b in zip(ins, held)]:
        copy.wait()
    dh = held[0][...]
    for i in range(1, count):
        dh = dh + held[i][...].astype(f32)
    y, vec, dy = held[count : count + 3]
    scaled, inv_std = normalize(y[...])
    dyf = dy[...].astype(f32)
    dy1 = dyf + norm_back(dh, scaled, inv_std, vec[5:6, :])
    da = dy1.astype(bf16)
    da_s[...] = da
    move.put(da_s, da_out)
    dy1_s[...] = dy1
    move.put(dy1_s, dy1_out)
    small[0:1, :] = jnp.sum(dh * scaled, axis=0, keepdims=True)
    small[1:2, :] = jnp.sum(dh, axis=0, keepdims=True)
    small[2:3, :] = jnp.sum(da.astype(f32), axis=0, keepdims=True)
    small[3:4, :] = jnp.sum(dyf, axis=0, keepdims=True)
    move.put(small, small_out)
    move.drain()


def attend_back_kernel(n, half, qb, place, *refs):
    das, ins = refs[:n], refs[n : n + 4]
    dqkv_out, keep, send, db_out, da_out = refs[n + 4 : n + 9]
    da, qkv, lse, wo, w, dqkv, dh_s, send_s, db, do, bias, acc_k, acc_v, sems = refs[n + 9 :]
    rows = 2 * half
    move = Mover(sems)
    copies = [move.start(das[r], da.at[rows_at(place.j ^ r, rows), :]) for r in range(n)]
    loads = [move.start(a, b) for a, b in zip(ins, (wo, qkv, lse, w))]
    total = qkv.shape[0]
    hd = do.shape[1]
    heads = hd // HEAD
    bias[...] = jnp.where(key_mask(place, total, n, half, 128), 0.0, -1.0).astype(f32)
    loads[0].wait()
    for copy in copies:
        copy.wait()
    move.put(da, da_out)
    block = min(512, total)
    for i in range(total // block):
        at = slice(i * block, (i + 1) * block)
        do[at, :] = dot(da[at, :], wo[...], NT).astype(bf16)
    for copy in loads[1:]:
        copy.wait()
    for head in range(heads):
        cols = slice(head * HEAD, (head + 1) * HEAD)
        kh = qkv[:, hd + head * HEAD : hd + (head + 1) * HEAD]
        vh = qkv[:, 2 * hd + head * HEAD : 2 * hd + (head + 1) * HEAD]
        kt = kh.astype(f32).T.astype(bf16)
        acc_k[...] = jnp.zeros_like(acc_k)
        acc_v[...] = jnp.zeros_like(acc_v)

        def step(i, _, cols=cols, kh=kh, vh=vh, kt=kt, head=head):
            at = rows_at(i, qb)
            qh = qkv[at, cols]
            doh = do[at, cols]
            scores = dot(kh, qh, NT)
            probs = jnp.where(bias[:, 0:1] >= 0.0, jnp.exp(scores - lse[head : head + 1, at]), 0.0)
            dp = dot(vh, doh, NT)
            centre = jnp.sum(probs * dp, axis=0, keepdims=True)
            ds = (probs * (dp - centre)).astype(bf16)
            acc_v[...] += dot(probs.astype(bf16), doh)
            acc_k[...] += dot(ds, qh)
            dq = dot(kt, ds)
            dqkv[at, cols] = (dq.T.astype(bf16).astype(f32) * 0.125).astype(bf16)
            return 0

        lax.fori_loop(0, total // qb, step, 0)
        dqkv[:, hd + head * HEAD : hd + (head + 1) * HEAD] = acc_k[...].astype(bf16)
        dqkv[:, 2 * hd + head * HEAD : 2 * hd + (head + 1) * HEAD] = acc_v[...].astype(bf16)
    move.put(dqkv, dqkv_out)
    sums = jnp.zeros(db.shape, f32)
    for i in range(total // block):
        at = slice(i * block, (i + 1) * block)
        grads = dqkv[at, :]
        sums = sums + jnp.sum(grads.astype(f32), axis=0, keepdims=True)
        dh_s[at, :] = dot(grads, w[...], NT)
    db[...] = sums
    send_rows(move, place, n, rows, dh_s, send_s, keep, send)
    move.put(db, db_out)
    move.drain()


def attn_grads_kernel(n, dp_size, groups, first_row, place, *refs):
    ins, outs = refs[:7], refs[7 : 7 + dp_size]
    dqkv, h, w, hat, two, db, up, small, grads, packed_s, sems = refs[7 + dp_size :]
    move = Mover(sems)
    j = place.j
    loads = [move.start(a, b) for a, b in zip(ins, (dqkv, h, w, hat, two, db, up))]
    ndev = packed_s.shape[0]
    hd = dqkv.shape[1] // 3
    rs = h.shape[1] // ndev
    chunk = up.shape[1] // groups
    loads[0].wait()
    loads[1].wait()
    grads[...] = dot(h[...], dqkv[...], TN).astype(bf16)
    for copy in loads[2:]:
        copy.wait()
    small[...] = jnp.zeros_like(small)
    step_rows = min(512, hat.shape[0])

    def step(i, _):
        at = rows_at(i, step_rows)
        dh = dot(dqkv[at, :], w[...], NT)
        small[0:1, :] += jnp.sum(dh * hat[at, :].astype(f32), axis=0, keepdims=True)
        small[1:2, :] += jnp.sum(dh, axis=0, keepdims=True)
        return 0

    lax.fori_loop(0, hat.shape[0] // step_rows, step, 0)
    small[4:8, :] = two[...]
    zeros = jnp.zeros((packed_s.shape[1] - rs, packed_s.shape[2]), bf16)
    for d in range(ndev):
        packed_s[d, rs:, :] = zeros
        packed_s[d, :rs, :] = grads[d * rs : (d + 1) * rs, :]
        packed_s[d, first_row : first_row + 8, :rs] = small[:, d * rs : (d + 1) * rs].astype(bf16)
    for t in range(groups):
        cols = slice(t * rs, (t + 1) * rs)
        at = j * groups + t
        packed_s[at, first_row + 2 : first_row + 3, :rs] = db[:, :hd][:, cols].astype(bf16)
        packed_s[at, first_row + 3 : first_row + 4, :rs] = db[:, 2 * hd :][:, cols].astype(bf16)
        packed_s[t * n + j, first_row : first_row + 1, hd : hd + chunk] = up[
            :, t * chunk : (t + 1) * chunk
        ].astype(bf16)
    seq_size = ndev // dp_size
    for i in list(range(1, dp_size)) + [0]:
        move.put(packed_s.at[pl.ds((place.dp ^ i) * seq_size, seq_size)], outs[i])
    move.drain()


def out_grads_kernel(dp_size, groups, place, da_in, o_in, *refs):
    outs = refs[:dp_size]
    da, o, grads, stage, sems = refs[dp_size:]
    move = Mover(sems)
    for copy in [move.start(o_in, o), move.start(da_in, da)]:
        copy.wait()
    all_rows = dot(o[...], da[...], TN)
    rs = grads.shape[1]
    for t in range(groups):
        grads[t] = all_rows[t * rs : (t + 1) * rs, :]
    slots = groups // dp_size
    for k in range(dp_size):
        for i in range(slots):
            stage[k, i] = grads[(place.dp ^ k) * slots + (place.h ^ i)].astype(bf16)
        move.put(stage.at[k], outs[k])
    move.drain()


def last_kernel(count, place, *refs):
    ins, rider = refs[: count + 3], refs[count + 3]
    kept, sent = refs[count + 4 : count + 6]
    held = refs[count + 6 : 2 * count + 9]
    out_s, sems = refs[2 * count + 9 :]
    move = Mover(sems)
    half = kept.shape[0]
    move.put(rider.at[1], sent.at[half:, :])
    for copy in [move.start(a, b) for a, b in zip(ins, held)]:
        copy.wait()
    x, dy1, vec = held[count:]
    dh = held[0][...]
    for i in range(1, count):
        dh = dh + held[i][...].astype(f32)
    scaled, inv_std = normalize(x[...].astype(f32))
    out_s[...] = (dy1[...] + norm_back(dh, scaled, inv_std, vec[0:1, :])).astype(bf16)
    move.put(out_s.at[half:, :], sent.at[:half, :])
    move.put(out_s.at[:half, :], kept)
    move.drain()


def ffn_sum_kernel(count, place, *refs):
    ins, (up_out, down_out) = refs[:count], refs[count : count + 2]
    held, (total, up_s, down_s, sems) = refs[count + 2 : 2 * count + 2], refs[2 * count + 2 :]
    move = Mover(sems)
    for copy in [move.start(a, b) for a, b in zip(ins, held)]:
        copy.wait()
    ffn = held[0][...].astype(f32)
    for piece in held[1:]:
        ffn = ffn + piece[...].astype(f32)
    total[...] = ffn
    n, rs, mine = up_s.shape
    chunk, width = down_s.shape
    for m in range(n):
        up_s[m] = total[m * rs : (m + 1) * rs, :].astype(bf16)
    move.put(up_s, up_out)
    feats = n * rs
    for c in range(width // mine):
        down_s[:, c * mine : (c + 1) * mine] = total[feats + c * chunk : feats + (c + 1) * chunk, :]
    move.put(down_s, down_out)
    move.drain()


def unpack_kernel(n, groups, first_row, place, *refs):
    back, up_back, out_w = refs[:3]
    halves = refs[3:7]
    output, frames_grad, out_w_grad, up, wq, wk, wv = refs[7:14]
    vectors = refs[14:23]
    back_s, up_back_s, in_s, out_s, up_s, q_s, k_s, v_s = refs[23:31]
    vectors_s, sems = refs[31:40], refs[40]
    move = Mover(sems)
    load, more, third = move.start(back, back_s), move.start(up_back, up_back_s), move.start(out_w, in_s)
    half = output.shape[1]
    for i, target in enumerate((output, frames_grad)):
        move.put(halves[2 * i], target.at[place.h])
        move.put(halves[2 * i + 1].at[:half, :], target.at[1 - place.h])
    third.wait()
    out_s[...] = in_s[...].astype(f32)
    move.put(out_s, out_w_grad)
    rs = wq.shape[0]
    hd = wq.shape[1] // n
    chunk = up.shape[1] // (n * groups)
    more.wait()
    for m in range(n):
        for g in range(groups):
            at = (g * n + m) * chunk
            up_s[:, at : at + chunk] = up_back_s[m, :, g * chunk : (g + 1) * chunk].astype(f32)
    move.put(up_s, up)
    load.wait()
    sums = jnp.zeros((8, 3 * hd), f32)
    for m in range(n):
        cols = slice(m * hd, (m + 1) * hd)
        total = back_s[m].astype(f32)
        for i in range(m + n, back_s.shape[0], n):
            total = total + back_s[i].astype(f32)
        for i, target in enumerate((q_s, k_s, v_s)):
            target[:, cols] = total[:rs, i * hd : (i + 1) * hd]
        sums = sums + total[first_row:, :]
    for a, b in ((q_s, wq), (k_s, wk), (v_s, wv)):
        move.put(a, b)
    for i in range(8):
        vectors_s[i][...] = sums[i : i + 1, :rs]
    vectors_s[8][...] = sums[0:1, hd : hd + chunk]
    for a, b in zip(vectors_s, vectors):
        move.put(a, b)
    move.drain()


def on_device(
    dp_size,
    seq_size,
    frames,
    out_grad,
    order,
    lengths,
    first_gain,
    first_shift,
    query_weight,
    query_bias,
    key_weight,
    value_weight,
    value_bias,
    output_weight,
    output_bias,
    second_gain,
    second_shift,
    up_weight,
    up_bias,
    down_weight,
    down_bias,
):
    slots, half, width = frames.shape
    n = seq_size // slots
    groups = dp_size * slots
    ndev = dp_size * seq_size
    hd = width // n
    heads = hd // HEAD
    rs = query_weight.shape[0]
    hidden = up_weight.shape[1]
    chunk = hidden // ndev
    mine = hidden // n
    parts = width // mine
    feats = n * rs
    rows = 2 * half
    total = n * rows
    qb = 512
    count = n // 2
    both = ("dp", "seq")
    first_row = -(-rs // 8) * 8
    block_rows = first_row + 8

    scale = -(-total // 1024)
    grid = (slots, n, scale)

    def xor(value, bit):
        return lax.ppermute(value, "seq", [(i, i ^ bit) for i in range(seq_size)])

    def gather_direct(value):
        got = [xor(value, r) for r in range(n - 2, 0, -2)]
        return [value] + got[::-1]

    def gather_pair(even):
        out = []
        for piece in even:
            out += [piece, xor(piece, 1)]
        return out

    def pair(keep, recv):
        outs = [sds((rows, width), f32)] + [sds((rows, width), bf16)] * (count - 1)
        return call(
        grid,
            pair_kernel,
            [keep, Near(recv)],
            near(outs),
            "pair",
            cost(1),
            scratch=[vmem(keep), vmem(recv)] + [vmem(o) for o in outs],
            sems=3 * count,
        )

    def scatter(pieces):
        return [pieces[0]] + [xor(pieces[i], 2 * i) for i in range(count - 1, 0, -1)][::-1]

    def to_group(value, i):
        pairs = []
        for d in range(ndev):
            dp_of, seq_of = d // seq_size, d % seq_size
            g_of = (dp_of * slots + seq_of // n) ^ i
            pairs.append((d, g_of // slots * seq_size + g_of % slots * n + seq_of % n))
        return lax.ppermute(value, both, pairs)

    def members(value):
        index = [[s * n + i for i in range(n)] for s in range(slots)]
        return lax.all_to_all(value, "seq", 0, 0, tiled=True, axis_index_groups=index)

    def fold(kept, got):
        outs = [sds(a.shape, bf16) for a in kept]
        return call(
            grid,
            functools.partial(fold_kernel, len(kept)),
            near(list(kept) + list(got)),
            near(outs),
            "fold",
            cost(2),
            scratch=[vmem(a) for a in list(kept) + list(got) + outs],
            sems=3 * len(kept),
        )

    def spread(pieces):
        bit = len(pieces)
        while bit < groups:
            pieces = pieces + [to_group(piece, bit) for piece in pieces]
            bit *= 2
        return pieces

    def to_dp(value, i):
        return lax.ppermute(value, "dp", [(d, d ^ i) for d in range(dp_size)])

    def owner_pairs(k):
        pairs = []
        for d in range(ndev):
            g_of = (d % groups) ^ (k * slots)
            pairs.append((d, g_of // slots * seq_size + g_of % slots * n + d // groups))
        return pairs

    owners = owner_pairs(0)
    out_w = jnp.stack([lax.ppermute(output_weight, both, owner_pairs(k)) for k in range(dp_size)])

    small_in = [first_gain, first_shift, query_bias, value_bias, output_bias, second_gain, second_shift, down_bias]
    small_in = [v.reshape(1, -1) for v in small_in + [up_bias]]
    weights_in = [query_weight, key_weight, value_weight]
    half_sds, row_sds = sds((half, width), bf16), sds((rows, width), bf16)
    packed_sds, up_sds = sds((seq_size, block_rows, 3 * hd), bf16), sds((n, rs, mine), bf16)
    x_own, x_send, dy_own, dy_send = call(
        grid, rows_kernel, [frames, out_grad], near([half_sds] * 4), "rows", cost(1), sems=4
    )
    x_recv = xor(x_send, n)
    (packed,) = call(
        grid,
        functools.partial(pack_kernel, n, slots, groups, first_row),
        [after(weights_in[0], x_send)] + weights_in[1:] + small_in,
        near([packed_sds]),
        "pack",
        cost(2),
        scratch=[vmem(w) for w in weights_in] + [vmem(v) for v in small_in] + [pltpu.VMEM((n, block_rows, 3 * hd), bf16)],
        sems=12 + slots,
    )
    (up_packed,) = call(
        grid,
        functools.partial(pack_up_kernel, n, groups),
        [up_weight],
        near([up_sds]),
        "pack_up",
        cost(1),
        scratch=[vmem(up_weight), vmem(up_sds)],
        sems=2,
    )
    attn_w = lax.all_to_all(packed, "seq", 0, 0, tiled=True)
    up_mine = members(after(up_packed, attn_w))
    x = jnp.concatenate([x_own, x_recv])
    x_even = gather_direct(x)
    wos = [out_w, xor(out_w, n)]
    dy_recv = xor(after(dy_send, attn_w), n)
    attn_ws = [attn_w]
    while len(attn_ws) < dp_size:
        attn_ws += [to_dp(piece, len(attn_ws)) for piece in attn_ws]
    ffn_sds = sds((feats + parts * chunk, mine), bf16)
    (ffn_w,) = call(
        grid,
        functools.partial(join_kernel, n),
        near([up_mine.reshape(feats, mine), down_weight]),
        near([ffn_sds]),
        "join",
        cost(1),
        sems=1 + parts,
    )
    ffn_half = to_group(after(ffn_w, attn_w), 1)
    xs = gather_pair([after(piece, attn_ws[-1], wos[-1]) for piece in x_even])
    dy = jnp.concatenate([dy_own, dy_recv])

    ffn_go, dy_go, xs, attn_ws, wos = lax.optimization_barrier((ffn_w, dy, tuple(xs), tuple(attn_ws), tuple(wos)))
    xs, attn_ws, wos = list(xs), list(attn_ws), list(wos)
    ffn_ws = [ffn_w, ffn_half, to_group(ffn_go, 2)]
    dy_even = gather_direct(dy_go)
    x_sds = sds((total, width), bf16)
    keep_sds = send_sds = sds((total // 2, width), bf16)
    s_half = pltpu.VMEM((2, total // 2, width), bf16)
    outs = [
        x_sds,
        x_sds,
        sds((total, 3 * hd), bf16),
        sds((total, hd), bf16),
        sds((heads, total), f32),
        sds((width, 3 * hd), bf16),
        sds((8, width), f32),
        sds((1, mine), f32),
        sds((hd, width), bf16),
        keep_sds,
        send_sds,
    ]
    s_hat, s_h, s_qkv, s_o, s_lse, s_w, s_vec, s_bias, s_wo, _, _ = [vmem(o) for o in outs]
    s_rows = pltpu.VMEM((total, width), f32)
    s_got = pltpu.VMEM((ndev, block_rows, 3 * hd), bf16)
    s_wo3 = pltpu.VMEM((groups, rs, width), bf16)
    hat, h_first, qkv, o_heads, lse, w_qkv, vec, bias_up, wo, keep, send = call(
        grid,
        functools.partial(first_kernel, n, dp_size, groups, half, qb, first_row),
        near(xs + attn_ws + wos),
        outs[:-1] + near(outs[-1:]),
        "first",
        cost(17),
        scratch=[vmem(x_sds), s_hat, s_h, s_qkv, s_o, s_lse, s_got, s_w, s_vec, s_bias, s_wo3, s_wo, s_rows, s_half]
        + [pltpu.VMEM((total, 128), f32)],
        sems=3 * n + groups + dp_size + 10,
        lengths=(order, lengths),
        limit=48,
    )
    send = after(send, *ffn_ws[1:], *dy_even[1:])

    y_sds = sds((rows, width), f32)
    y_pieces = pair(keep, xor(send, 1))
    ys = scatter(y_pieces)
    dys = gather_pair([dy_even[0]] + [after(piece, y_pieces[0]) for piece in dy_even[1:]])
    ffn_ws = spread(ffn_ws + [to_group(after(ffn_ws[1], y_pieces[0]), 2)])
    y1, h2 = call(
        grid,
        functools.partial(mid_kernel, count),
        near(ys + [x]) + [vec],
        [y_sds, Near(row_sds)],
        "mid",
        cost(2),
        scratch=[vmem(a) for a in ys + [row_sds, vec, y_sds, row_sds]],
        sems=count + 4,
    )
    h2_even = gather_direct(h2)

    outs = [x_sds, sds((total, mine), f32), sds((width, mine), bf16), sds((mine, width), bf16)]
    dy_all, dg, w_up, w_down = call(
        grid,
        functools.partial(down_back_kernel, n, groups),
        near(dys + ffn_ws),
        outs,
        "down_back",
        cost(5),
        scratch=[vmem(o) for o in outs],
        sems=2 * n + groups * (parts + 1) + 3,
        limit=14 * scale,
    )
    h2s = gather_pair(h2_even[:1] + [after(piece, dg) for piece in h2_even[1:]])

    act_sds = sds((total, mine), bf16)
    outs = [x_sds, act_sds, act_sds, keep_sds, send_sds, sds((1, mine), f32)]
    h2_all, g, du, keep, send, d_bias_up = call(
        grid,
        functools.partial(ffn_kernel, n),
        near(h2s) + [w_up, bias_up, dg],
        outs[:4] + near(outs[4:5]) + outs[5:],
        "ffn",
        cost(9),
        scratch=[vmem(a) for a in [w_up, bias_up, dg] + outs[:3]] + [s_rows, s_half, vmem(outs[5])],
        sems=3 * n + 7,
        limit=28 * scale,
    )
    dh2 = scatter(pair(keep, xor(send, 1)))

    g_then = after(g, dh2[0])
    out_keep, out_send = call(
        grid,
        functools.partial(down_kernel, n),
        [g_then, w_down],
        [keep_sds, Near(send_sds)],
        "down",
        cost(4),
        scratch=[vmem(g), vmem(w_down), s_rows, s_half],
        sems=n + 2,
        limit=16 * scale,
    )
    ffn_parts = call(
        grid,
        functools.partial(ffn_grads_kernel, groups),
        [h2_all, du, dy_all, g_then],
        [sds(ffn_sds.shape, f32)] + near([ffn_sds] * (groups - 1)),
        "ffn_grads",
        cost(0),
        scratch=[vmem(a) for a in (x_sds, act_sds, x_sds, act_sds)]
        + [pltpu.VMEM((groups,) + ffn_sds.shape, f32), pltpu.VMEM((groups - 1,) + ffn_sds.shape, bf16)],
        sems=4 + groups,
        limit=20 * scale,
    )

    small_sds = sds((4, width), f32)
    outs = [y_sds, row_sds, small_sds]
    dy1, da, small_two = call(
        grid,
        functools.partial(mid_back_kernel, count),
        near(dh2) + [after(y1, ffn_parts[0], out_keep), vec, Near(dy)],
        outs[:1] + near(outs[1:2]) + outs[2:],
        "mid_back",
        cost(3),
        scratch=[vmem(a) for a in dh2 + [y1, vec, row_sds] + outs],
        sems=count + 6,
    )
    da_even = gather_direct(da)
    bit = groups // 2
    while bit > 2:
        ffn_parts = fold(ffn_parts[:bit], [to_group(piece, bit) for piece in ffn_parts[bit:]])
        bit //= 2
    ffn_got = [to_group(piece, 2) for piece in ffn_parts[2:4]]
    out_kept = pair(out_keep, xor(after(out_send, da), 1))
    (ffn_next,) = fold([after(ffn_parts[1], out_kept[0])], ffn_got[1:])
    das = gather_pair([da_even[0]] + [after(piece, ffn_next) for piece in da_even[1:]])

    out_kept, das, ffn_next = lax.optimization_barrier((tuple(out_kept), tuple(das), ffn_next))
    out_kept, das = list(out_kept), list(das)
    ffn_got = [ffn_got[0], to_group(ffn_next, 1)]
    out_pieces = scatter(out_kept)
    ins = [wo, qkv, lse, w_qkv]
    outs = [sds((total, 3 * hd), bf16), keep_sds, send_sds, sds((1, 3 * hd), f32), x_sds]
    d_qkv, keep, send, d_bias_qkv, da_all = call(
        grid,
        functools.partial(attend_back_kernel, n, half, qb),
        near(das) + ins,
        outs[:2] + near(outs[2:3]) + outs[3:],
        "attend_back",
        cost(0),
        scratch=[vmem(x_sds)]
        + [vmem(a) for a in (qkv, lse, wo, w_qkv, outs[0])]
        + [s_rows, s_half, vmem(outs[3]), pltpu.VMEM((total, hd), bf16), pltpu.VMEM((total, 128), f32)]
        + [pltpu.VMEM((total, HEAD), f32)] * 2,
        sems=2 * n + 9,
        lengths=(order, lengths),
        limit=48,
    )
    recv = xor(after(send, *out_pieces[1:], *ffn_got), 1)

    ins = [d_qkv, h_first, w_qkv, hat, small_two, d_bias_qkv, d_bias_up]
    attn_parts = call(
        grid,
        functools.partial(attn_grads_kernel, n, dp_size, groups, first_row),
        ins,
        near([packed_sds] * dp_size),
        "attn_grads",
        cost(6),
        scratch=[vmem(a) for a in ins]
        + [
            pltpu.VMEM((8, width), f32),
            pltpu.VMEM((width, 3 * hd), bf16),
            pltpu.VMEM((ndev, block_rows, 3 * hd), bf16),
        ],
        sems=7 + dp_size,
        limit=20 * scale,
    )
    dh1_pieces = pair(after(keep, attn_parts[0]), recv)
    dh1 = scatter(dh1_pieces)
    bit = dp_size // 2
    while bit > 1:
        attn_parts = fold(attn_parts[:bit], [to_dp(piece, bit) for piece in attn_parts[bit:]])
        bit //= 2
    attn_got = to_dp(attn_parts[1], 1)

    ffn_sums = [after(ffn_parts[0], dh1_pieces[0])] + ffn_got
    down_sds = sds((chunk, width), f32)
    up_back, down_weight_grad = call(
        grid,
        functools.partial(ffn_sum_kernel, 3),
        ffn_sums[:1] + near(ffn_sums[1:]),
        [Near(up_sds), down_sds],
        "ffn_sum",
        cost(2),
        scratch=[vmem(a) for a in ffn_sums] + [pltpu.VMEM(ffn_sds.shape, f32), vmem(up_sds), vmem(down_sds)],
        sems=5,
    )
    up_back = members(up_back)
    out_parts = call(
        grid,
        functools.partial(out_grads_kernel, dp_size, groups),
        [da_all, after(o_heads, dh1_pieces[0])],
        near([sds((slots, rs, width), bf16)] * dp_size),
        "out_grads",
        cost(2),
        scratch=[
            vmem(x_sds),
            vmem(o_heads),
            pltpu.VMEM((groups, rs, width), f32),
            pltpu.VMEM((dp_size, slots, rs, width), bf16),
        ],
        sems=2 + dp_size,
        limit=10 * scale,
    )
    bit = dp_size // 2
    while bit > 1:
        out_parts = fold(out_parts[:bit], [to_dp(piece, bit) for piece in out_parts[bit:]])
        bit //= 2

    (attn_sum,) = fold([after(attn_parts[0], up_back)], [attn_got])
    back = lax.all_to_all(attn_sum, "seq", 0, 0, tiled=True)
    (out_w_sum,) = fold([after(out_parts[0], attn_sum)], [to_dp(out_parts[1], 1)])

    ins = out_pieces + [y1, vec]
    out_own, out_sent = call(
        grid,
        functools.partial(out_kernel, count),
        near([after(ins[0], attn_sum)] + ins[1:count]) + ins[count:],
        near([half_sds] * 2),
        "out",
        cost(2),
        scratch=[vmem(a) for a in ins + [row_sds]],
        sems=len(ins) + 2,
    )
    out_other = xor(out_sent, n)

    ins = dh1 + [x, after(dy1, attn_sum), vec]
    kept, sent = call(
        grid,
        functools.partial(last_kernel, count),
        near(ins[: count + 1]) + ins[count + 1 :] + near([out_w_sum]),
        near([half_sds, sds((half + rs, width), bf16)]),
        "last",
        cost(2),
        scratch=[vmem(a) for a in ins + [row_sds]],
        sems=len(ins) + 3,
    )
    other = xor(sent, n)
    out_w = (out_w_sum[0].astype(f32) + other[half:].astype(f32)).astype(bf16)
    out_w = lax.ppermute(out_w, both, [(b, a) for a, b in owners])
    frames_sds = sds(frames.shape, bf16)
    weight_sds = sds((rs, width), f32)
    outs = [weight_sds, sds((rs, hidden), f32)] + [weight_sds] * 3
    vectors = [sds((1, rs), f32)] * 8 + [sds((1, chunk), f32)]
    output, frames_grad, output_weight_grad, up_weight_grad, d_query, d_key, d_value, *vectors = call(
        grid,
        functools.partial(unpack_kernel, n, groups, first_row),
        near([back, up_back, out_w, out_own, out_other, kept, other]),
        [frames_sds] * 2 + outs + vectors,
        "unpack",
        cost(2),
        scratch=[vmem(a) for a in [back, up_back, out_w] + outs + vectors],
        sems=24,
    )
    vectors = [v.reshape(-1) for v in vectors]
    return (
        output,
        frames_grad,
        vectors[0],
        vectors[1],
        d_query,
        vectors[2],
        d_key,
        d_value,
        vectors[3],
        output_weight_grad,
        vectors[6],
        vectors[4],
        vectors[5],
        up_weight_grad,
        vectors[8],
        down_weight_grad,
        vectors[7],
    )


def solution(mesh):
    vector = P(("dp", "seq"))
    matrix = P(("dp", "seq"), None)
    rows = P("dp", "seq", None)
    return jax.shard_map(
        functools.partial(on_device, mesh.shape["dp"], mesh.shape["seq"]),
        mesh=mesh,
        in_specs=(
            rows,
            rows,
            P("dp"),
            P(),
            vector,
            vector,
            matrix,
            vector,
            matrix,
            matrix,
            vector,
            matrix,
            vector,
            vector,
            vector,
            matrix,
            vector,
            matrix,
            vector,
        ),
        out_specs=(
            rows,
            rows,
            vector,
            vector,
            matrix,
            vector,
            matrix,
            matrix,
            vector,
            matrix,
            vector,
            vector,
            vector,
            matrix,
            vector,
            matrix,
            vector,
        ),
        check_vma=False,
    )
```

```python
import functools

import jax
import jax.numpy as jnp
from jax import lax
from jax.experimental import pallas as pl
from jax.experimental.pallas import tpu as pltpu
from jax.sharding import PartitionSpec as P

HEAD = 64
f32 = jnp.float32
bf16 = jnp.bfloat16
norm_eps = 1e-05
inv_root_two = 0.7071067811865476
inv_root_tau = 0.3989422804014327
NN = (((1,), (0,)), ((), ()))
NT = (((1,), (1,)), ((), ()))
TN = (((0,), (0,)), ((), ()))
MIB = 1024 * 1024


def dot(a, b, dims=NN):
    return lax.dot_general(a, b, dims, preferred_element_type=f32)


def normalize(rows):
    average = jnp.mean(rows, axis=-1, keepdims=True)
    centered = rows - average
    inv_std = lax.rsqrt(jnp.mean(centered * centered, axis=-1, keepdims=True) + norm_eps)
    return centered * inv_std, inv_std


def norm_back(grad_rows, scaled, inv_std, gain):
    grad_hat = grad_rows * gain
    return inv_std * (
        grad_hat
        - jnp.mean(grad_hat, axis=-1, keepdims=True)
        - scaled * jnp.mean(grad_hat * scaled, axis=-1, keepdims=True)
    )


def sds(shape, dtype):
    return jax.ShapeDtypeStruct(shape, dtype)


def vmem(like):
    return pltpu.VMEM(like.shape, like.dtype)


class Near:
    def __init__(self, array):
        self.array = array
        self.shape, self.dtype = array.shape, array.dtype


class Held(Near):
    pass


def near(arrays):
    return [Near(a) for a in arrays]


def held_in(arrays):
    return [Held(a) for a in arrays]


class Place:
    def __init__(self, slots, n):
        seq_at = lax.axis_index("seq")
        self.h, self.j = seq_at // n, seq_at % n
        self.dp = lax.axis_index("dp")
        self.group = self.dp * slots + self.h
        self.length = None


def call(grid, kernel, args, outs, name, flops=0, scratch=(), sems=1, limit=None, lengths=()):
    here = pl.BlockSpec(memory_space=pltpu.HBM)
    anywhere = pl.BlockSpec(memory_space=pl.ANY)
    scalars = pl.BlockSpec(memory_space=pltpu.SMEM)
    inside = pl.BlockSpec(memory_space=pltpu.VMEM)

    def spec(a):
        return inside if isinstance(a, Held) else anywhere if isinstance(a, Near) else here

    nbytes = sum(a.shape[0] * a.shape[1] * a.dtype.itemsize for a in list(args) + list(outs))

    def body(*refs):
        place = Place(*grid[:2])
        if lengths:
            order_ref, lengths_ref = refs[:2]
            place.length = lengths_ref[order_ref[place.h]]
        kernel(place, *refs[len(lengths) :])

    return pl.pallas_call(
        body,
        out_shape=tuple(o.array if isinstance(o, Near) else pltpu.HBM(o.shape, o.dtype) for o in outs),
        in_specs=[scalars] * len(lengths) + [spec(a) for a in args],
        out_specs=tuple(spec(o) for o in outs),
        scratch_shapes=list(scratch) + [pltpu.SemaphoreType.DMA((sems,))],
        compiler_params=pltpu.CompilerParams(vmem_limit_bytes=(limit or 8 * grid[2]) * MIB),
        cost_estimate=pl.CostEstimate(flops=int(flops), bytes_accessed=int(nbytes), transcendentals=0),
        name=name,
    )(
        *lengths,
        *[a.array if isinstance(a, Near) else pltpu.with_memory_space_constraint(a, pltpu.HBM) for a in args],
    )


class Mover:
    def __init__(self, sems):
        self.sems, self.used, self.open = sems, 0, []

    def start(self, source, target):
        copy = pltpu.make_async_copy(source, target, self.sems.at[self.used])
        self.used += 1
        copy.start()
        return copy

    def put(self, source, target):
        self.open.append(self.start(source, target))

    def drain(self):
        for copy in self.open:
            copy.wait()
        self.open = []


def cost(microseconds):
    return microseconds * 1150 * 10**6


def after(value, *others):
    return lax.optimization_barrier((value,) + others)[0]


def rows_at(index, rows):
    return pl.ds(pl.multiple_of(index * rows, rows), rows)


def send_rows(move, place, n, rows, source, stage, keep, send):
    for r in list(range(1, n, 2)) + list(range(0, n, 2)):
        here = slice((r // 2) * rows, (r // 2 + 1) * rows)
        stage[r % 2, here, :] = source[rows_at(place.j ^ r, rows), :].astype(bf16)
        move.put(stage.at[r % 2, here, :], (send if r % 2 else keep).at[here, :])


def rows_kernel(place, frames, out_grad, x_own, x_send, dy_own, dy_send, sems):
    move = Mover(sems)
    for rows, own, sent in ((frames, x_own, x_send), (out_grad, dy_own, dy_send)):
        move.put(rows.at[1 - place.h], sent)
        move.put(rows.at[place.h], own)
    move.drain()


def pack_kernel(n, slots, groups, first_row, place, *refs):
    wq, wk, wv = refs[:3]
    small = refs[3:12]
    packed, q_s, k_s, v_s, *rest = refs[12:]
    small_s, (packed_s, sems) = rest[:9], rest[9:]
    move = Mover(sems)
    loads = [move.start(a, b) for a, b in ((wq, q_s), (wk, k_s), (wv, v_s))]
    loads += [move.start(a, b) for a, b in zip(small, small_s)]
    for copy in loads:
        copy.wait()
    rs = wq.shape[0]
    hd = wq.shape[1] // n
    chunk = small[8].shape[1]
    zeros = jnp.zeros((packed_s.shape[1] - rs, packed_s.shape[2]), bf16)
    for m in range(n):
        cols = slice(m * hd, (m + 1) * hd)
        packed_s[m, rs:, :] = zeros
        packed_s[m, :rs, :hd] = q_s[:, cols]
        packed_s[m, :rs, hd : 2 * hd] = k_s[:, cols]
        packed_s[m, :rs, 2 * hd : 3 * hd] = v_s[:, cols]
        for i in range(8):
            packed_s[m, first_row + i : first_row + i + 1, :rs] = small_s[i][...]
        packed_s[m, first_row : first_row + 1, hd : hd + chunk] = small_s[8][...]
    for i in range(slots):
        move.put(packed_s, packed.at[i * n : (i + 1) * n])
    move.drain()


def pack_up_kernel(n, groups, place, up, packed, up_s, packed_s, sems):
    move = Mover(sems)
    move.start(up, up_s).wait()
    chunk = up.shape[1] // (n * groups)
    for m in range(n):
        for g in range(groups):
            at = (g * n + m) * chunk
            packed_s[m, :, g * chunk : (g + 1) * chunk] = up_s[:, at : at + chunk]
    move.put(packed_s, packed)
    move.drain()


def join_kernel(n, place, up, down, ffn, sems):
    move = Mover(sems)
    width, mine = down.shape[1], ffn.shape[1]
    chunk = down.shape[0]
    feats = ffn.shape[0] - width // mine * chunk
    move.put(up, ffn.at[:feats, :])
    for c in range(width // mine):
        move.put(down.at[:, c * mine : (c + 1) * mine], ffn.at[feats + c * chunk : feats + (c + 1) * chunk, :])
    move.drain()


def key_mask(place, rows, n, half, width):
    row = lax.broadcasted_iota(jnp.int32, (rows, width), 0)
    member = row // (2 * half)
    inside = row % (2 * half)
    own = (inside < half).astype(jnp.int32)
    h = place.h
    block_half = own * h + (1 - own) * (1 - h)
    frame = (block_half * n + member) * half + inside % half
    return frame < place.length


def first_kernel(n, dp_size, groups, half, qb, first_row, place, *refs):
    xs, gots, wos = refs[:n], refs[n : n + dp_size], refs[n + dp_size : n + dp_size + groups // dp_size]
    at = n + dp_size + groups // dp_size
    outs = refs[at : at + 11]
    hat_out, h_out, qkv_out, o_out, lse_out, w_out, vec_out, bias_up_out, wo_out, keep, send = outs
    x_s, hat_s, h_s, qkv_s, o_s, lse_s, got_s, w_s, vec_s, bias_up_s, wo3, wo_s, y_s, send_s, bias, sems = refs[at + 11 :]
    move = Mover(sems)
    j = place.j
    rows = 2 * half
    total = n * rows
    ndev = got_s.shape[0]
    hd = got_s.shape[2] // 3
    seq_size = ndev // dp_size
    rs = x_s.shape[1] // ndev
    chunk = bias_up_s.shape[1] // groups
    load = [move.start(gots[i], got_s.at[pl.ds((place.dp ^ i) * seq_size, seq_size)]) for i in range(dp_size)]
    copies = [move.start(xs[r], x_s.at[rows_at(j ^ r, rows), :]) for r in range(n)]
    slots = groups // dp_size
    outw = [
        move.start(wos[i].at[k], wo3.at[(place.dp ^ k) * slots + (place.h ^ i)])
        for k in range(dp_size)
        for i in range(slots)
    ]
    bias[...] = jnp.where(key_mask(place, total, n, half, 128), 0.0, -1.0).astype(f32)
    for copy in load:
        copy.wait()
    for d in range(ndev):
        w_s[d * rs : (d + 1) * rs, :] = got_s[d, :rs, :]
        vec_s[:, d * rs : (d + 1) * rs] = got_s[d, first_row : first_row + 8, :rs].astype(f32)
    bq, bv = [], []
    for t in range(groups):
        bias_up_s[:, t * chunk : (t + 1) * chunk] = got_s[
            t * n + j, first_row : first_row + 1, hd : hd + chunk
        ].astype(f32)
        bq.append(got_s[j * groups + t, first_row + 2 : first_row + 3, :rs].astype(f32))
        bv.append(got_s[j * groups + t, first_row + 3 : first_row + 4, :rs].astype(f32))
    bq = jnp.concatenate(bq, axis=1)
    bv = jnp.concatenate(bv, axis=1)
    move.put(w_s, w_out)
    move.put(vec_s, vec_out)
    move.put(bias_up_s, bias_up_out)
    for r in range(n):
        copies[r].wait()
        base = pl.multiple_of((j ^ r) * rows, rows)
        for part in range(2):
            at = pl.ds(base + part * half, half)
            scaled, _ = normalize(x_s[at, :].astype(f32))
            hat_s[at, :] = scaled.astype(bf16)
            h_s[at, :] = (scaled * vec_s[0:1, :] + vec_s[1:2, :]).astype(bf16)
    block = min(512, total)
    for i in range(total // block):
        at = slice(i * block, (i + 1) * block)
        qkv = dot(h_s[at, :], w_s[...])
        qkv_s[at, :hd] = ((qkv[:, :hd] + bq) * 0.125).astype(bf16)
        qkv_s[at, hd : 2 * hd] = qkv[:, hd : 2 * hd].astype(bf16)
        qkv_s[at, 2 * hd :] = (qkv[:, 2 * hd :] + bv).astype(bf16)
    move.put(hat_s, hat_out)
    move.put(h_s, h_out)
    move.put(qkv_s, qkv_out)
    heads = hd // HEAD
    for head in range(heads):
        cols = slice(head * HEAD, (head + 1) * HEAD)
        kh = qkv_s[:, hd + head * HEAD : hd + (head + 1) * HEAD]
        vt = qkv_s[:, 2 * hd + head * HEAD : 2 * hd + (head + 1) * HEAD].astype(f32).T.astype(bf16)

        def step(i, _, cols=cols, kh=kh, vt=vt, head=head):
            at = rows_at(i, qb)
            scores = dot(kh, qkv_s[at, cols], NT)
            scores = jnp.where(bias[:, 0:1] >= 0.0, scores, -1e30)
            row_max = jnp.max(scores, axis=0, keepdims=True)
            e = jnp.exp(scores - row_max)
            row_sum = jnp.sum(e, axis=0, keepdims=True)
            ot = dot(vt, e.astype(bf16)) / row_sum
            o_s[at, cols] = ot.T.astype(bf16)
            lse_s[head : head + 1, at] = row_max + jnp.log(row_sum)
            return 0

        lax.fori_loop(0, total // qb, step, 0)
    move.put(o_s, o_out)
    move.put(lse_s, lse_out)
    for copy in outw:
        copy.wait()
    for t in range(groups):
        wo_s[t * rs : (t + 1) * rs, :] = wo3[t]
    move.put(wo_s, wo_out)
    for i in range(total // block):
        at = slice(i * block, (i + 1) * block)
        y_s[at, :] = dot(o_s[at, :], wo_s[...])
    send_rows(move, place, n, rows, y_s, send_s, keep, send)
    move.drain()


def mid_kernel(count, place, *refs):
    ins, x, vec = refs[:count], refs[count], refs[count + 1]
    y_out, h_out, vec_s, y_s, sems = refs[count + 2 :]
    move = Mover(sems)
    load = move.start(vec, vec_s)
    y = ins[0][...]
    for i in range(1, count):
        y = y + ins[i][...].astype(f32)
    load.wait()
    y = x[...].astype(f32) + y + vec_s[4:5, :]
    y_s[...] = y
    move.put(y_s, y_out)
    scaled, _ = normalize(y)
    h_out[...] = (scaled * vec_s[5:6, :] + vec_s[6:7, :]).astype(bf16)
    move.drain()


def down_back_kernel(n, groups, place, *refs):
    dys, ws = refs[:n], refs[n : n + groups]
    dy_out, dg_out, w_up_out, w_down_out, dy_s, dg_s, w_up, w_down, sems = refs[n + groups :]
    move = Mover(sems)
    j, g = place.j, place.group
    rows = dys[0].shape[0]
    chunk = w_down.shape[0] // groups
    mine = w_up.shape[1]
    feats = w_up.shape[0] // groups
    first, last = [], []
    for i in range(groups):
        for c in range(w_down.shape[1] // mine):
            source = ws[i].at[feats + c * chunk : feats + (c + 1) * chunk, :]
            first.append(move.start(source, w_down.at[rows_at(g ^ i, chunk), c * mine : (c + 1) * mine]))
    copies = [move.start(dys[r], dy_s.at[rows_at(j ^ r, rows), :]) for r in range(n)]
    for i in range(groups):
        last.append(move.start(ws[i].at[:feats, :], w_up.at[rows_at(g ^ i, feats), :]))
    for copy in first:
        copy.wait()
    move.put(w_down, w_down_out)
    for copy in copies:
        copy.wait()
    block = min(512, dy_s.shape[0])
    for i in range(dy_s.shape[0] // block):
        at = slice(i * block, (i + 1) * block)
        dg_s[at, :] = dot(dy_s[at, :], w_down[...], NT)
        move.put(dg_s.at[at, :], dg_out.at[at, :])
    for copy in last:
        copy.wait()
    move.put(w_up, w_up_out)
    move.put(dy_s, dy_out)
    move.drain()


def ffn_kernel(n, place, *refs):
    hs = refs[:n]
    w_up_in, b_up_in, dg_in = refs[n : n + 3]
    h_out, g_out, du_out, keep, send, db_out = refs[n + 3 : n + 9]
    w_up, b_up, dg, h_s, g_s, du_s, dh_s, send_s, db, sems = refs[n + 9 :]
    move = Mover(sems)
    rows = hs[0].shape[0]
    total = n * rows
    copies = [move.start(hs[r], h_s.at[rows_at(place.j ^ r, rows), :]) for r in range(n)]
    copies += [move.start(w_up_in, w_up), move.start(b_up_in, b_up)]
    late = move.start(dg_in, dg)
    for copy in copies:
        copy.wait()
    block = min(512, total)
    sums = jnp.zeros(db.shape, f32)
    for i in range(total // block):
        at = slice(i * block, (i + 1) * block)
        u = dot(h_s[at, :], w_up[...]) + b_up[...]
        cdf = 0.5 * (1.0 + lax.erf(u * inv_root_two))
        g_s[at, :] = (u * cdf).astype(bf16)
        slope = cdf + u * jnp.exp(-0.5 * u * u) * inv_root_tau
        if i == 0:
            late.wait()
        du = (dg[at, :] * slope).astype(bf16)
        du_s[at, :] = du
        sums = sums + jnp.sum(du.astype(f32), axis=0, keepdims=True)
        dh_s[at, :] = dot(du, w_up[...], NT)
    db[...] = sums
    send_rows(move, place, n, rows, dh_s, send_s, keep, send)
    move.put(h_s, h_out)
    move.put(g_s, g_out)
    move.put(du_s, du_out)
    move.put(db, db_out)
    move.drain()


def down_kernel(n, place, g_in, w_in, keep, send, g, w, out_s, send_s, sems):
    move = Mover(sems)
    for copy in [move.start(w_in, w), move.start(g_in, g)]:
        copy.wait()
    total = g.shape[0]
    block = min(512, total)
    for i in range(total // block):
        at = slice(i * block, (i + 1) * block)
        out_s[at, :] = dot(g[at, :], w[...])
    send_rows(move, place, n, total // n, out_s, send_s, keep, send)
    move.drain()


def ffn_grads_kernel(groups, place, h_in, du_in, dy_in, g_in, *refs):
    outs = refs[:groups]
    h, du, dy, g, grads, stage, sems = refs[groups:]
    move = Mover(sems)
    loads = [move.start(a, b) for a, b in ((h_in, h), (du_in, du), (dy_in, dy), (g_in, g))]
    feats = h.shape[1] // groups
    mine = du.shape[1]
    chunk = mine // groups
    loads[0].wait()
    loads[1].wait()
    for i in range(groups):
        grads[i, :feats, :] = dot(h[:, i * feats : (i + 1) * feats], du[...], TN)
    loads[2].wait()
    loads[3].wait()
    for c in range(dy.shape[1] // mine):
        part = dot(g[...], dy[:, c * mine : (c + 1) * mine], TN)
        for i in range(groups):
            grads[i, feats + c * chunk : feats + (c + 1) * chunk, :] = part[i * chunk : (i + 1) * chunk, :]
    for i in range(1, groups):
        stage[i - 1] = grads[place.group ^ i].astype(bf16)
        move.put(stage.at[i - 1], outs[i])
    move.put(grads.at[place.group], outs[0])
    move.drain()


def pair_kernel(place, keep, recv, *refs):
    *outs, keep_s, sems = refs
    move = Mover(sems)
    rows = outs[0].shape[0]
    order = list(range(1, len(outs))) + [0]
    loads = {}
    for i in order:
        here = slice(i * rows, (i + 1) * rows)
        loads[i] = move.start(keep.at[here, :], keep_s.at[here, :])
    for i in order:
        here = slice(i * rows, (i + 1) * rows)
        loads[i].wait()
        outs[i][...] = (keep_s[here, :].astype(f32) + recv[here, :].astype(f32)).astype(outs[i].dtype)


def fold_kernel(count, place, *refs):
    kept, got, outs = refs[:count], refs[count : 2 * count], refs[2 * count : 3 * count]
    for a, b, out in zip(kept, got, outs):
        out[...] = (a[...].astype(f32) + b[...].astype(f32)).astype(bf16)


def out_kernel(count, place, *refs):
    ins = refs[: count + 2]
    kept, sent = refs[count + 2 : count + 4]
    held = refs[count + 4 : 2 * count + 6]
    out_s, sems = refs[2 * count + 6 :]
    move = Mover(sems)
    for copy in [move.start(a, b) for a, b in zip(ins, held)]:
        copy.wait()
    total = held[0][...] + held[count][...]
    for i in range(1, count):
        total = total + held[i][...].astype(f32)
    out_s[...] = (total + held[count + 1][7:8, :]).astype(bf16)
    half = kept.shape[0]
    move.put(out_s.at[half:, :], sent)
    move.put(out_s.at[:half, :], kept)
    move.drain()


def mid_back_kernel(count, place, *refs):
    ins, (y_in, vec_in, dy) = refs[:count], refs[count : count + 3]
    dy1_out, da_out, small_out, y, vec, dy1_s, small, sems = refs[count + 3 :]
    move = Mover(sems)
    loads = [move.start(y_in, y), move.start(vec_in, vec)]
    dh = ins[0][...]
    for i in range(1, count):
        dh = dh + ins[i][...].astype(f32)
    for copy in loads:
        copy.wait()
    scaled, inv_std = normalize(y[...])
    dyf = dy[...].astype(f32)
    dy1 = dyf + norm_back(dh, scaled, inv_std, vec[5:6, :])
    da = dy1.astype(bf16)
    da_out[...] = da
    dy1_s[...] = dy1
    move.put(dy1_s, dy1_out)
    small[0:1, :] = jnp.sum(dh * scaled, axis=0, keepdims=True)
    small[1:2, :] = jnp.sum(dh, axis=0, keepdims=True)
    small[2:3, :] = jnp.sum(da.astype(f32), axis=0, keepdims=True)
    small[3:4, :] = jnp.sum(dyf, axis=0, keepdims=True)
    move.put(small, small_out)
    move.drain()


def attend_back_kernel(n, half, qb, place, *refs):
    das, ins = refs[:n], refs[n : n + 4]
    dqkv_out, keep, send, db_out, da_out = refs[n + 4 : n + 9]
    da, qkv, lse, wo, w, dqkv, dh_s, send_s, db, do, bias, acc_k, acc_v, sems = refs[n + 9 :]
    rows = 2 * half
    move = Mover(sems)
    copies = [move.start(das[r], da.at[rows_at(place.j ^ r, rows), :]) for r in range(n)]
    loads = [move.start(a, b) for a, b in zip(ins, (wo, qkv, lse, w))]
    total = qkv.shape[0]
    hd = do.shape[1]
    heads = hd // HEAD
    bias[...] = jnp.where(key_mask(place, total, n, half, 128), 0.0, -1.0).astype(f32)
    loads[0].wait()
    for copy in copies:
        copy.wait()
    move.put(da, da_out)
    block = min(512, total)
    for i in range(total // block):
        at = slice(i * block, (i + 1) * block)
        do[at, :] = dot(da[at, :], wo[...], NT).astype(bf16)
    for copy in loads[1:]:
        copy.wait()
    for head in range(heads):
        cols = slice(head * HEAD, (head + 1) * HEAD)
        kh = qkv[:, hd + head * HEAD : hd + (head + 1) * HEAD]
        vh = qkv[:, 2 * hd + head * HEAD : 2 * hd + (head + 1) * HEAD]
        kt = kh.astype(f32).T.astype(bf16)
        acc_k[...] = jnp.zeros_like(acc_k)
        acc_v[...] = jnp.zeros_like(acc_v)

        def step(i, _, cols=cols, kh=kh, vh=vh, kt=kt, head=head):
            at = rows_at(i, qb)
            qh = qkv[at, cols]
            doh = do[at, cols]
            scores = dot(kh, qh, NT)
            probs = jnp.where(bias[:, 0:1] >= 0.0, jnp.exp(scores - lse[head : head + 1, at]), 0.0)
            dp = dot(vh, doh, NT)
            centre = jnp.sum(probs * dp, axis=0, keepdims=True)
            ds = (probs * (dp - centre)).astype(bf16)
            acc_v[...] += dot(probs.astype(bf16), doh)
            acc_k[...] += dot(ds, qh)
            dq = dot(kt, ds)
            dqkv[at, cols] = (dq.T.astype(bf16).astype(f32) * 0.125).astype(bf16)
            return 0

        lax.fori_loop(0, total // qb, step, 0)
        dqkv[:, hd + head * HEAD : hd + (head + 1) * HEAD] = acc_k[...].astype(bf16)
        dqkv[:, 2 * hd + head * HEAD : 2 * hd + (head + 1) * HEAD] = acc_v[...].astype(bf16)
    move.put(dqkv, dqkv_out)
    sums = jnp.zeros(db.shape, f32)
    for i in range(total // block):
        at = slice(i * block, (i + 1) * block)
        grads = dqkv[at, :]
        sums = sums + jnp.sum(grads.astype(f32), axis=0, keepdims=True)
        dh_s[at, :] = dot(grads, w[...], NT)
    db[...] = sums
    send_rows(move, place, n, rows, dh_s, send_s, keep, send)
    move.put(db, db_out)
    move.drain()


def attn_grads_kernel(n, dp_size, groups, first_row, place, *refs):
    ins, outs = refs[:7], refs[7 : 7 + dp_size]
    dqkv, h, w, hat, two, db, up, small, grads, packed_s, sems = refs[7 + dp_size :]
    move = Mover(sems)
    j = place.j
    loads = [move.start(a, b) for a, b in zip(ins, (dqkv, h, w, hat, two, db, up))]
    ndev = packed_s.shape[0]
    hd = dqkv.shape[1] // 3
    rs = h.shape[1] // ndev
    chunk = up.shape[1] // groups
    loads[0].wait()
    loads[1].wait()
    grads[...] = dot(h[...], dqkv[...], TN).astype(bf16)
    for copy in loads[2:]:
        copy.wait()
    small[...] = jnp.zeros_like(small)
    step_rows = min(512, hat.shape[0])

    def step(i, _):
        at = rows_at(i, step_rows)
        dh = dot(dqkv[at, :], w[...], NT)
        small[0:1, :] += jnp.sum(dh * hat[at, :].astype(f32), axis=0, keepdims=True)
        small[1:2, :] += jnp.sum(dh, axis=0, keepdims=True)
        return 0

    lax.fori_loop(0, hat.shape[0] // step_rows, step, 0)
    small[4:8, :] = two[...]
    zeros = jnp.zeros((packed_s.shape[1] - rs, packed_s.shape[2]), bf16)
    for d in range(ndev):
        packed_s[d, rs:, :] = zeros
        packed_s[d, :rs, :] = grads[d * rs : (d + 1) * rs, :]
        packed_s[d, first_row : first_row + 8, :rs] = small[:, d * rs : (d + 1) * rs].astype(bf16)
    for t in range(groups):
        cols = slice(t * rs, (t + 1) * rs)
        at = j * groups + t
        packed_s[at, first_row + 2 : first_row + 3, :rs] = db[:, :hd][:, cols].astype(bf16)
        packed_s[at, first_row + 3 : first_row + 4, :rs] = db[:, 2 * hd :][:, cols].astype(bf16)
        packed_s[t * n + j, first_row : first_row + 1, hd : hd + chunk] = up[
            :, t * chunk : (t + 1) * chunk
        ].astype(bf16)
    seq_size = ndev // dp_size
    for i in list(range(1, dp_size)) + [0]:
        move.put(packed_s.at[pl.ds((place.dp ^ i) * seq_size, seq_size)], outs[i])
    move.drain()


def out_grads_kernel(dp_size, groups, place, da_in, o_in, *refs):
    outs = refs[:dp_size]
    da, o, grads, stage, sems = refs[dp_size:]
    move = Mover(sems)
    for copy in [move.start(o_in, o), move.start(da_in, da)]:
        copy.wait()
    all_rows = dot(o[...], da[...], TN)
    rs = grads.shape[1]
    for t in range(groups):
        grads[t] = all_rows[t * rs : (t + 1) * rs, :]
    slots = groups // dp_size
    for k in range(dp_size):
        for i in range(slots):
            stage[k, i] = grads[(place.dp ^ k) * slots + (place.h ^ i)].astype(bf16)
        move.put(stage.at[k], outs[k])
    move.drain()


def last_kernel(count, place, *refs):
    ins, rider = refs[: count + 3], refs[count + 3]
    kept, sent = refs[count + 4 : count + 6]
    held = refs[count + 6 : 2 * count + 9]
    out_s, sems = refs[2 * count + 9 :]
    move = Mover(sems)
    half = kept.shape[0]
    move.put(rider.at[1], sent.at[half:, :])
    for copy in [move.start(a, b) for a, b in zip(ins, held)]:
        copy.wait()
    x, dy1, vec = held[count:]
    dh = held[0][...]
    for i in range(1, count):
        dh = dh + held[i][...].astype(f32)
    scaled, inv_std = normalize(x[...].astype(f32))
    out_s[...] = (dy1[...] + norm_back(dh, scaled, inv_std, vec[0:1, :])).astype(bf16)
    move.put(out_s.at[half:, :], sent.at[:half, :])
    move.put(out_s.at[:half, :], kept)
    move.drain()


def ffn_sum_kernel(count, place, *refs):
    ins, (up_out, down_out) = refs[:count], refs[count : count + 2]
    held, (total, up_s, down_s, sems) = refs[count + 2 : 2 * count + 2], refs[2 * count + 2 :]
    move = Mover(sems)
    for copy in [move.start(a, b) for a, b in zip(ins, held)]:
        copy.wait()
    ffn = held[0][...].astype(f32)
    for piece in held[1:]:
        ffn = ffn + piece[...].astype(f32)
    total[...] = ffn
    n, rs, mine = up_s.shape
    chunk, width = down_s.shape
    for m in range(n):
        up_s[m] = total[m * rs : (m + 1) * rs, :].astype(bf16)
    move.put(up_s, up_out)
    feats = n * rs
    for c in range(width // mine):
        down_s[:, c * mine : (c + 1) * mine] = total[feats + c * chunk : feats + (c + 1) * chunk, :]
    move.put(down_s, down_out)
    move.drain()


def unpack_kernel(n, groups, first_row, place, *refs):
    back, up_back, out_w = refs[:3]
    halves = refs[3:7]
    output, frames_grad, out_w_grad, up, wq, wk, wv = refs[7:14]
    vectors = refs[14:23]
    back_s, up_back_s, in_s, out_s, up_s, q_s, k_s, v_s = refs[23:31]
    vectors_s, sems = refs[31:40], refs[40]
    move = Mover(sems)
    load, more, third = move.start(back, back_s), move.start(up_back, up_back_s), move.start(out_w, in_s)
    half = output.shape[1]
    for i, target in enumerate((output, frames_grad)):
        move.put(halves[2 * i], target.at[place.h])
        move.put(halves[2 * i + 1].at[:half, :], target.at[1 - place.h])
    third.wait()
    out_s[...] = in_s[...].astype(f32)
    move.put(out_s, out_w_grad)
    rs = wq.shape[0]
    hd = wq.shape[1] // n
    chunk = up.shape[1] // (n * groups)
    more.wait()
    for m in range(n):
        for g in range(groups):
            at = (g * n + m) * chunk
            up_s[:, at : at + chunk] = up_back_s[m, :, g * chunk : (g + 1) * chunk].astype(f32)
    move.put(up_s, up)
    load.wait()
    sums = jnp.zeros((8, 3 * hd), f32)
    for m in range(n):
        cols = slice(m * hd, (m + 1) * hd)
        total = back_s[m].astype(f32)
        for i in range(m + n, back_s.shape[0], n):
            total = total + back_s[i].astype(f32)
        for i, target in enumerate((q_s, k_s, v_s)):
            target[:, cols] = total[:rs, i * hd : (i + 1) * hd]
        sums = sums + total[first_row:, :]
    for a, b in ((q_s, wq), (k_s, wk), (v_s, wv)):
        move.put(a, b)
    for i in range(8):
        vectors_s[i][...] = sums[i : i + 1, :rs]
    vectors_s[8][...] = sums[0:1, hd : hd + chunk]
    for a, b in zip(vectors_s, vectors):
        move.put(a, b)
    move.drain()


def on_device(
    dp_size,
    seq_size,
    frames,
    out_grad,
    order,
    lengths,
    first_gain,
    first_shift,
    query_weight,
    query_bias,
    key_weight,
    value_weight,
    value_bias,
    output_weight,
    output_bias,
    second_gain,
    second_shift,
    up_weight,
    up_bias,
    down_weight,
    down_bias,
):
    slots, half, width = frames.shape
    n = seq_size // slots
    groups = dp_size * slots
    ndev = dp_size * seq_size
    hd = width // n
    heads = hd // HEAD
    rs = query_weight.shape[0]
    hidden = up_weight.shape[1]
    chunk = hidden // ndev
    mine = hidden // n
    parts = width // mine
    feats = n * rs
    rows = 2 * half
    total = n * rows
    qb = 512
    count = n // 2
    both = ("dp", "seq")
    first_row = -(-rs // 8) * 8
    block_rows = first_row + 8

    scale = -(-total // 1024)
    grid = (slots, n, scale)

    def xor(value, bit):
        return lax.ppermute(value, "seq", [(i, i ^ bit) for i in range(seq_size)])

    def gather_direct(value):
        got = [xor(value, r) for r in range(n - 2, 0, -2)]
        return [value] + got[::-1]

    def gather_pair(even):
        out = []
        for piece in even:
            out += [piece, xor(piece, 1)]
        return out

    def pair(keep, recv):
        outs = [sds((rows, width), f32)] + [sds((rows, width), bf16)] * (count - 1)
        return call(
        grid,
            pair_kernel,
            [keep, Held(recv)],
            held_in(outs),
            "pair",
            cost(1),
            scratch=[vmem(keep)],
            sems=count,
        )

    def scatter(pieces):
        return [pieces[0]] + [xor(pieces[i], 2 * i) for i in range(count - 1, 0, -1)][::-1]

    def to_group(value, i):
        pairs = []
        for d in range(ndev):
            dp_of, seq_of = d // seq_size, d % seq_size
            g_of = (dp_of * slots + seq_of // n) ^ i
            pairs.append((d, g_of // slots * seq_size + g_of % slots * n + seq_of % n))
        return lax.ppermute(value, both, pairs)

    def members(value):
        index = [[s * n + i for i in range(n)] for s in range(slots)]
        return lax.all_to_all(value, "seq", 0, 0, tiled=True, axis_index_groups=index)

    def fold(kept, got):
        outs = [sds(a.shape, bf16) for a in kept]
        return call(
            grid,
            functools.partial(fold_kernel, len(kept)),
            held_in(list(kept) + list(got)),
            held_in(outs),
            "fold",
            cost(2),
            sems=1,
            limit=16,
        )

    def spread(pieces):
        bit = len(pieces)
        while bit < groups:
            pieces = pieces + [to_group(piece, bit) for piece in pieces]
            bit *= 2
        return pieces

    def to_dp(value, i):
        return lax.ppermute(value, "dp", [(d, d ^ i) for d in range(dp_size)])

    def owner_pairs(k):
        pairs = []
        for d in range(ndev):
            g_of = (d % groups) ^ (k * slots)
            pairs.append((d, g_of // slots * seq_size + g_of % slots * n + d // groups))
        return pairs

    owners = owner_pairs(0)
    out_w = jnp.stack([lax.ppermute(output_weight, both, owner_pairs(k)) for k in range(dp_size)])

    small_in = [first_gain, first_shift, query_bias, value_bias, output_bias, second_gain, second_shift, down_bias]
    small_in = [v.reshape(1, -1) for v in small_in + [up_bias]]
    weights_in = [query_weight, key_weight, value_weight]
    half_sds, row_sds = sds((half, width), bf16), sds((rows, width), bf16)
    packed_sds, up_sds = sds((seq_size, block_rows, 3 * hd), bf16), sds((n, rs, mine), bf16)
    x_own, x_send, dy_own, dy_send = call(
        grid, rows_kernel, [frames, out_grad], near([half_sds] * 4), "rows", cost(1), sems=4
    )
    x_recv = xor(x_send, n)
    (packed,) = call(
        grid,
        functools.partial(pack_kernel, n, slots, groups, first_row),
        [after(weights_in[0], x_send)] + weights_in[1:] + small_in,
        near([packed_sds]),
        "pack",
        cost(2),
        scratch=[vmem(w) for w in weights_in] + [vmem(v) for v in small_in] + [pltpu.VMEM((n, block_rows, 3 * hd), bf16)],
        sems=12 + slots,
    )
    (up_packed,) = call(
        grid,
        functools.partial(pack_up_kernel, n, groups),
        [up_weight],
        near([up_sds]),
        "pack_up",
        cost(1),
        scratch=[vmem(up_weight), vmem(up_sds)],
        sems=2,
    )
    attn_w = lax.all_to_all(packed, "seq", 0, 0, tiled=True)
    up_mine = members(after(up_packed, attn_w))
    x = jnp.concatenate([x_own, x_recv])
    x_even = gather_direct(x)
    wos = [out_w, xor(out_w, n)]
    dy_recv = xor(after(dy_send, attn_w), n)
    attn_ws = [attn_w]
    while len(attn_ws) < dp_size:
        attn_ws += [to_dp(piece, len(attn_ws)) for piece in attn_ws]
    ffn_sds = sds((feats + parts * chunk, mine), bf16)
    (ffn_w,) = call(
        grid,
        functools.partial(join_kernel, n),
        near([up_mine.reshape(feats, mine), down_weight]),
        near([ffn_sds]),
        "join",
        cost(1),
        sems=1 + parts,
    )
    ffn_half = to_group(after(ffn_w, attn_w), 1)
    xs = gather_pair([after(piece, attn_ws[-1], wos[-1]) for piece in x_even])
    dy = jnp.concatenate([dy_own, dy_recv])

    ffn_go, dy_go, xs, attn_ws, wos = lax.optimization_barrier((ffn_w, dy, tuple(xs), tuple(attn_ws), tuple(wos)))
    xs, attn_ws, wos = list(xs), list(attn_ws), list(wos)
    ffn_ws = [ffn_w, ffn_half, to_group(ffn_go, 2)]
    dy_even = gather_direct(dy_go)
    x_sds = sds((total, width), bf16)
    keep_sds = send_sds = sds((total // 2, width), bf16)
    s_half = pltpu.VMEM((2, total // 2, width), bf16)
    outs = [
        x_sds,
        x_sds,
        sds((total, 3 * hd), bf16),
        sds((total, hd), bf16),
        sds((heads, total), f32),
        sds((width, 3 * hd), bf16),
        sds((8, width), f32),
        sds((1, mine), f32),
        sds((hd, width), bf16),
        keep_sds,
        send_sds,
    ]
    s_hat, s_h, s_qkv, s_o, s_lse, s_w, s_vec, s_bias, s_wo, _, _ = [vmem(o) for o in outs]
    s_rows = pltpu.VMEM((total, width), f32)
    s_got = pltpu.VMEM((ndev, block_rows, 3 * hd), bf16)
    s_wo3 = pltpu.VMEM((groups, rs, width), bf16)
    hat, h_first, qkv, o_heads, lse, w_qkv, vec, bias_up, wo, keep, send = call(
        grid,
        functools.partial(first_kernel, n, dp_size, groups, half, qb, first_row),
        near(xs + attn_ws + wos),
        outs[:-1] + near(outs[-1:]),
        "first",
        cost(17),
        scratch=[vmem(x_sds), s_hat, s_h, s_qkv, s_o, s_lse, s_got, s_w, s_vec, s_bias, s_wo3, s_wo, s_rows, s_half]
        + [pltpu.VMEM((total, 128), f32)],
        sems=3 * n + groups + dp_size + 10,
        lengths=(order, lengths),
        limit=48,
    )
    send = after(send, *ffn_ws[1:], *dy_even[1:])

    y_sds = sds((rows, width), f32)
    y_pieces = pair(keep, xor(send, 1))
    ys = scatter(y_pieces)
    dys = gather_pair([dy_even[0]] + [after(piece, y_pieces[0]) for piece in dy_even[1:]])
    ffn_ws = spread(ffn_ws + [to_group(after(ffn_ws[1], y_pieces[0]), 2)])
    y1, h2 = call(
        grid,
        functools.partial(mid_kernel, count),
        held_in(ys + [x]) + [vec],
        [y_sds, Held(row_sds)],
        "mid",
        cost(2),
        scratch=[vmem(vec), vmem(y_sds)],
        sems=2,
    )
    h2_even = gather_direct(h2)

    outs = [x_sds, sds((total, mine), f32), sds((width, mine), bf16), sds((mine, width), bf16)]
    dy_all, dg, w_up, w_down = call(
        grid,
        functools.partial(down_back_kernel, n, groups),
        near(dys + ffn_ws),
        outs,
        "down_back",
        cost(5),
        scratch=[vmem(o) for o in outs],
        sems=2 * n + groups * (parts + 1) + 3,
        limit=14 * scale,
    )
    h2s = gather_pair(h2_even[:1] + [after(piece, dg) for piece in h2_even[1:]])

    act_sds = sds((total, mine), bf16)
    outs = [x_sds, act_sds, act_sds, keep_sds, send_sds, sds((1, mine), f32)]
    h2_all, g, du, keep, send, d_bias_up = call(
        grid,
        functools.partial(ffn_kernel, n),
        near(h2s) + [w_up, bias_up, dg],
        outs[:4] + near(outs[4:5]) + outs[5:],
        "ffn",
        cost(9),
        scratch=[vmem(a) for a in [w_up, bias_up, dg] + outs[:3]] + [s_rows, s_half, vmem(outs[5])],
        sems=3 * n + 7,
        limit=28 * scale,
    )
    dh2 = scatter(pair(keep, xor(send, 1)))

    g_then = after(g, dh2[0])
    out_keep, out_send = call(
        grid,
        functools.partial(down_kernel, n),
        [g_then, w_down],
        [keep_sds, Near(send_sds)],
        "down",
        cost(4),
        scratch=[vmem(g), vmem(w_down), s_rows, s_half],
        sems=n + 2,
        limit=16 * scale,
    )
    ffn_parts = call(
        grid,
        functools.partial(ffn_grads_kernel, groups),
        [h2_all, du, dy_all, g_then],
        [sds(ffn_sds.shape, f32)] + near([ffn_sds] * (groups - 1)),
        "ffn_grads",
        cost(0),
        scratch=[vmem(a) for a in (x_sds, act_sds, x_sds, act_sds)]
        + [pltpu.VMEM((groups,) + ffn_sds.shape, f32), pltpu.VMEM((groups - 1,) + ffn_sds.shape, bf16)],
        sems=4 + groups,
        limit=20 * scale,
    )

    small_sds = sds((4, width), f32)
    outs = [y_sds, row_sds, small_sds]
    dy1, da, small_two = call(
        grid,
        functools.partial(mid_back_kernel, count),
        held_in(dh2) + [after(y1, ffn_parts[0], out_keep), vec, Held(dy)],
        outs[:1] + held_in(outs[1:2]) + outs[2:],
        "mid_back",
        cost(3),
        scratch=[vmem(y1), vmem(vec), vmem(y_sds), vmem(small_sds)],
        sems=4,
    )
    da_even = gather_direct(da)
    bit = groups // 2
    while bit > 2:
        ffn_parts = fold(ffn_parts[:bit], [to_group(piece, bit) for piece in ffn_parts[bit:]])
        bit //= 2
    ffn_got = [to_group(piece, 2) for piece in ffn_parts[2:4]]
    out_kept = pair(out_keep, xor(after(out_send, da), 1))
    (ffn_next,) = fold([after(ffn_parts[1], out_kept[0])], ffn_got[1:])
    das = gather_pair([da_even[0]] + [after(piece, ffn_next) for piece in da_even[1:]])

    out_kept, das, ffn_next = lax.optimization_barrier((tuple(out_kept), tuple(das), ffn_next))
    out_kept, das = list(out_kept), list(das)
    ffn_got = [ffn_got[0], to_group(ffn_next, 1)]
    out_pieces = scatter(out_kept)
    ins = [wo, qkv, lse, w_qkv]
    outs = [sds((total, 3 * hd), bf16), keep_sds, send_sds, sds((1, 3 * hd), f32), x_sds]
    d_qkv, keep, send, d_bias_qkv, da_all = call(
        grid,
        functools.partial(attend_back_kernel, n, half, qb),
        near(das) + ins,
        outs[:2] + near(outs[2:3]) + outs[3:],
        "attend_back",
        cost(0),
        scratch=[vmem(x_sds)]
        + [vmem(a) for a in (qkv, lse, wo, w_qkv, outs[0])]
        + [s_rows, s_half, vmem(outs[3]), pltpu.VMEM((total, hd), bf16), pltpu.VMEM((total, 128), f32)]
        + [pltpu.VMEM((total, HEAD), f32)] * 2,
        sems=2 * n + 9,
        lengths=(order, lengths),
        limit=48,
    )
    recv = xor(after(send, *out_pieces[1:], *ffn_got), 1)

    ins = [d_qkv, h_first, w_qkv, hat, small_two, d_bias_qkv, d_bias_up]
    attn_parts = call(
        grid,
        functools.partial(attn_grads_kernel, n, dp_size, groups, first_row),
        ins,
        near([packed_sds] * dp_size),
        "attn_grads",
        cost(6),
        scratch=[vmem(a) for a in ins]
        + [
            pltpu.VMEM((8, width), f32),
            pltpu.VMEM((width, 3 * hd), bf16),
            pltpu.VMEM((ndev, block_rows, 3 * hd), bf16),
        ],
        sems=7 + dp_size,
        limit=20 * scale,
    )
    dh1_pieces = pair(after(keep, attn_parts[0]), recv)
    dh1 = scatter(dh1_pieces)
    bit = dp_size // 2
    while bit > 1:
        attn_parts = fold(attn_parts[:bit], [to_dp(piece, bit) for piece in attn_parts[bit:]])
        bit //= 2
    attn_got = to_dp(attn_parts[1], 1)

    ffn_sums = [after(ffn_parts[0], dh1_pieces[0])] + ffn_got
    down_sds = sds((chunk, width), f32)
    up_back, down_weight_grad = call(
        grid,
        functools.partial(ffn_sum_kernel, 3),
        ffn_sums[:1] + near(ffn_sums[1:]),
        [Near(up_sds), down_sds],
        "ffn_sum",
        cost(2),
        scratch=[vmem(a) for a in ffn_sums] + [pltpu.VMEM(ffn_sds.shape, f32), vmem(up_sds), vmem(down_sds)],
        sems=5,
    )
    up_back = members(up_back)
    out_parts = call(
        grid,
        functools.partial(out_grads_kernel, dp_size, groups),
        [da_all, after(o_heads, dh1_pieces[0])],
        near([sds((slots, rs, width), bf16)] * dp_size),
        "out_grads",
        cost(2),
        scratch=[
            vmem(x_sds),
            vmem(o_heads),
            pltpu.VMEM((groups, rs, width), f32),
            pltpu.VMEM((dp_size, slots, rs, width), bf16),
        ],
        sems=2 + dp_size,
        limit=10 * scale,
    )
    bit = dp_size // 2
    while bit > 1:
        out_parts = fold(out_parts[:bit], [to_dp(piece, bit) for piece in out_parts[bit:]])
        bit //= 2

    (attn_sum,) = fold([after(attn_parts[0], up_back)], [attn_got])
    back = lax.all_to_all(attn_sum, "seq", 0, 0, tiled=True)
    (out_w_sum,) = fold([after(out_parts[0], attn_sum)], [to_dp(out_parts[1], 1)])

    ins = out_pieces + [y1, vec]
    out_own, out_sent = call(
        grid,
        functools.partial(out_kernel, count),
        near([after(ins[0], attn_sum)] + ins[1:count]) + ins[count:],
        near([half_sds] * 2),
        "out",
        cost(2),
        scratch=[vmem(a) for a in ins + [row_sds]],
        sems=len(ins) + 2,
    )
    out_other = xor(out_sent, n)

    ins = dh1 + [x, after(dy1, attn_sum), vec]
    kept, sent = call(
        grid,
        functools.partial(last_kernel, count),
        near(ins[: count + 1]) + ins[count + 1 :] + near([out_w_sum]),
        near([half_sds, sds((half + rs, width), bf16)]),
        "last",
        cost(2),
        scratch=[vmem(a) for a in ins + [row_sds]],
        sems=len(ins) + 3,
    )
    other = xor(sent, n)
    out_w = (out_w_sum[0].astype(f32) + other[half:].astype(f32)).astype(bf16)
    out_w = lax.ppermute(out_w, both, [(b, a) for a, b in owners])
    frames_sds = sds(frames.shape, bf16)
    weight_sds = sds((rs, width), f32)
    outs = [weight_sds, sds((rs, hidden), f32)] + [weight_sds] * 3
    vectors = [sds((1, rs), f32)] * 8 + [sds((1, chunk), f32)]
    output, frames_grad, output_weight_grad, up_weight_grad, d_query, d_key, d_value, *vectors = call(
        grid,
        functools.partial(unpack_kernel, n, groups, first_row),
        near([back, up_back, out_w, out_own, out_other, kept, other]),
        [frames_sds] * 2 + outs + vectors,
        "unpack",
        cost(2),
        scratch=[vmem(a) for a in [back, up_back, out_w] + outs + vectors],
        sems=24,
    )
    vectors = [v.reshape(-1) for v in vectors]
    return (
        output,
        frames_grad,
        vectors[0],
        vectors[1],
        d_query,
        vectors[2],
        d_key,
        d_value,
        vectors[3],
        output_weight_grad,
        vectors[6],
        vectors[4],
        vectors[5],
        up_weight_grad,
        vectors[8],
        down_weight_grad,
        vectors[7],
    )


def solution(mesh):
    vector = P(("dp", "seq"))
    matrix = P(("dp", "seq"), None)
    rows = P("dp", "seq", None)
    return jax.shard_map(
        functools.partial(on_device, mesh.shape["dp"], mesh.shape["seq"]),
        mesh=mesh,
        in_specs=(
            rows,
            rows,
            P("dp"),
            P(),
            vector,
            vector,
            matrix,
            vector,
            matrix,
            matrix,
            vector,
            matrix,
            vector,
            vector,
            vector,
            matrix,
            vector,
            matrix,
            vector,
        ),
        out_specs=(
            rows,
            rows,
            vector,
            vector,
            matrix,
            vector,
            matrix,
            matrix,
            vector,
            matrix,
            vector,
            vector,
            vector,
            matrix,
            vector,
            matrix,
            vector,
        ),
        check_vma=False,
    )
```

```python
import functools

import jax
import jax.numpy as jnp
from jax import lax
from jax.experimental import pallas as pl
from jax.experimental.pallas import tpu as pltpu
from jax.sharding import PartitionSpec as P

HEAD = 64
f32 = jnp.float32
bf16 = jnp.bfloat16
norm_eps = 1e-05
inv_root_two = 0.7071067811865476
inv_root_tau = 0.3989422804014327
NN = (((1,), (0,)), ((), ()))
NT = (((1,), (1,)), ((), ()))
TN = (((0,), (0,)), ((), ()))
MIB = 1024 * 1024


def dot(a, b, dims=NN):
    return lax.dot_general(a, b, dims, preferred_element_type=f32)


def normalize(rows):
    average = jnp.mean(rows, axis=-1, keepdims=True)
    centered = rows - average
    inv_std = lax.rsqrt(jnp.mean(centered * centered, axis=-1, keepdims=True) + norm_eps)
    return centered * inv_std, inv_std


def norm_back(grad_rows, scaled, inv_std, gain):
    grad_hat = grad_rows * gain
    return inv_std * (
        grad_hat
        - jnp.mean(grad_hat, axis=-1, keepdims=True)
        - scaled * jnp.mean(grad_hat * scaled, axis=-1, keepdims=True)
    )


def sds(shape, dtype):
    return jax.ShapeDtypeStruct(shape, dtype)


def vmem(like):
    return pltpu.VMEM(like.shape, like.dtype)


class Near:
    def __init__(self, array):
        self.array = array
        self.shape, self.dtype = array.shape, array.dtype


class Held(Near):
    pass


def near(arrays):
    return [Near(a) for a in arrays]


def held_in(arrays):
    return [Held(a) for a in arrays]


class Place:
    def __init__(self, slots, n):
        seq_at = lax.axis_index("seq")
        self.h, self.j = seq_at // n, seq_at % n
        self.dp = lax.axis_index("dp")
        self.group = self.dp * slots + self.h
        self.length = None


def call(grid, kernel, args, outs, name, flops=0, scratch=(), sems=1, limit=None, lengths=()):
    here = pl.BlockSpec(memory_space=pltpu.HBM)
    anywhere = pl.BlockSpec(memory_space=pl.ANY)
    scalars = pl.BlockSpec(memory_space=pltpu.SMEM)
    inside = pl.BlockSpec(memory_space=pltpu.VMEM)

    def spec(a):
        return inside if isinstance(a, Held) else anywhere if isinstance(a, Near) else here

    nbytes = sum(a.shape[0] * a.shape[1] * a.dtype.itemsize for a in list(args) + list(outs))

    def body(*refs):
        place = Place(*grid[:2])
        if lengths:
            order_ref, lengths_ref = refs[:2]
            place.length = lengths_ref[order_ref[place.h]]
        kernel(place, *refs[len(lengths) :])

    return pl.pallas_call(
        body,
        out_shape=tuple(o.array if isinstance(o, Near) else pltpu.HBM(o.shape, o.dtype) for o in outs),
        in_specs=[scalars] * len(lengths) + [spec(a) for a in args],
        out_specs=tuple(spec(o) for o in outs),
        scratch_shapes=list(scratch) + [pltpu.SemaphoreType.DMA((sems,))],
        compiler_params=pltpu.CompilerParams(vmem_limit_bytes=(limit or 8 * grid[2]) * MIB),
        cost_estimate=pl.CostEstimate(flops=int(flops), bytes_accessed=int(nbytes), transcendentals=0),
        name=name,
    )(
        *lengths,
        *[a.array if isinstance(a, Near) else pltpu.with_memory_space_constraint(a, pltpu.HBM) for a in args],
    )


class Mover:
    def __init__(self, sems):
        self.sems, self.used, self.open = sems, 0, []

    def start(self, source, target):
        copy = pltpu.make_async_copy(source, target, self.sems.at[self.used])
        self.used += 1
        copy.start()
        return copy

    def put(self, source, target):
        self.open.append(self.start(source, target))

    def drain(self):
        for copy in self.open:
            copy.wait()
        self.open = []


def cost(microseconds):
    return microseconds * 1150 * 10**6


def after(value, *others):
    return lax.optimization_barrier((value,) + others)[0]


def rows_at(index, rows):
    return pl.ds(pl.multiple_of(index * rows, rows), rows)


def send_rows(move, place, n, rows, source, stage, keep, send):
    for r in list(range(1, n, 2)) + list(range(0, n, 2)):
        here = slice((r // 2) * rows, (r // 2 + 1) * rows)
        stage[r % 2, here, :] = source[rows_at(place.j ^ r, rows), :].astype(bf16)
        move.put(stage.at[r % 2, here, :], (send if r % 2 else keep).at[here, :])


def rows_kernel(place, frames, out_grad, x_own, x_send, dy_own, dy_send, sems):
    move = Mover(sems)
    for rows, own, sent in ((frames, x_own, x_send), (out_grad, dy_own, dy_send)):
        move.put(rows.at[1 - place.h], sent)
        move.put(rows.at[place.h], own)
    move.drain()


def pack_kernel(n, slots, groups, first_row, place, *refs):
    wq, wk, wv = refs[:3]
    small = refs[3:12]
    packed, q_s, k_s, v_s, *rest = refs[12:]
    small_s, (packed_s, sems) = rest[:9], rest[9:]
    move = Mover(sems)
    loads = [move.start(a, b) for a, b in ((wq, q_s), (wk, k_s), (wv, v_s))]
    loads += [move.start(a, b) for a, b in zip(small, small_s)]
    for copy in loads:
        copy.wait()
    rs = wq.shape[0]
    hd = wq.shape[1] // n
    chunk = small[8].shape[1]
    zeros = jnp.zeros((packed_s.shape[1] - rs, packed_s.shape[2]), bf16)
    for m in range(n):
        cols = slice(m * hd, (m + 1) * hd)
        packed_s[m, rs:, :] = zeros
        packed_s[m, :rs, :hd] = q_s[:, cols]
        packed_s[m, :rs, hd : 2 * hd] = k_s[:, cols]
        packed_s[m, :rs, 2 * hd : 3 * hd] = v_s[:, cols]
        for i in range(8):
            packed_s[m, first_row + i : first_row + i + 1, :rs] = small_s[i][...]
        packed_s[m, first_row : first_row + 1, hd : hd + chunk] = small_s[8][...]
    for i in range(slots):
        move.put(packed_s, packed.at[i * n : (i + 1) * n])
    move.drain()


def pack_up_kernel(n, groups, place, up, packed, up_s, packed_s, sems):
    move = Mover(sems)
    move.start(up, up_s).wait()
    chunk = up.shape[1] // (n * groups)
    for m in range(n):
        for g in range(groups):
            at = (g * n + m) * chunk
            packed_s[m, :, g * chunk : (g + 1) * chunk] = up_s[:, at : at + chunk]
    move.put(packed_s, packed)
    move.drain()


def join_kernel(n, place, up, down, ffn, sems):
    move = Mover(sems)
    width, mine = down.shape[1], ffn.shape[1]
    chunk = down.shape[0]
    feats = ffn.shape[0] - width // mine * chunk
    move.put(up, ffn.at[:feats, :])
    for c in range(width // mine):
        move.put(down.at[:, c * mine : (c + 1) * mine], ffn.at[feats + c * chunk : feats + (c + 1) * chunk, :])
    move.drain()


def key_mask(place, rows, n, half, width):
    row = lax.broadcasted_iota(jnp.int32, (rows, width), 0)
    member = row // (2 * half)
    inside = row % (2 * half)
    own = (inside < half).astype(jnp.int32)
    h = place.h
    block_half = own * h + (1 - own) * (1 - h)
    frame = (block_half * n + member) * half + inside % half
    return frame < place.length


def first_kernel(n, dp_size, groups, half, qb, first_row, place, *refs):
    xs, gots, wos = refs[:n], refs[n : n + dp_size], refs[n + dp_size : n + dp_size + groups // dp_size]
    at = n + dp_size + groups // dp_size
    outs = refs[at : at + 11]
    hat_out, h_out, qkv_out, o_out, lse_out, w_out, vec_out, bias_up_out, wo_out, keep, send = outs
    x_s, hat_s, h_s, qkv_s, o_s, lse_s, got_s, w_s, vec_s, bias_up_s, wo3, wo_s, y_s, send_s, bias, sems = refs[at + 11 :]
    move = Mover(sems)
    j = place.j
    rows = 2 * half
    total = n * rows
    ndev = got_s.shape[0]
    hd = got_s.shape[2] // 3
    seq_size = ndev // dp_size
    rs = x_s.shape[1] // ndev
    chunk = bias_up_s.shape[1] // groups
    load = [move.start(gots[i], got_s.at[pl.ds((place.dp ^ i) * seq_size, seq_size)]) for i in range(dp_size)]
    copies = [move.start(xs[r], x_s.at[rows_at(j ^ r, rows), :]) for r in range(n)]
    slots = groups // dp_size
    outw = [
        move.start(wos[i].at[k], wo3.at[(place.dp ^ k) * slots + (place.h ^ i)])
        for k in range(dp_size)
        for i in range(slots)
    ]
    bias[...] = jnp.where(key_mask(place, total, n, half, 128), 0.0, -1.0).astype(f32)
    for copy in load:
        copy.wait()
    for d in range(ndev):
        w_s[d * rs : (d + 1) * rs, :] = got_s[d, :rs, :]
        vec_s[:, d * rs : (d + 1) * rs] = got_s[d, first_row : first_row + 8, :rs].astype(f32)
    bq, bv = [], []
    for t in range(groups):
        bias_up_s[:, t * chunk : (t + 1) * chunk] = got_s[
            t * n + j, first_row : first_row + 1, hd : hd + chunk
        ].astype(f32)
        bq.append(got_s[j * groups + t, first_row + 2 : first_row + 3, :rs].astype(f32))
        bv.append(got_s[j * groups + t, first_row + 3 : first_row + 4, :rs].astype(f32))
    bq = jnp.concatenate(bq, axis=1)
    bv = jnp.concatenate(bv, axis=1)
    move.put(w_s, w_out)
    move.put(vec_s, vec_out)
    move.put(bias_up_s, bias_up_out)
    for r in range(n):
        copies[r].wait()
        base = pl.multiple_of((j ^ r) * rows, rows)
        for part in range(2):
            at = pl.ds(base + part * half, half)
            scaled, _ = normalize(x_s[at, :].astype(f32))
            hat_s[at, :] = scaled.astype(bf16)
            h_s[at, :] = (scaled * vec_s[0:1, :] + vec_s[1:2, :]).astype(bf16)
    block = min(512, total)
    for i in range(total // block):
        at = slice(i * block, (i + 1) * block)
        qkv = dot(h_s[at, :], w_s[...])
        qkv_s[at, :hd] = ((qkv[:, :hd] + bq) * 0.125).astype(bf16)
        qkv_s[at, hd : 2 * hd] = qkv[:, hd : 2 * hd].astype(bf16)
        qkv_s[at, 2 * hd :] = (qkv[:, 2 * hd :] + bv).astype(bf16)
    move.put(hat_s, hat_out)
    move.put(h_s, h_out)
    move.put(qkv_s, qkv_out)
    heads = hd // HEAD
    for head in range(heads):
        cols = slice(head * HEAD, (head + 1) * HEAD)
        kh = qkv_s[:, hd + head * HEAD : hd + (head + 1) * HEAD]
        vt = qkv_s[:, 2 * hd + head * HEAD : 2 * hd + (head + 1) * HEAD].astype(f32).T.astype(bf16)

        def step(i, _, cols=cols, kh=kh, vt=vt, head=head):
            at = rows_at(i, qb)
            scores = dot(kh, qkv_s[at, cols], NT)
            scores = jnp.where(bias[:, 0:1] >= 0.0, scores, -1e30)
            row_max = jnp.max(scores, axis=0, keepdims=True)
            e = jnp.exp(scores - row_max)
            row_sum = jnp.sum(e, axis=0, keepdims=True)
            ot = dot(vt, e.astype(bf16)) / row_sum
            o_s[at, cols] = ot.T.astype(bf16)
            lse_s[head : head + 1, at] = row_max + jnp.log(row_sum)
            return 0

        lax.fori_loop(0, total // qb, step, 0)
    move.put(o_s, o_out)
    move.put(lse_s, lse_out)
    for copy in outw:
        copy.wait()
    for t in range(groups):
        wo_s[t * rs : (t + 1) * rs, :] = wo3[t]
    move.put(wo_s, wo_out)
    for i in range(total // block):
        at = slice(i * block, (i + 1) * block)
        y_s[at, :] = dot(o_s[at, :], wo_s[...])
    send_rows(move, place, n, rows, y_s, send_s, keep, send)
    move.drain()


def mid_kernel(count, place, *refs):
    ins, x, vec = refs[:count], refs[count], refs[count + 1]
    y_out, h_out, vec_s, y_s, sems = refs[count + 2 :]
    move = Mover(sems)
    load = move.start(vec, vec_s)
    y = ins[0][...]
    for i in range(1, count):
        y = y + ins[i][...].astype(f32)
    load.wait()
    y = x[...].astype(f32) + y + vec_s[4:5, :]
    y_s[...] = y
    move.put(y_s, y_out)
    scaled, _ = normalize(y)
    h_out[...] = (scaled * vec_s[5:6, :] + vec_s[6:7, :]).astype(bf16)
    move.drain()


def down_back_kernel(n, groups, place, *refs):
    dys, ws = refs[:n], refs[n : n + groups]
    dy_out, dg_out, w_up_out, w_down_out, dy_s, dg_s, w_up, w_down, sems = refs[n + groups :]
    move = Mover(sems)
    j, g = place.j, place.group
    rows = dys[0].shape[0]
    chunk = w_down.shape[0] // groups
    mine = w_up.shape[1]
    feats = w_up.shape[0] // groups
    first, last = [], []
    for i in range(groups):
        for c in range(w_down.shape[1] // mine):
            source = ws[i].at[feats + c * chunk : feats + (c + 1) * chunk, :]
            first.append(move.start(source, w_down.at[rows_at(g ^ i, chunk), c * mine : (c + 1) * mine]))
    copies = [move.start(dys[r], dy_s.at[rows_at(j ^ r, rows), :]) for r in range(n)]
    for i in range(groups):
        last.append(move.start(ws[i].at[:feats, :], w_up.at[rows_at(g ^ i, feats), :]))
    for copy in first:
        copy.wait()
    move.put(w_down, w_down_out)
    for copy in copies:
        copy.wait()
    block = min(512, dy_s.shape[0])
    for i in range(dy_s.shape[0] // block):
        at = slice(i * block, (i + 1) * block)
        dg_s[at, :] = dot(dy_s[at, :], w_down[...], NT)
        move.put(dg_s.at[at, :], dg_out.at[at, :])
    for copy in last:
        copy.wait()
    move.put(w_up, w_up_out)
    move.put(dy_s, dy_out)
    move.drain()


def ffn_kernel(n, place, *refs):
    hs = refs[:n]
    w_up_in, b_up_in, dg_in = refs[n : n + 3]
    h_out, g_out, du_out, keep, send, db_out = refs[n + 3 : n + 9]
    w_up, b_up, dg, h_s, g_s, du_s, dh_s, send_s, db, sems = refs[n + 9 :]
    move = Mover(sems)
    rows = hs[0].shape[0]
    total = n * rows
    copies = [move.start(hs[r], h_s.at[rows_at(place.j ^ r, rows), :]) for r in range(n)]
    copies += [move.start(w_up_in, w_up), move.start(b_up_in, b_up)]
    late = move.start(dg_in, dg)
    for copy in copies:
        copy.wait()
    block = min(512, total)
    sums = jnp.zeros(db.shape, f32)
    for i in range(total // block):
        at = slice(i * block, (i + 1) * block)
        u = dot(h_s[at, :], w_up[...]) + b_up[...]
        cdf = 0.5 * (1.0 + lax.erf(u * inv_root_two))
        g_s[at, :] = (u * cdf).astype(bf16)
        slope = cdf + u * jnp.exp(-0.5 * u * u) * inv_root_tau
        if i == 0:
            late.wait()
        du = (dg[at, :] * slope).astype(bf16)
        du_s[at, :] = du
        sums = sums + jnp.sum(du.astype(f32), axis=0, keepdims=True)
        dh_s[at, :] = dot(du, w_up[...], NT)
    db[...] = sums
    send_rows(move, place, n, rows, dh_s, send_s, keep, send)
    move.put(h_s, h_out)
    move.put(g_s, g_out)
    move.put(du_s, du_out)
    move.put(db, db_out)
    move.drain()


def down_kernel(n, place, g_in, w_in, keep, send, g, w, out_s, send_s, sems):
    move = Mover(sems)
    for copy in [move.start(w_in, w), move.start(g_in, g)]:
        copy.wait()
    total = g.shape[0]
    block = min(512, total)
    for i in range(total // block):
        at = slice(i * block, (i + 1) * block)
        out_s[at, :] = dot(g[at, :], w[...])
    send_rows(move, place, n, total // n, out_s, send_s, keep, send)
    move.drain()


def ffn_grads_kernel(groups, place, h_in, du_in, dy_in, g_in, *refs):
    outs = refs[:groups]
    h, du, dy, g, grads, stage, sems = refs[groups:]
    move = Mover(sems)
    loads = [move.start(a, b) for a, b in ((h_in, h), (du_in, du), (dy_in, dy), (g_in, g))]
    feats = h.shape[1] // groups
    mine = du.shape[1]
    chunk = mine // groups
    loads[0].wait()
    loads[1].wait()
    for i in range(groups):
        grads[i, :feats, :] = dot(h[:, i * feats : (i + 1) * feats], du[...], TN)
    loads[2].wait()
    loads[3].wait()
    for c in range(dy.shape[1] // mine):
        part = dot(g[...], dy[:, c * mine : (c + 1) * mine], TN)
        for i in range(groups):
            grads[i, feats + c * chunk : feats + (c + 1) * chunk, :] = part[i * chunk : (i + 1) * chunk, :]
    for i in range(1, groups):
        stage[i - 1] = grads[place.group ^ i].astype(bf16)
        move.put(stage.at[i - 1], outs[i])
    move.put(grads.at[place.group], outs[0])
    move.drain()


def pair_kernel(place, keep, recv, *refs):
    *outs, keep_s, sems = refs
    move = Mover(sems)
    rows = outs[0].shape[0]
    order = list(range(1, len(outs))) + [0]
    loads = {}
    for i in order:
        here = slice(i * rows, (i + 1) * rows)
        loads[i] = move.start(keep.at[here, :], keep_s.at[here, :])
    for i in order:
        here = slice(i * rows, (i + 1) * rows)
        loads[i].wait()
        outs[i][...] = (keep_s[here, :].astype(f32) + recv[here, :].astype(f32)).astype(outs[i].dtype)


def fold_kernel(count, place, *refs):
    kept, got, outs = refs[:count], refs[count : 2 * count], refs[2 * count : 3 * count]
    for a, b, out in zip(kept, got, outs):
        out[...] = (a[...].astype(f32) + b[...].astype(f32)).astype(bf16)


def out_kernel(count, place, *refs):
    ins = refs[: count + 2]
    kept, sent = refs[count + 2 : count + 4]
    held = refs[count + 4 : 2 * count + 6]
    out_s, sems = refs[2 * count + 6 :]
    move = Mover(sems)
    for copy in [move.start(a, b) for a, b in zip(ins, held)]:
        copy.wait()
    total = held[0][...] + held[count][...]
    for i in range(1, count):
        total = total + held[i][...].astype(f32)
    out_s[...] = (total + held[count + 1][7:8, :]).astype(bf16)
    half = kept.shape[0]
    move.put(out_s.at[half:, :], sent)
    move.put(out_s.at[:half, :], kept)
    move.drain()


def mid_back_kernel(count, place, *refs):
    ins, (y_in, vec_in, dy) = refs[:count], refs[count : count + 3]
    dy1_out, da_out, small_out, y, vec, dy1_s, small, sems = refs[count + 3 :]
    move = Mover(sems)
    loads = [move.start(y_in, y), move.start(vec_in, vec)]
    dh = ins[0][...]
    for i in range(1, count):
        dh = dh + ins[i][...].astype(f32)
    for copy in loads:
        copy.wait()
    scaled, inv_std = normalize(y[...])
    dyf = dy[...].astype(f32)
    dy1 = dyf + norm_back(dh, scaled, inv_std, vec[5:6, :])
    da = dy1.astype(bf16)
    da_out[...] = da
    dy1_s[...] = dy1
    move.put(dy1_s, dy1_out)
    small[0:1, :] = jnp.sum(dh * scaled, axis=0, keepdims=True)
    small[1:2, :] = jnp.sum(dh, axis=0, keepdims=True)
    small[2:3, :] = jnp.sum(da.astype(f32), axis=0, keepdims=True)
    small[3:4, :] = jnp.sum(dyf, axis=0, keepdims=True)
    move.put(small, small_out)
    move.drain()


def attend_back_kernel(n, half, qb, place, *refs):
    das, ins = refs[:n], refs[n : n + 4]
    dqkv_out, keep, send, db_out, da_out = refs[n + 4 : n + 9]
    da, qkv, lse, wo, w, dqkv, dh_s, send_s, db, do, bias, acc_k, acc_v, sems = refs[n + 9 :]
    rows = 2 * half
    move = Mover(sems)
    copies = [move.start(das[r], da.at[rows_at(place.j ^ r, rows), :]) for r in range(n)]
    loads = [move.start(a, b) for a, b in zip(ins, (wo, qkv, lse, w))]
    total = qkv.shape[0]
    hd = do.shape[1]
    heads = hd // HEAD
    bias[...] = jnp.where(key_mask(place, total, n, half, 128), 0.0, -1.0).astype(f32)
    loads[0].wait()
    for copy in copies:
        copy.wait()
    move.put(da, da_out)
    block = min(512, total)
    for i in range(total // block):
        at = slice(i * block, (i + 1) * block)
        do[at, :] = dot(da[at, :], wo[...], NT).astype(bf16)
    for copy in loads[1:]:
        copy.wait()
    for head in range(heads):
        cols = slice(head * HEAD, (head + 1) * HEAD)
        kh = qkv[:, hd + head * HEAD : hd + (head + 1) * HEAD]
        vh = qkv[:, 2 * hd + head * HEAD : 2 * hd + (head + 1) * HEAD]
        kt = kh.astype(f32).T.astype(bf16)
        acc_k[...] = jnp.zeros_like(acc_k)
        acc_v[...] = jnp.zeros_like(acc_v)

        def step(i, _, cols=cols, kh=kh, vh=vh, kt=kt, head=head):
            at = rows_at(i, qb)
            qh = qkv[at, cols]
            doh = do[at, cols]
            scores = dot(kh, qh, NT)
            probs = jnp.where(bias[:, 0:1] >= 0.0, jnp.exp(scores - lse[head : head + 1, at]), 0.0)
            dp = dot(vh, doh, NT)
            centre = jnp.sum(probs * dp, axis=0, keepdims=True)
            ds = (probs * (dp - centre)).astype(bf16)
            acc_v[...] += dot(probs.astype(bf16), doh)
            acc_k[...] += dot(ds, qh)
            dq = dot(kt, ds)
            dqkv[at, cols] = (dq.T.astype(bf16).astype(f32) * 0.125).astype(bf16)
            return 0

        lax.fori_loop(0, total // qb, step, 0)
        dqkv[:, hd + head * HEAD : hd + (head + 1) * HEAD] = acc_k[...].astype(bf16)
        dqkv[:, 2 * hd + head * HEAD : 2 * hd + (head + 1) * HEAD] = acc_v[...].astype(bf16)
    move.put(dqkv, dqkv_out)
    sums = jnp.zeros(db.shape, f32)
    for i in range(total // block):
        at = slice(i * block, (i + 1) * block)
        grads = dqkv[at, :]
        sums = sums + jnp.sum(grads.astype(f32), axis=0, keepdims=True)
        dh_s[at, :] = dot(grads, w[...], NT)
    db[...] = sums
    send_rows(move, place, n, rows, dh_s, send_s, keep, send)
    move.put(db, db_out)
    move.drain()


def attn_grads_kernel(n, dp_size, groups, first_row, place, *refs):
    ins, outs = refs[:7], refs[7 : 7 + dp_size]
    dqkv, h, w, hat, two, db, up, small, grads, packed_s, sems = refs[7 + dp_size :]
    move = Mover(sems)
    j = place.j
    loads = [move.start(a, b) for a, b in zip(ins, (dqkv, h, w, hat, two, db, up))]
    ndev = packed_s.shape[0]
    hd = dqkv.shape[1] // 3
    rs = h.shape[1] // ndev
    chunk = up.shape[1] // groups
    loads[0].wait()
    loads[1].wait()
    grads[...] = dot(h[...], dqkv[...], TN).astype(bf16)
    for copy in loads[2:]:
        copy.wait()
    small[...] = jnp.zeros_like(small)
    step_rows = min(512, hat.shape[0])

    def step(i, _):
        at = rows_at(i, step_rows)
        dh = dot(dqkv[at, :], w[...], NT)
        small[0:1, :] += jnp.sum(dh * hat[at, :].astype(f32), axis=0, keepdims=True)
        small[1:2, :] += jnp.sum(dh, axis=0, keepdims=True)
        return 0

    lax.fori_loop(0, hat.shape[0] // step_rows, step, 0)
    small[4:8, :] = two[...]
    zeros = jnp.zeros((packed_s.shape[1] - rs, packed_s.shape[2]), bf16)
    for d in range(ndev):
        packed_s[d, rs:, :] = zeros
        packed_s[d, :rs, :] = grads[d * rs : (d + 1) * rs, :]
        packed_s[d, first_row : first_row + 8, :rs] = small[:, d * rs : (d + 1) * rs].astype(bf16)
    for t in range(groups):
        cols = slice(t * rs, (t + 1) * rs)
        at = j * groups + t
        packed_s[at, first_row + 2 : first_row + 3, :rs] = db[:, :hd][:, cols].astype(bf16)
        packed_s[at, first_row + 3 : first_row + 4, :rs] = db[:, 2 * hd :][:, cols].astype(bf16)
        packed_s[t * n + j, first_row : first_row + 1, hd : hd + chunk] = up[
            :, t * chunk : (t + 1) * chunk
        ].astype(bf16)
    seq_size = ndev // dp_size
    for i in list(range(1, dp_size)) + [0]:
        move.put(packed_s.at[pl.ds((place.dp ^ i) * seq_size, seq_size)], outs[i])
    move.drain()


def out_grads_kernel(dp_size, groups, place, da_in, o_in, *refs):
    outs = refs[:dp_size]
    da, o, grads, stage, sems = refs[dp_size:]
    move = Mover(sems)
    for copy in [move.start(o_in, o), move.start(da_in, da)]:
        copy.wait()
    all_rows = dot(o[...], da[...], TN)
    rs = grads.shape[1]
    for t in range(groups):
        grads[t] = all_rows[t * rs : (t + 1) * rs, :]
    slots = groups // dp_size
    for k in range(dp_size):
        for i in range(slots):
            stage[k, i] = grads[(place.dp ^ k) * slots + (place.h ^ i)].astype(bf16)
        move.put(stage.at[k], outs[k])
    move.drain()


def last_kernel(count, place, *refs):
    ins, (x, dy1_in, vec_in, rider) = refs[:count], refs[count : count + 4]
    kept, sent, dy1, vec, sems = refs[count + 4 :]
    move = Mover(sems)
    loads = [move.start(dy1_in, dy1), move.start(vec_in, vec)]
    half = kept.shape[0]
    sent[half:, :] = rider[1]
    dh = ins[0][...]
    for i in range(1, count):
        dh = dh + ins[i][...].astype(f32)
    scaled, inv_std = normalize(x[...].astype(f32))
    for copy in loads:
        copy.wait()
    out = (dy1[...] + norm_back(dh, scaled, inv_std, vec[0:1, :])).astype(bf16)
    sent[:half, :] = out[half:]
    kept[...] = out[:half]


def ffn_sum_kernel(count, place, *refs):
    ins, (up_out, down_out) = refs[:count], refs[count : count + 2]
    held, (total, up_s, down_s, sems) = refs[count + 2 : 2 * count + 2], refs[2 * count + 2 :]
    move = Mover(sems)
    for copy in [move.start(a, b) for a, b in zip(ins, held)]:
        copy.wait()
    ffn = held[0][...].astype(f32)
    for piece in held[1:]:
        ffn = ffn + piece[...].astype(f32)
    total[...] = ffn
    n, rs, mine = up_s.shape
    chunk, width = down_s.shape
    for m in range(n):
        up_s[m] = total[m * rs : (m + 1) * rs, :].astype(bf16)
    move.put(up_s, up_out)
    feats = n * rs
    for c in range(width // mine):
        down_s[:, c * mine : (c + 1) * mine] = total[feats + c * chunk : feats + (c + 1) * chunk, :]
    move.put(down_s, down_out)
    move.drain()


def unpack_kernel(n, groups, first_row, place, *refs):
    back, up_back, out_w = refs[:3]
    halves = refs[3:7]
    output, frames_grad, out_w_grad, up, wq, wk, wv = refs[7:14]
    vectors = refs[14:23]
    back_s, up_back_s, in_s, out_s, up_s, q_s, k_s, v_s = refs[23:31]
    vectors_s, sems = refs[31:40], refs[40]
    move = Mover(sems)
    load, more, third = move.start(back, back_s), move.start(up_back, up_back_s), move.start(out_w, in_s)
    half = output.shape[1]
    for i, target in enumerate((output, frames_grad)):
        move.put(halves[2 * i], target.at[place.h])
        move.put(halves[2 * i + 1].at[:half, :], target.at[1 - place.h])
    third.wait()
    out_s[...] = in_s[...].astype(f32)
    move.put(out_s, out_w_grad)
    rs = wq.shape[0]
    hd = wq.shape[1] // n
    chunk = up.shape[1] // (n * groups)
    more.wait()
    for m in range(n):
        for g in range(groups):
            at = (g * n + m) * chunk
            up_s[:, at : at + chunk] = up_back_s[m, :, g * chunk : (g + 1) * chunk].astype(f32)
    move.put(up_s, up)
    load.wait()
    sums = jnp.zeros((8, 3 * hd), f32)
    for m in range(n):
        cols = slice(m * hd, (m + 1) * hd)
        total = back_s[m].astype(f32)
        for i in range(m + n, back_s.shape[0], n):
            total = total + back_s[i].astype(f32)
        for i, target in enumerate((q_s, k_s, v_s)):
            target[:, cols] = total[:rs, i * hd : (i + 1) * hd]
        sums = sums + total[first_row:, :]
    for a, b in ((q_s, wq), (k_s, wk), (v_s, wv)):
        move.put(a, b)
    for i in range(8):
        vectors_s[i][...] = sums[i : i + 1, :rs]
    vectors_s[8][...] = sums[0:1, hd : hd + chunk]
    for a, b in zip(vectors_s, vectors):
        move.put(a, b)
    move.drain()


def on_device(
    dp_size,
    seq_size,
    frames,
    out_grad,
    order,
    lengths,
    first_gain,
    first_shift,
    query_weight,
    query_bias,
    key_weight,
    value_weight,
    value_bias,
    output_weight,
    output_bias,
    second_gain,
    second_shift,
    up_weight,
    up_bias,
    down_weight,
    down_bias,
):
    slots, half, width = frames.shape
    n = seq_size // slots
    groups = dp_size * slots
    ndev = dp_size * seq_size
    hd = width // n
    heads = hd // HEAD
    rs = query_weight.shape[0]
    hidden = up_weight.shape[1]
    chunk = hidden // ndev
    mine = hidden // n
    parts = width // mine
    feats = n * rs
    rows = 2 * half
    total = n * rows
    qb = 512
    count = n // 2
    both = ("dp", "seq")
    first_row = -(-rs // 8) * 8
    block_rows = first_row + 8

    scale = -(-total // 1024)
    grid = (slots, n, scale)

    def xor(value, bit):
        return lax.ppermute(value, "seq", [(i, i ^ bit) for i in range(seq_size)])

    def gather_direct(value):
        got = [xor(value, r) for r in range(n - 2, 0, -2)]
        return [value] + got[::-1]

    def gather_pair(even):
        out = []
        for piece in even:
            out += [piece, xor(piece, 1)]
        return out

    def pair(keep, recv):
        outs = [sds((rows, width), f32)] + [sds((rows, width), bf16)] * (count - 1)
        return call(
        grid,
            pair_kernel,
            [keep, Held(recv)],
            held_in(outs),
            "pair",
            cost(1),
            scratch=[vmem(keep)],
            sems=count,
        )

    def scatter(pieces):
        return [pieces[0]] + [xor(pieces[i], 2 * i) for i in range(count - 1, 0, -1)][::-1]

    def to_group(value, i):
        pairs = []
        for d in range(ndev):
            dp_of, seq_of = d // seq_size, d % seq_size
            g_of = (dp_of * slots + seq_of // n) ^ i
            pairs.append((d, g_of // slots * seq_size + g_of % slots * n + seq_of % n))
        return lax.ppermute(value, both, pairs)

    def members(value):
        index = [[s * n + i for i in range(n)] for s in range(slots)]
        return lax.all_to_all(value, "seq", 0, 0, tiled=True, axis_index_groups=index)

    def fold(kept, got):
        outs = [sds(a.shape, bf16) for a in kept]
        return call(
            grid,
            functools.partial(fold_kernel, len(kept)),
            held_in(list(kept) + list(got)),
            held_in(outs),
            "fold",
            cost(2),
            sems=1,
            limit=16,
        )

    def spread(pieces):
        bit = len(pieces)
        while bit < groups:
            pieces = pieces + [to_group(piece, bit) for piece in pieces]
            bit *= 2
        return pieces

    def to_dp(value, i):
        return lax.ppermute(value, "dp", [(d, d ^ i) for d in range(dp_size)])

    def owner_pairs(k):
        pairs = []
        for d in range(ndev):
            g_of = (d % groups) ^ (k * slots)
            pairs.append((d, g_of // slots * seq_size + g_of % slots * n + d // groups))
        return pairs

    owners = owner_pairs(0)
    out_w = jnp.stack([lax.ppermute(output_weight, both, owner_pairs(k)) for k in range(dp_size)])

    small_in = [first_gain, first_shift, query_bias, value_bias, output_bias, second_gain, second_shift, down_bias]
    small_in = [v.reshape(1, -1) for v in small_in + [up_bias]]
    weights_in = [query_weight, key_weight, value_weight]
    half_sds, row_sds = sds((half, width), bf16), sds((rows, width), bf16)
    packed_sds, up_sds = sds((seq_size, block_rows, 3 * hd), bf16), sds((n, rs, mine), bf16)
    x_own, x_send, dy_own, dy_send = call(
        grid, rows_kernel, [frames, out_grad], near([half_sds] * 4), "rows", cost(1), sems=4
    )
    x_recv = xor(x_send, n)
    (packed,) = call(
        grid,
        functools.partial(pack_kernel, n, slots, groups, first_row),
        [after(weights_in[0], x_send)] + weights_in[1:] + small_in,
        near([packed_sds]),
        "pack",
        cost(2),
        scratch=[vmem(w) for w in weights_in] + [vmem(v) for v in small_in] + [pltpu.VMEM((n, block_rows, 3 * hd), bf16)],
        sems=12 + slots,
    )
    (up_packed,) = call(
        grid,
        functools.partial(pack_up_kernel, n, groups),
        [up_weight],
        near([up_sds]),
        "pack_up",
        cost(1),
        scratch=[vmem(up_weight), vmem(up_sds)],
        sems=2,
    )
    attn_w = lax.all_to_all(packed, "seq", 0, 0, tiled=True)
    up_mine = members(after(up_packed, attn_w))
    x = jnp.concatenate([x_own, x_recv])
    x_even = gather_direct(x)
    wos = [out_w, xor(out_w, n)]
    dy_recv = xor(after(dy_send, attn_w), n)
    attn_ws = [attn_w]
    while len(attn_ws) < dp_size:
        attn_ws += [to_dp(piece, len(attn_ws)) for piece in attn_ws]
    ffn_sds = sds((feats + parts * chunk, mine), bf16)
    (ffn_w,) = call(
        grid,
        functools.partial(join_kernel, n),
        near([up_mine.reshape(feats, mine), down_weight]),
        near([ffn_sds]),
        "join",
        cost(1),
        sems=1 + parts,
    )
    ffn_half = to_group(after(ffn_w, attn_w), 1)
    xs = gather_pair([after(piece, attn_ws[-1], wos[-1]) for piece in x_even])
    dy = jnp.concatenate([dy_own, dy_recv])

    ffn_go, dy_go, xs, attn_ws, wos = lax.optimization_barrier((ffn_w, dy, tuple(xs), tuple(attn_ws), tuple(wos)))
    xs, attn_ws, wos = list(xs), list(attn_ws), list(wos)
    ffn_ws = [ffn_w, ffn_half, to_group(ffn_go, 2)]
    dy_even = gather_direct(dy_go)
    x_sds = sds((total, width), bf16)
    keep_sds = send_sds = sds((total // 2, width), bf16)
    s_half = pltpu.VMEM((2, total // 2, width), bf16)
    outs = [
        x_sds,
        x_sds,
        sds((total, 3 * hd), bf16),
        sds((total, hd), bf16),
        sds((heads, total), f32),
        sds((width, 3 * hd), bf16),
        sds((8, width), f32),
        sds((1, mine), f32),
        sds((hd, width), bf16),
        keep_sds,
        send_sds,
    ]
    s_hat, s_h, s_qkv, s_o, s_lse, s_w, s_vec, s_bias, s_wo, _, _ = [vmem(o) for o in outs]
    s_rows = pltpu.VMEM((total, width), f32)
    s_got = pltpu.VMEM((ndev, block_rows, 3 * hd), bf16)
    s_wo3 = pltpu.VMEM((groups, rs, width), bf16)
    hat, h_first, qkv, o_heads, lse, w_qkv, vec, bias_up, wo, keep, send = call(
        grid,
        functools.partial(first_kernel, n, dp_size, groups, half, qb, first_row),
        near(xs + attn_ws + wos),
        outs[:-1] + near(outs[-1:]),
        "first",
        cost(17),
        scratch=[vmem(x_sds), s_hat, s_h, s_qkv, s_o, s_lse, s_got, s_w, s_vec, s_bias, s_wo3, s_wo, s_rows, s_half]
        + [pltpu.VMEM((total, 128), f32)],
        sems=3 * n + groups + dp_size + 10,
        lengths=(order, lengths),
        limit=48,
    )
    send = after(send, *ffn_ws[1:], *dy_even[1:])

    y_sds = sds((rows, width), f32)
    y_pieces = pair(keep, xor(send, 1))
    ys = scatter(y_pieces)
    dys = gather_pair([dy_even[0]] + [after(piece, y_pieces[0]) for piece in dy_even[1:]])
    ffn_ws = spread(ffn_ws + [to_group(after(ffn_ws[1], y_pieces[0]), 2)])
    y1, h2 = call(
        grid,
        functools.partial(mid_kernel, count),
        held_in(ys + [x]) + [vec],
        [y_sds, Held(row_sds)],
        "mid",
        cost(2),
        scratch=[vmem(vec), vmem(y_sds)],
        sems=2,
    )
    h2_even = gather_direct(h2)

    outs = [x_sds, sds((total, mine), f32), sds((width, mine), bf16), sds((mine, width), bf16)]
    dy_all, dg, w_up, w_down = call(
        grid,
        functools.partial(down_back_kernel, n, groups),
        near(dys + ffn_ws),
        outs,
        "down_back",
        cost(5),
        scratch=[vmem(o) for o in outs],
        sems=2 * n + groups * (parts + 1) + 3,
        limit=14 * scale,
    )
    h2s = gather_pair(h2_even[:1] + [after(piece, dg) for piece in h2_even[1:]])

    act_sds = sds((total, mine), bf16)
    outs = [x_sds, act_sds, act_sds, keep_sds, send_sds, sds((1, mine), f32)]
    h2_all, g, du, keep, send, d_bias_up = call(
        grid,
        functools.partial(ffn_kernel, n),
        near(h2s) + [w_up, bias_up, dg],
        outs[:4] + near(outs[4:5]) + outs[5:],
        "ffn",
        cost(9),
        scratch=[vmem(a) for a in [w_up, bias_up, dg] + outs[:3]] + [s_rows, s_half, vmem(outs[5])],
        sems=3 * n + 7,
        limit=28 * scale,
    )
    dh2 = scatter(pair(keep, xor(send, 1)))

    g_then = after(g, dh2[0])
    out_keep, out_send = call(
        grid,
        functools.partial(down_kernel, n),
        [g_then, w_down],
        [keep_sds, Near(send_sds)],
        "down",
        cost(4),
        scratch=[vmem(g), vmem(w_down), s_rows, s_half],
        sems=n + 2,
        limit=16 * scale,
    )
    ffn_parts = call(
        grid,
        functools.partial(ffn_grads_kernel, groups),
        [h2_all, du, dy_all, g_then],
        [sds(ffn_sds.shape, f32)] + near([ffn_sds] * (groups - 1)),
        "ffn_grads",
        cost(0),
        scratch=[vmem(a) for a in (x_sds, act_sds, x_sds, act_sds)]
        + [pltpu.VMEM((groups,) + ffn_sds.shape, f32), pltpu.VMEM((groups - 1,) + ffn_sds.shape, bf16)],
        sems=4 + groups,
        limit=20 * scale,
    )

    small_sds = sds((4, width), f32)
    outs = [y_sds, row_sds, small_sds]
    dy1, da, small_two = call(
        grid,
        functools.partial(mid_back_kernel, count),
        held_in(dh2) + [after(y1, ffn_parts[0], out_keep), vec, Held(dy)],
        outs[:1] + held_in(outs[1:2]) + outs[2:],
        "mid_back",
        cost(3),
        scratch=[vmem(y1), vmem(vec), vmem(y_sds), vmem(small_sds)],
        sems=4,
    )
    da_even = gather_direct(da)
    bit = groups // 2
    while bit > 2:
        ffn_parts = fold(ffn_parts[:bit], [to_group(piece, bit) for piece in ffn_parts[bit:]])
        bit //= 2
    ffn_got = [to_group(piece, 2) for piece in ffn_parts[2:4]]
    out_kept = pair(out_keep, xor(after(out_send, da), 1))
    (ffn_next,) = fold([after(ffn_parts[1], out_kept[0])], ffn_got[1:])
    das = gather_pair([da_even[0]] + [after(piece, ffn_next) for piece in da_even[1:]])

    out_kept, das, ffn_next = lax.optimization_barrier((tuple(out_kept), tuple(das), ffn_next))
    out_kept, das = list(out_kept), list(das)
    ffn_got = [ffn_got[0], to_group(ffn_next, 1)]
    out_pieces = scatter(out_kept)
    ins = [wo, qkv, lse, w_qkv]
    outs = [sds((total, 3 * hd), bf16), keep_sds, send_sds, sds((1, 3 * hd), f32), x_sds]
    d_qkv, keep, send, d_bias_qkv, da_all = call(
        grid,
        functools.partial(attend_back_kernel, n, half, qb),
        near(das) + ins,
        outs[:2] + near(outs[2:3]) + outs[3:],
        "attend_back",
        cost(0),
        scratch=[vmem(x_sds)]
        + [vmem(a) for a in (qkv, lse, wo, w_qkv, outs[0])]
        + [s_rows, s_half, vmem(outs[3]), pltpu.VMEM((total, hd), bf16), pltpu.VMEM((total, 128), f32)]
        + [pltpu.VMEM((total, HEAD), f32)] * 2,
        sems=2 * n + 9,
        lengths=(order, lengths),
        limit=48,
    )
    recv = xor(after(send, *out_pieces[1:], *ffn_got), 1)

    ins = [d_qkv, h_first, w_qkv, hat, small_two, d_bias_qkv, d_bias_up]
    attn_parts = call(
        grid,
        functools.partial(attn_grads_kernel, n, dp_size, groups, first_row),
        ins,
        near([packed_sds] * dp_size),
        "attn_grads",
        cost(6),
        scratch=[vmem(a) for a in ins]
        + [
            pltpu.VMEM((8, width), f32),
            pltpu.VMEM((width, 3 * hd), bf16),
            pltpu.VMEM((ndev, block_rows, 3 * hd), bf16),
        ],
        sems=7 + dp_size,
        limit=20 * scale,
    )
    dh1_pieces = pair(after(keep, attn_parts[0]), recv)
    dh1 = scatter(dh1_pieces)
    bit = dp_size // 2
    while bit > 1:
        attn_parts = fold(attn_parts[:bit], [to_dp(piece, bit) for piece in attn_parts[bit:]])
        bit //= 2
    attn_got = to_dp(attn_parts[1], 1)

    ffn_sums = [after(ffn_parts[0], dh1_pieces[0])] + ffn_got
    down_sds = sds((chunk, width), f32)
    up_back, down_weight_grad = call(
        grid,
        functools.partial(ffn_sum_kernel, 3),
        ffn_sums[:1] + near(ffn_sums[1:]),
        [Near(up_sds), down_sds],
        "ffn_sum",
        cost(2),
        scratch=[vmem(a) for a in ffn_sums] + [pltpu.VMEM(ffn_sds.shape, f32), vmem(up_sds), vmem(down_sds)],
        sems=5,
    )
    up_back = members(up_back)
    out_parts = call(
        grid,
        functools.partial(out_grads_kernel, dp_size, groups),
        [da_all, after(o_heads, dh1_pieces[0])],
        near([sds((slots, rs, width), bf16)] * dp_size),
        "out_grads",
        cost(2),
        scratch=[
            vmem(x_sds),
            vmem(o_heads),
            pltpu.VMEM((groups, rs, width), f32),
            pltpu.VMEM((dp_size, slots, rs, width), bf16),
        ],
        sems=2 + dp_size,
        limit=10 * scale,
    )
    bit = dp_size // 2
    while bit > 1:
        out_parts = fold(out_parts[:bit], [to_dp(piece, bit) for piece in out_parts[bit:]])
        bit //= 2

    (attn_sum,) = fold([after(attn_parts[0], up_back)], [attn_got])
    back = lax.all_to_all(attn_sum, "seq", 0, 0, tiled=True)
    (out_w_sum,) = fold([after(out_parts[0], attn_sum)], [to_dp(out_parts[1], 1)])

    ins = out_pieces + [y1, vec]
    out_own, out_sent = call(
        grid,
        functools.partial(out_kernel, count),
        near([after(ins[0], attn_sum)] + ins[1:count]) + ins[count:],
        near([half_sds] * 2),
        "out",
        cost(2),
        scratch=[vmem(a) for a in ins + [row_sds]],
        sems=len(ins) + 2,
    )
    out_other = xor(out_sent, n)

    ins = dh1 + [x, after(dy1, attn_sum), vec]
    kept, sent = call(
        grid,
        functools.partial(last_kernel, count),
        held_in(ins[: count + 1]) + ins[count + 1 :] + held_in([out_w_sum]),
        held_in([half_sds, sds((half + rs, width), bf16)]),
        "last",
        cost(2),
        scratch=[vmem(dy1), vmem(vec)],
        sems=2,
    )
    other = xor(sent, n)
    out_w = (out_w_sum[0].astype(f32) + other[half:].astype(f32)).astype(bf16)
    out_w = lax.ppermute(out_w, both, [(b, a) for a, b in owners])
    frames_sds = sds(frames.shape, bf16)
    weight_sds = sds((rs, width), f32)
    outs = [weight_sds, sds((rs, hidden), f32)] + [weight_sds] * 3
    vectors = [sds((1, rs), f32)] * 8 + [sds((1, chunk), f32)]
    output, frames_grad, output_weight_grad, up_weight_grad, d_query, d_key, d_value, *vectors = call(
        grid,
        functools.partial(unpack_kernel, n, groups, first_row),
        near([back, up_back, out_w, out_own, out_other, kept, other]),
        [frames_sds] * 2 + outs + vectors,
        "unpack",
        cost(2),
        scratch=[vmem(a) for a in [back, up_back, out_w] + outs + vectors],
        sems=24,
    )
    vectors = [v.reshape(-1) for v in vectors]
    return (
        output,
        frames_grad,
        vectors[0],
        vectors[1],
        d_query,
        vectors[2],
        d_key,
        d_value,
        vectors[3],
        output_weight_grad,
        vectors[6],
        vectors[4],
        vectors[5],
        up_weight_grad,
        vectors[8],
        down_weight_grad,
        vectors[7],
    )


def solution(mesh):
    vector = P(("dp", "seq"))
    matrix = P(("dp", "seq"), None)
    rows = P("dp", "seq", None)
    return jax.shard_map(
        functools.partial(on_device, mesh.shape["dp"], mesh.shape["seq"]),
        mesh=mesh,
        in_specs=(
            rows,
            rows,
            P("dp"),
            P(),
            vector,
            vector,
            matrix,
            vector,
            matrix,
            matrix,
            vector,
            matrix,
            vector,
            vector,
            vector,
            matrix,
            vector,
            matrix,
            vector,
        ),
        out_specs=(
            rows,
            rows,
            vector,
            vector,
            matrix,
            vector,
            matrix,
            matrix,
            vector,
            matrix,
            vector,
            vector,
            vector,
            matrix,
            vector,
            matrix,
            vector,
        ),
        check_vma=False,
    )
```
